32 devices in a mesh: groups: 2 (over y), role: 4 (over x, core), tp: 4 (over z).
Axes of the slice: x: 2, y: 2, z: 4, core: 2. Of those that a mesh axis runs over, the one named last changes fastest.
Arguments:
- residual: bfloat16 [64, 8192], P(('groups', 'tp'), 'role'), parts along dimension 0, may hold values from -20 to 20
- attn_gain: float32 [8192], P('role'), may hold values from 0.1 to 1.9
- w_query: bfloat16 [8192, 4096], P('role', 'tp'), may hold values from -0.0625 to 0.0625
- w_key: bfloat16 [8192, 512], P('role', 'tp'), may hold values from -0.0625 to 0.0625
- w_value: bfloat16 [8192, 512], P('role', 'tp'), may hold values from -0.0625 to 0.0625
- w_output: bfloat16 [4096, 8192], P('tp', 'role'), may hold values from -0.09375 to 0.09375
- cache_keys: bfloat16 [64, 256, 512], P(('groups', 'role', 'tp')), parts along dimension 0, may hold values from -300 to 300
- cache_values: bfloat16 [64, 256, 512], P(('groups', 'role', 'tp')), parts along dimension 0, may hold values from -12 to 12
- lengths: int32 [64], P(('groups', 'role', 'tp')), parts along dimension 0, may hold values from 2 to 256
- served: int32 [64], P('groups'), parts along dimension 0, may hold values 0 or 1
- ffn_gain: float32 [8192], P('role'), may hold values from 0.1 to 1.9
- w_gate: bfloat16 [8192, 14336], P('role', 'tp'), may hold values from -0.0625 to 0.0625
- w_up: bfloat16 [8192, 14336], P('role', 'tp'), may hold values from -0.0625 to 0.0625
- w_down: bfloat16 [14336, 8192], P('tp', 'role'), may hold values from -0.046875 to 0.046875
Outputs:
- layer_out: bfloat16 [64, 8192], P(('groups', 'tp'), 'role'), parts along dimension 0
The draws below stay inside these ranges and needn't reach their ends.
There are 2 independent parts, one for each index of `groups`. The reference program is written for one: setup_inputs(seed, part) draws one part's arguments, and reference() takes and returns one part's arrays. A program takes and returns all parts, laid end to end along the dimension named above; an argument that names none is the same for every part. Nothing has to cross between parts.
Inputs may be any that keep to these rules, and one draw needn't show every extreme that they name: Each request's new token stands at position lengths; cached positions from lengths on are unused.
All inputs are finite; a program needn't handle non-finite values.
Results may differ from the reference program's by a relative error of at most 0.024.
Values may be sent and summed in bfloat16 or wider, within the bound.
No kernel may reach another device: no remote copies, remote signals or barrier semaphores. Data moves between devices by JAX's collectives and lax.ppermute only.
A program may use at most 128 MiB of HBM per device.

```python
import jax
import jax.numpy as jnp
from jax import lax

D = 8192
HEADS = 32
KV_HEADS = 4
HEAD_DIM = 128
FF = 14336
WINDOW = 256
GROUP = 8
REQUESTS = 32
N_ROLE = 4
N_TP = 4


def draw_residual(key, part):
    position = jnp.arange(D, dtype=jnp.float32) / D
    lowest = 0.5
    highest = 2.0
    scale = lowest * jnp.power(jnp.float32(highest / lowest), position)
    sampled = jnp.clip(jax.random.normal(key, (REQUESTS, D), jnp.float32), -6.0, 6.0)
    return (sampled * scale[None, :]).astype(jnp.bfloat16)


def draw_cache_keys(key, part):
    sampled = jnp.clip(jax.random.normal(key, (REQUESTS, WINDOW, KV_HEADS * HEAD_DIM), jnp.float32), -5.0, 5.0)
    return sampled.astype(jnp.bfloat16)


def plant(array, own_key, least, top_value):
    extent = array.shape
    index_at = [jax.random.randint(jax.random.fold_in(own_key, axis), (), 0, extent[axis]) for axis in range(len(extent))]
    array = array.at[tuple(index_at)].set(least)
    longest = extent.index(max(extent))
    index_at[longest] = (index_at[longest] + 1) % extent[longest]
    return array.at[tuple(index_at)].set(top_value)


def shard_levels(rng, extent, pieces, low, top_value):
    def one(dim, blocks):
        heights = jax.random.uniform(jax.random.fold_in(jax.random.fold_in(rng, 6), dim), (blocks,), jnp.float32, low / len(pieces), top_value / len(pieces))
        return jnp.repeat(jnp.exp(heights), extent[dim] // blocks).reshape((-1,) + (1,) * (len(extent) - dim - 1))

    loudness = one(*pieces[0])
    for cut in pieces[1:]:
        loudness = loudness * one(*cut)
    return loudness


def scatter_about(rng, shape, scale, most, pieces=(), held_as=jnp.bfloat16):
    entries = scale * jax.random.normal(rng, shape, jnp.float32)
    if pieces:
        entries = entries * shard_levels(rng, shape, pieces, -0.22, 0.18)
    return jnp.clip(entries, -most, most).astype(held_as)


def setup_inputs(seed: int = 0, part: int = 0) -> dict:
    seeds = jax.random.split(jax.random.key(seed), 15)
    part_keys = jax.random.split(jax.random.fold_in(seeds[14], part), 15)
    return {
        "residual": draw_residual(jax.random.fold_in(jax.random.fold_in(seeds[14], part), 71), part),
        "attn_gain": jnp.clip(1.0 + 0.18 * jax.random.normal(seeds[1], (D,), jnp.float32), 0.1, 1.9),
        "w_query": scatter_about(seeds[2], (D, HEADS * HEAD_DIM), D ** -0.5, 0.0625, ((0, 4), (1, 4))),
        "w_key": scatter_about(seeds[3], (D, KV_HEADS * HEAD_DIM), D ** -0.5, 0.0625, ((0, 4), (1, 4))),
        "w_value": scatter_about(seeds[4], (D, KV_HEADS * HEAD_DIM), D ** -0.5, 0.0625, ((0, 4), (1, 4))),
        "w_output": scatter_about(seeds[5], (HEADS * HEAD_DIM, D), (HEADS * HEAD_DIM) ** -0.5, 0.09375, ((0, 4), (1, 4))),
        "cache_keys": draw_cache_keys(jax.random.fold_in(jax.random.fold_in(seeds[14], part), 71), part),
        "cache_values": scatter_about(part_keys[7], (REQUESTS, WINDOW, KV_HEADS * HEAD_DIM), 2.0, 12.0, ((0, 16),)),
        "lengths": plant(jax.random.randint(part_keys[8], (REQUESTS,), 2, WINDOW + 1), jax.random.fold_in(part_keys[8], 1), 2, WINDOW).astype(jnp.int32),
        "served": plant((jax.random.randint(part_keys[9], (REQUESTS,), 0, 4) < 3).astype(jnp.int32), jax.random.fold_in(part_keys[9], 1), 0, 1),
        "ffn_gain": jnp.clip(1.0 + 0.18 * jax.random.normal(seeds[10], (D,), jnp.float32), 0.1, 1.9),
        "w_gate": scatter_about(seeds[11], (D, FF), D ** -0.5, 0.0625, ((0, 4), (1, 4))),
        "w_up": scatter_about(seeds[12], (D, FF), D ** -0.5, 0.0625, ((0, 4), (1, 4))),
        "w_down": scatter_about(seeds[13], (FF, D), FF ** -0.5, 0.046875, ((0, 4), (1, 4))),
    }


epsilon = 1e-05
rope_base = 500000.0

def rotate(vectors, positions):
    halfway = vectors.shape[-1] // 2
    frequency = jnp.power(jnp.float32(rope_base), -jnp.arange(halfway, dtype=jnp.float32) * 2.0 / vectors.shape[-1])
    angles = positions.astype(jnp.float32)[:, None, None] * frequency[None, None, :]
    cosine = jnp.cos(angles)
    sine_part = jnp.sin(angles)
    leading = vectors[..., :halfway]
    trailing = vectors[..., halfway:]
    return jnp.concatenate([leading * cosine - trailing * sine_part, trailing * cosine + leading * sine_part], axis=-1)

def attend(queries, new_key, new_value, keys, values, lengths):
    batch_rows = queries.shape[0]
    factor = HEAD_DIM ** (-0.5)
    grouped = queries.reshape(batch_rows, KV_HEADS, GROUP, HEAD_DIM).astype(jnp.float32)
    key_blocks = keys.reshape(batch_rows, WINDOW, KV_HEADS, HEAD_DIM).astype(jnp.float32)
    value_blocks = values.reshape(batch_rows, WINDOW, KV_HEADS, HEAD_DIM).astype(jnp.float32)
    scores = jnp.einsum('nkgd,nwkd->nkgw', grouped, key_blocks) * factor
    self_score = jnp.einsum('nkgd,nkd->nkg', grouped, new_key.astype(jnp.float32)) * factor
    usable = jnp.arange(WINDOW, dtype=jnp.int32)[None, :] < lengths[:, None]
    scores = jnp.where(usable[:, None, None, :], scores, -jnp.inf)
    highest = jnp.maximum(lax.optimization_barrier(jnp.max(scores, axis=-1)), self_score)
    weights = jnp.exp(scores - highest[..., None])
    self_weight = jnp.exp(self_score - highest)
    denominator = lax.optimization_barrier(jnp.sum(weights, axis=-1)) + self_weight
    chances = (weights / denominator[..., None]).astype(jnp.bfloat16).astype(jnp.float32)
    self_chance = (self_weight / denominator).astype(jnp.bfloat16).astype(jnp.float32)
    attended = jnp.einsum('nkgw,nwkd->nkgd', chances, value_blocks)
    attended = attended + self_chance[..., None] * new_value.astype(jnp.float32)[:, :, None, :]
    return attended.reshape(batch_rows, HEADS * HEAD_DIM).astype(jnp.bfloat16)

def block_sum(left, right, blocks):
    block_size = right.shape[0] // blocks
    accumulated = jnp.zeros((left.shape[0], right.shape[1]), jnp.float32)
    for block_index in range(blocks):
        partial_value = jnp.dot(left[:, block_index * block_size:(block_index + 1) * block_size], right[block_index * block_size:(block_index + 1) * block_size], preferred_element_type=jnp.float32)
        rounded = lax.optimization_barrier(partial_value.astype(jnp.bfloat16))
        accumulated = accumulated + rounded.astype(jnp.float32)
    return accumulated

def rms_normed(stream, gain):
    widened = stream.astype(jnp.float32)
    inverse = lax.rsqrt(lax.optimization_barrier(jnp.mean(widened * widened, axis=1, keepdims=True)) + epsilon)
    return (widened * inverse * gain[None, :]).astype(jnp.bfloat16)

def reference(residual, attn_gain, w_query, w_key, w_value, w_output, cache_keys, cache_values, lengths, served, ffn_gain, w_gate, w_up, w_down):
    count = residual.shape[0]
    normed = rms_normed(residual, attn_gain)
    queries = jnp.dot(normed, w_query, preferred_element_type=jnp.float32).reshape(count, HEADS, HEAD_DIM)
    new_key = jnp.dot(normed, w_key, preferred_element_type=jnp.float32).reshape(count, KV_HEADS, HEAD_DIM)
    new_value = jnp.dot(normed, w_value, preferred_element_type=jnp.float32).reshape(count, KV_HEADS, HEAD_DIM).astype(jnp.bfloat16)
    queries = rotate(queries, lengths).astype(jnp.bfloat16)
    new_key = rotate(new_key, lengths).astype(jnp.bfloat16)
    attended = attend(queries, new_key, new_value, cache_keys, cache_values, lengths)
    attn = block_sum(attended, w_output, N_TP)
    live_rows = served.astype(jnp.float32)[:, None]
    middle = (residual.astype(jnp.float32) + live_rows * attn).astype(jnp.bfloat16)
    mid_normed = rms_normed(middle, ffn_gain)
    gate_total = block_sum(mid_normed, w_gate, N_ROLE)
    up_total = block_sum(mid_normed, w_up, N_ROLE)
    hidden = (jax.nn.silu(gate_total) * up_total).astype(jnp.bfloat16)
    ffn = block_sum(hidden, w_down, N_TP)
    return (middle.astype(jnp.float32) + live_rows * ffn).astype(jnp.bfloat16)
```

```python
import math

import jax
import jax.numpy as jnp
from jax import lax
from jax.experimental import pallas as pl
from jax.experimental.pallas import tpu as pltpu
from jax.sharding import PartitionSpec as P

D = 8192
HEADS = 32
KV_HEADS = 4
HEAD_DIM = 128
WINDOW = 256
GROUP = 8


epsilon = 1e-05
rope_base = 500000.0


def rotate(vectors, positions):
    halfway = vectors.shape[-1] // 2
    frequency = jnp.power(
        jnp.float32(rope_base), -jnp.arange(halfway, dtype=jnp.float32) * 2.0 / vectors.shape[-1]
    )
    angles = positions.astype(jnp.float32)[:, None, None] * frequency[None, None, :]
    cosine = jnp.cos(angles)
    sine_part = jnp.sin(angles)
    leading = vectors[..., :halfway]
    trailing = vectors[..., halfway:]
    return jnp.concatenate(
        [leading * cosine - trailing * sine_part, trailing * cosine + leading * sine_part], axis=-1
    )


def attend(queries, new_key, new_value, keys, values, lengths):
    batch_rows = queries.shape[0]
    factor = HEAD_DIM ** (-0.5)
    grouped = queries.reshape(batch_rows, KV_HEADS, GROUP, HEAD_DIM)
    key_blocks = keys.reshape(batch_rows, WINDOW, KV_HEADS, HEAD_DIM)
    value_blocks = values.reshape(batch_rows, WINDOW, KV_HEADS, HEAD_DIM)
    scores = (
        jnp.einsum("nkgd,nwkd->nkgw", grouped, key_blocks, preferred_element_type=jnp.float32)
        * factor
    )
    self_score = (
        jnp.einsum("nkgd,nkd->nkg", grouped, new_key, preferred_element_type=jnp.float32) * factor
    )
    usable = jnp.arange(WINDOW, dtype=jnp.int32)[None, :] < lengths[:, None]
    scores = jnp.where(usable[:, None, None, :], scores, -jnp.inf)
    highest = jnp.maximum(jnp.max(scores, axis=-1), self_score)
    weights = jnp.exp(scores - highest[..., None])
    self_weight = jnp.exp(self_score - highest)
    denominator = jnp.sum(weights, axis=-1) + self_weight
    chances = (weights / denominator[..., None]).astype(jnp.bfloat16)
    self_chance = (self_weight / denominator).astype(jnp.bfloat16)
    attended = jnp.einsum(
        "nkgw,nwkd->nkgd", chances, value_blocks, preferred_element_type=jnp.float32
    )
    attended = (
        attended
        + self_chance.astype(jnp.float32)[..., None] * new_value.astype(jnp.float32)[:, :, None, :]
    )
    return attended.reshape(batch_rows, HEADS * HEAD_DIM).astype(jnp.bfloat16)


def feed_forward(middle, ffn_gain, w_gate, w_up, w_down):
    widened = middle.astype(jnp.float32)
    squares = lax.psum(jnp.sum(widened * widened, axis=1), "role")
    inverse = lax.rsqrt(squares / D + epsilon)
    mid_normed = (widened * inverse[:, None] * ffn_gain[None, :]).astype(jnp.bfloat16)
    gate_part = jnp.dot(mid_normed, w_gate, preferred_element_type=jnp.float32)
    up_part = jnp.dot(mid_normed, w_up, preferred_element_type=jnp.float32)
    gate_total, up_total = (
        lax.psum(gate_part.astype(jnp.bfloat16), "role").astype(jnp.float32),
        lax.psum(up_part.astype(jnp.bfloat16), "role").astype(jnp.float32),
    )
    hidden = (jax.nn.silu(gate_total) * up_total).astype(jnp.bfloat16)
    down_terms = jnp.dot(hidden, w_down, preferred_element_type=jnp.float32)
    return lax.psum_scatter(
        down_terms.astype(jnp.bfloat16), "tp", scatter_dimension=0, tiled=True
    ).astype(jnp.float32)


def local(
    residual,
    attn_gain,
    w_query,
    w_key,
    w_value,
    w_output,
    cache_keys,
    cache_values,
    lengths,
    served,
    ffn_gain,
    w_gate,
    w_up,
    w_down,
):
    own_rows = residual.shape[0]
    tp_count = lax.axis_size("tp")
    row_start = lax.axis_index("tp") * own_rows
    live_own = lax.dynamic_slice_in_dim(served, row_start, own_rows, 0).astype(jnp.float32)[:, None]
    rows_all = lax.all_gather(residual, "tp", axis=0, tiled=True)
    widened = rows_all.astype(jnp.float32)
    squares = lax.psum(jnp.sum(widened * widened, axis=1), "role")
    inverse = lax.rsqrt(squares / D + epsilon)
    normed = (widened * inverse[:, None] * attn_gain[None, :]).astype(jnp.bfloat16)
    partial_value = jnp.concatenate(
        [
            jnp.dot(normed, w_query, preferred_element_type=jnp.float32),
            jnp.dot(normed, w_key, preferred_element_type=jnp.float32),
            jnp.dot(normed, w_value, preferred_element_type=jnp.float32),
        ],
        axis=1,
    )
    summed = lax.psum_scatter(
        partial_value.astype(jnp.bfloat16), "role", scatter_dimension=0, tiled=True
    ).astype(jnp.float32)
    gathered = lax.all_to_all(
        summed.astype(jnp.bfloat16), "tp", split_axis=0, concat_axis=1, tiled=True
    ).astype(summed.dtype)
    local_rows = gathered.shape[0]
    query_cols = w_query.shape[1]
    kv_cols = w_key.shape[1]
    blocks = gathered.reshape(local_rows, tp_count, query_cols + 2 * kv_cols)
    queries = blocks[:, :, :query_cols].reshape(local_rows, HEADS, HEAD_DIM)
    new_key = blocks[:, :, query_cols : query_cols + kv_cols].reshape(
        local_rows, KV_HEADS, HEAD_DIM
    )
    new_value = (
        blocks[:, :, query_cols + kv_cols :]
        .reshape(local_rows, KV_HEADS, HEAD_DIM)
        .astype(jnp.bfloat16)
    )
    queries = rotate(queries, lengths).astype(jnp.bfloat16)
    new_key = rotate(new_key, lengths).astype(jnp.bfloat16)
    attended = attend(queries, new_key, new_value, cache_keys, cache_values, lengths)
    head_block = lax.all_to_all(attended, "tp", split_axis=1, concat_axis=0, tiled=True)
    attn_terms = jnp.dot(
        lax.all_gather(head_block, "role", axis=0, tiled=True),
        w_output,
        preferred_element_type=jnp.float32,
    )
    attn = lax.psum_scatter(
        attn_terms.astype(jnp.bfloat16), "tp", scatter_dimension=0, tiled=True
    ).astype(jnp.float32)
    middle_own = (residual.astype(jnp.float32) + live_own * attn).astype(jnp.bfloat16)
    middle = lax.all_gather(middle_own, "tp", axis=0, tiled=True)
    ffn = feed_forward(middle, ffn_gain, w_gate, w_up, w_down)
    return (middle_own.astype(jnp.float32) + live_own * ffn).astype(jnp.bfloat16)


LANES = 128
MIB = 2**20
COVER = 100
CHUNK = 512


def exchange_fits(residual, w_query, w_key, w_gate):
    tp_count, role_count = lax.axis_size("tp"), lax.axis_size("role")
    return (
        tp_count in (2, 4)
        and role_count in (2, 4)
        and residual.shape[0] % 8 == 0
        and w_query.shape[1] % HEAD_DIM == 0
        and w_key.shape[1] % HEAD_DIM == 0
        and w_gate.shape[1] % (2 * LANES) == 0
    )


def turn(vectors, cosine, sine):
    halfway = vectors.shape[-1] // 2
    cosine, sine = cosine[:, None, :], sine[:, None, :]
    leading, trailing = vectors[..., :halfway], vectors[..., halfway:]
    return jnp.concatenate(
        [leading * cosine - trailing * sine, trailing * cosine + leading * sine], axis=-1
    )


def swap(value, axis, distance):
    count = lax.axis_size(axis)
    return lax.ppermute(value, axis, [(i, i ^ distance) for i in range(count)])


def in_vmem(value):
    return pltpu.with_memory_space_constraint(value, pltpu.VMEM)


def call(kernel, outs, args, scratch=(), limit=4 * MIB, smem=0, cost=0):
    specs = [pl.BlockSpec(memory_space=pltpu.SMEM)] * smem
    specs += [pl.BlockSpec(memory_space=pltpu.VMEM)] * (len(args) - smem)
    return pl.pallas_call(
        kernel,
        out_shape=outs,
        in_specs=specs,
        out_specs=[pl.BlockSpec(memory_space=pltpu.VMEM)] * len(outs),
        scratch_shapes=list(scratch),
        compiler_params=pltpu.CompilerParams(vmem_limit_bytes=limit),
        cost_estimate=pl.CostEstimate(flops=cost * 10**9, bytes_accessed=MIB, transcendentals=0),
    )(*args)


def split_three(column):
    first = column.astype(jnp.bfloat16)
    left = column - first.astype(jnp.float32)
    second = left.astype(jnp.bfloat16)
    third = (left - second.astype(jnp.float32)).astype(jnp.bfloat16)
    lane = lax.broadcasted_iota(jnp.int32, (column.shape[0], LANES), 1)
    wide = jnp.where(lane == 0, first.astype(jnp.float32), 0.0)
    wide = jnp.where(lane == 1, second.astype(jnp.float32), wide)
    return jnp.where(lane == 2, third.astype(jnp.float32), wide).astype(jnp.bfloat16)


def angle_kernel(lengths_ref, cosine_ref, sine_ref):
    count, halfway = cosine_ref.shape
    step = lax.broadcasted_iota(jnp.int32, (1, halfway), 1).astype(jnp.float32)
    frequency = jnp.exp(step * (-2.0 / HEAD_DIM * math.log(rope_base)))
    angles = jnp.concatenate(
        [lengths_ref[i].astype(jnp.float32) * frequency for i in range(count)], axis=0
    )
    cosine_ref[...] = jnp.cos(angles)
    sine_ref[...] = jnp.sin(angles)


def project_kernel(*refs):
    *block_refs, gain_ref, wq_ref, wk_ref, wv_ref, out_ref, rows_ref = refs
    place = lax.axis_index("tp")
    own = block_refs[0].shape[0]
    for k, block_ref in enumerate(block_refs):
        start = pl.multiple_of((place ^ k) * own, own)
        rows_ref[pl.ds(start, own), :] = block_ref[...].astype(jnp.float32)
    rows = rows_ref[...]
    squares = jnp.sum(rows * rows, axis=1, keepdims=True)
    scaled = (rows * gain_ref[...]).astype(jnp.bfloat16)
    nq, nk = wq_ref.shape[1], wk_ref.shape[1]
    for start, w_ref in ((0, wq_ref), (nq, wk_ref), (nq + nk, wv_ref)):
        out_ref[:, start : start + w_ref.shape[1]] = jnp.dot(
            scaled, w_ref[...], preferred_element_type=jnp.float32
        ).astype(jnp.bfloat16)
    out_ref[:, nq + 2 * nk :] = split_three(squares)


def output_kernel(attended_ref, w_ref, *refs):
    *out_refs, rows_ref = refs
    place = lax.axis_index("tp")
    own = out_refs[0].shape[0]
    rows_ref[...] = jnp.dot(attended_ref[...], w_ref[...], preferred_element_type=jnp.float32)
    for k, out_ref in enumerate(out_refs):
        start = pl.multiple_of((place ^ k) * own, own)
        out_ref[...] = rows_ref[pl.ds(start, own), :].astype(jnp.bfloat16)


def add_kernel(served_ref, stream_ref, *refs):
    *term_refs, out_ref = refs
    own = stream_ref.shape[0]
    start = lax.axis_index("tp") * own
    row = lax.broadcasted_iota(jnp.int32, (own, LANES), 0)
    live = jnp.zeros((own, LANES), jnp.int32)
    for i in range(own):
        live = jnp.where(row == i, served_ref[start + i], live)
    live = live.astype(jnp.float32)[:, :1]
    total = term_refs[0][...].astype(jnp.float32)
    for term_ref in term_refs[1:]:
        total = total + term_ref[...].astype(jnp.float32)
    out_ref[...] = (stream_ref[...].astype(jnp.float32) + live * total).astype(
        jnp.bfloat16
    )


def gate_kernel(*refs):
    *block_refs, gain_ref, w_ref, scaled_ref, keep_ref, send_ref = refs
    rows = jnp.concatenate([ref[...].astype(jnp.float32) for ref in block_refs], axis=0)
    squares = jnp.sum(rows * rows, axis=1, keepdims=True)
    scaled = (rows * gain_ref[...]).astype(jnp.bfloat16)
    scaled_ref[...] = scaled
    width = w_ref.shape[1] // 2
    halves(scaled, w_ref, keep_ref, send_ref, width)
    tail = split_three(squares)
    send_ref[:, width:] = tail
    keep_ref[:, width:] = tail.astype(keep_ref.dtype)


def up_kernel(scaled_ref, w_ref, keep_ref, send_ref):
    halves(scaled_ref[...], w_ref, keep_ref, send_ref, w_ref.shape[1] // 2)


def halves(scaled, w_ref, keep_ref, send_ref, width):
    half = lax.rem(lax.axis_index("role"), 2)
    for side, out_ref in ((1 - half, send_ref), (half, keep_ref)):
        for at in range(0, width, CHUNK):
            size = min(CHUNK, width - at)
            start = pl.multiple_of(side * width + at, LANES)
            out_ref[:, at : at + size] = jnp.dot(
                scaled, w_ref[:, pl.ds(start, size)], preferred_element_type=jnp.float32
            ).astype(out_ref.dtype)


def pair_gate_kernel(keep_ref, got_ref, out_ref):
    wide = out_ref.shape[1] - LANES
    out_ref[:, :wide] = (
        keep_ref[:, :wide] + got_ref[:, :wide].astype(jnp.float32)
    ).astype(jnp.bfloat16)
    squares = jnp.sum(
        keep_ref[:, wide:] + got_ref[:, wide:].astype(jnp.float32), axis=1, keepdims=True
    )
    out_ref[:, wide:] = split_three(squares)


def pair_up_kernel(keep_ref, got_ref, out_ref):
    out_ref[...] = (keep_ref[...] + got_ref[...].astype(jnp.float32)).astype(jnp.bfloat16)


def hidden_kernel(gate_ref, gate_got_ref, up_ref, up_got_ref, out_ref):
    width = out_ref.shape[1]
    squares = jnp.sum(
        gate_ref[:, width:].astype(jnp.float32) + gate_got_ref[:, width:].astype(jnp.float32),
        axis=1,
        keepdims=True,
    )
    inverse = lax.rsqrt(squares / D + epsilon)
    gate = gate_ref[:, :width].astype(jnp.float32) + gate_got_ref[:, :width].astype(jnp.float32)
    up = up_ref[...].astype(jnp.float32) + up_got_ref[...].astype(jnp.float32)
    gate, up = gate * inverse, up * inverse
    out_ref[...] = (gate / (1.0 + jnp.exp(-gate)) * up).astype(jnp.bfloat16)


def down_kernel(own_ref, other_ref, w_ref, *out_refs):
    half = lax.rem(lax.axis_index("role"), 2)
    width = own_ref.shape[1]
    mine = pl.ds(pl.multiple_of(half * width, LANES), width)
    theirs = pl.ds(pl.multiple_of((1 - half) * width, LANES), width)
    own = out_refs[0].shape[0]
    for at in range(0, w_ref.shape[1], CHUNK):
        part = slice(at, min(at + CHUNK, w_ref.shape[1]))
        rows = jnp.dot(own_ref[...], w_ref[mine, part], preferred_element_type=jnp.float32)
        rows = rows + jnp.dot(
            other_ref[...], w_ref[theirs, part], preferred_element_type=jnp.float32
        )
        for k, out_ref in enumerate(out_refs):
            out_ref[:, part] = rows[k * own : (k + 1) * own].astype(jnp.bfloat16)


def local_exchange(
    residual,
    attn_gain,
    w_query,
    w_key,
    w_value,
    w_output,
    cache_keys,
    cache_values,
    lengths,
    served,
    ffn_gain,
    w_gate,
    w_up,
    w_down,
):
    if not exchange_fits(residual, w_query, w_key, w_gate):
        return local(
            residual,
            attn_gain,
            w_query,
            w_key,
            w_value,
            w_output,
            cache_keys,
            cache_values,
            lengths,
            served,
            ffn_gain,
            w_gate,
            w_up,
            w_down,
        )
    tp_count, role_count = lax.axis_size("tp"), lax.axis_size("role")
    devices = tp_count * role_count
    own, features = residual.shape
    rows = own * tp_count
    each = rows // devices
    block = jax.ShapeDtypeStruct((own, features), jnp.bfloat16)

    table = jax.ShapeDtypeStruct((each, HEAD_DIM // 2), jnp.float32)
    cosine, sine = call(angle_kernel, [table] * 2, [lengths], smem=1, cost=COVER)
    blocks = [residual] + [swap(residual, "tp", k) for k in range(1, tp_count)]
    query_cols, kv_cols = w_query.shape[1], w_key.shape[1]
    payload = query_cols + 2 * kv_cols + LANES
    (sums,) = call(
        project_kernel,
        [jax.ShapeDtypeStruct((rows, payload), jnp.bfloat16)],
        [*blocks, attn_gain[None, :], in_vmem(w_query), in_vmem(w_key), in_vmem(w_value)],
        scratch=[pltpu.VMEM((rows, features), jnp.float32)],
    )
    parts = lax.all_to_all(sums.reshape(devices, each, payload), ("role", "tp"), 0, 0)
    parts = parts.reshape(role_count, tp_count, each, payload).astype(jnp.float32)
    gathered = jnp.sum(parts, axis=0).transpose(1, 0, 2)
    squares = jnp.sum(gathered[:, :1, query_cols + 2 * kv_cols :], axis=2, keepdims=True)
    gathered = gathered[:, :, : query_cols + 2 * kv_cols] * lax.rsqrt(squares / D + epsilon)
    queries = gathered[:, :, :query_cols].reshape(each, HEADS, HEAD_DIM)
    new_key = gathered[:, :, query_cols : query_cols + kv_cols].reshape(each, KV_HEADS, HEAD_DIM)
    new_value = (
        gathered[:, :, query_cols + kv_cols :]
        .reshape(each, KV_HEADS, HEAD_DIM)
        .astype(jnp.bfloat16)
    )
    queries = turn(queries, cosine, sine).astype(jnp.bfloat16)
    new_key = turn(new_key, cosine, sine).astype(jnp.bfloat16)
    attended = attend(queries, new_key, new_value, cache_keys, cache_values, lengths)
    by_block = attended.reshape(each, tp_count, query_cols).transpose(1, 0, 2)
    sent = jnp.broadcast_to(by_block[None], (role_count, tp_count, each, query_cols))
    heads = lax.all_to_all(
        sent.reshape(devices, each, query_cols), ("role", "tp"), 0, 0
    ).reshape(rows, query_cols)

    terms = call(
        output_kernel,
        [block] * tp_count,
        [heads, in_vmem(w_output)],
        cost=COVER,
        scratch=[pltpu.VMEM((rows, features), jnp.float32)],
    )
    terms = [terms[0]] + [swap(terms[k], "tp", k) for k in range(1, tp_count)]
    (middle,) = call(add_kernel, [block], [served, residual, *terms], smem=1)

    blocks = [middle] + [swap(middle, "tp", k) for k in range(1, tp_count)]
    width = w_gate.shape[1] // 2
    wide = width + LANES
    scaled, gate, gate_send = call(
        gate_kernel,
        [
            jax.ShapeDtypeStruct((rows, features), jnp.bfloat16),
            jax.ShapeDtypeStruct((rows, wide), jnp.float32),
            jax.ShapeDtypeStruct((rows, wide), jnp.bfloat16),
        ],
        [*blocks, ffn_gain[None, :], in_vmem(w_gate)],
        cost=COVER,
    )
    gate_got = swap(gate_send, "role", 1)
    up, up_send = call(
        up_kernel,
        [
            jax.ShapeDtypeStruct((rows, width), jnp.float32),
            jax.ShapeDtypeStruct((rows, width), jnp.bfloat16),
        ],
        [scaled, in_vmem(w_up)],
        cost=COVER,
    )
    up_got = swap(up_send, "role", 1)
    if role_count > 2:
        (gate,) = call(
            pair_gate_kernel, [jax.ShapeDtypeStruct((rows, wide), jnp.bfloat16)], [gate, gate_got]
        )
        gate_got = swap(gate, "role", 2)
        (up,) = call(
            pair_up_kernel, [jax.ShapeDtypeStruct((rows, width), jnp.bfloat16)], [up, up_got]
        )
        up_got = swap(up, "role", 2)
    (hidden,) = call(
        hidden_kernel,
        [jax.ShapeDtypeStruct((rows, width), jnp.bfloat16)],
        [gate, gate_got, up, up_got],
    )
    other = swap(hidden, "role", 1)
    terms = call(down_kernel, [block] * tp_count, [hidden, other, in_vmem(w_down)])
    terms = [terms[0]] + [swap(terms[k], "tp", k) for k in range(1, tp_count)]
    return call(add_kernel, [block], [served, middle, *terms], smem=1)[0]


def solution(mesh):
    return jax.shard_map(
        local_exchange,
        mesh=mesh,
        in_specs=(
            P(("groups", "tp"), "role"),
            P("role"),
            P("role", "tp"),
            P("role", "tp"),
            P("role", "tp"),
            P("tp", "role"),
            P(("groups", "role", "tp"), None, None),
            P(("groups", "role", "tp"), None, None),
            P(("groups", "role", "tp")),
            P("groups"),
            P("role"),
            P("role", "tp"),
            P("role", "tp"),
            P("tp", "role"),
        ),
        out_specs=P(("groups", "tp"), "role"),
        check_vma=False,
    )
```

```python
import math

import jax
import jax.numpy as jnp
from jax import lax
from jax.experimental import pallas as pl
from jax.experimental.pallas import tpu as pltpu
from jax.sharding import PartitionSpec as P

D = 8192
HEADS = 32
KV_HEADS = 4
HEAD_DIM = 128
WINDOW = 256
GROUP = 8


epsilon = 1e-05
rope_base = 500000.0


def rotate(vectors, positions):
    halfway = vectors.shape[-1] // 2
    frequency = jnp.power(
        jnp.float32(rope_base), -jnp.arange(halfway, dtype=jnp.float32) * 2.0 / vectors.shape[-1]
    )
    angles = positions.astype(jnp.float32)[:, None, None] * frequency[None, None, :]
    cosine = jnp.cos(angles)
    sine_part = jnp.sin(angles)
    leading = vectors[..., :halfway]
    trailing = vectors[..., halfway:]
    return jnp.concatenate(
        [leading * cosine - trailing * sine_part, trailing * cosine + leading * sine_part], axis=-1
    )


def attend(queries, new_key, new_value, keys, values, lengths):
    batch_rows = queries.shape[0]
    factor = HEAD_DIM ** (-0.5)
    grouped = queries.reshape(batch_rows, KV_HEADS, GROUP, HEAD_DIM)
    key_blocks = keys.reshape(batch_rows, WINDOW, KV_HEADS, HEAD_DIM)
    value_blocks = values.reshape(batch_rows, WINDOW, KV_HEADS, HEAD_DIM)
    scores = (
        jnp.einsum("nkgd,nwkd->nkgw", grouped, key_blocks, preferred_element_type=jnp.float32)
        * factor
    )
    self_score = (
        jnp.einsum("nkgd,nkd->nkg", grouped, new_key, preferred_element_type=jnp.float32) * factor
    )
    usable = jnp.arange(WINDOW, dtype=jnp.int32)[None, :] < lengths[:, None]
    scores = jnp.where(usable[:, None, None, :], scores, -jnp.inf)
    highest = jnp.maximum(jnp.max(scores, axis=-1), self_score)
    weights = jnp.exp(scores - highest[..., None])
    self_weight = jnp.exp(self_score - highest)
    denominator = jnp.sum(weights, axis=-1) + self_weight
    chances = (weights / denominator[..., None]).astype(jnp.bfloat16)
    self_chance = (self_weight / denominator).astype(jnp.bfloat16)
    attended = jnp.einsum(
        "nkgw,nwkd->nkgd", chances, value_blocks, preferred_element_type=jnp.float32
    )
    attended = (
        attended
        + self_chance.astype(jnp.float32)[..., None] * new_value.astype(jnp.float32)[:, :, None, :]
    )
    return attended.reshape(batch_rows, HEADS * HEAD_DIM).astype(jnp.bfloat16)


def feed_forward(middle, ffn_gain, w_gate, w_up, w_down):
    widened = middle.astype(jnp.float32)
    squares = lax.psum(jnp.sum(widened * widened, axis=1), "role")
    inverse = lax.rsqrt(squares / D + epsilon)
    mid_normed = (widened * inverse[:, None] * ffn_gain[None, :]).astype(jnp.bfloat16)
    gate_part = jnp.dot(mid_normed, w_gate, preferred_element_type=jnp.float32)
    up_part = jnp.dot(mid_normed, w_up, preferred_element_type=jnp.float32)
    gate_total, up_total = (
        lax.psum(gate_part.astype(jnp.bfloat16), "role").astype(jnp.float32),
        lax.psum(up_part.astype(jnp.bfloat16), "role").astype(jnp.float32),
    )
    hidden = (jax.nn.silu(gate_total) * up_total).astype(jnp.bfloat16)
    down_terms = jnp.dot(hidden, w_down, preferred_element_type=jnp.float32)
    return lax.psum_scatter(
        down_terms.astype(jnp.bfloat16), "tp", scatter_dimension=0, tiled=True
    ).astype(jnp.float32)


def local(
    residual,
    attn_gain,
    w_query,
    w_key,
    w_value,
    w_output,
    cache_keys,
    cache_values,
    lengths,
    served,
    ffn_gain,
    w_gate,
    w_up,
    w_down,
):
    own_rows = residual.shape[0]
    tp_count = lax.axis_size("tp")
    row_start = lax.axis_index("tp") * own_rows
    live_own = lax.dynamic_slice_in_dim(served, row_start, own_rows, 0).astype(jnp.float32)[:, None]
    rows_all = lax.all_gather(residual, "tp", axis=0, tiled=True)
    widened = rows_all.astype(jnp.float32)
    squares = lax.psum(jnp.sum(widened * widened, axis=1), "role")
    inverse = lax.rsqrt(squares / D + epsilon)
    normed = (widened * inverse[:, None] * attn_gain[None, :]).astype(jnp.bfloat16)
    partial_value = jnp.concatenate(
        [
            jnp.dot(normed, w_query, preferred_element_type=jnp.float32),
            jnp.dot(normed, w_key, preferred_element_type=jnp.float32),
            jnp.dot(normed, w_value, preferred_element_type=jnp.float32),
        ],
        axis=1,
    )
    summed = lax.psum_scatter(
        partial_value.astype(jnp.bfloat16), "role", scatter_dimension=0, tiled=True
    ).astype(jnp.float32)
    gathered = lax.all_to_all(
        summed.astype(jnp.bfloat16), "tp", split_axis=0, concat_axis=1, tiled=True
    ).astype(summed.dtype)
    local_rows = gathered.shape[0]
    query_cols = w_query.shape[1]
    kv_cols = w_key.shape[1]
    blocks = gathered.reshape(local_rows, tp_count, query_cols + 2 * kv_cols)
    queries = blocks[:, :, :query_cols].reshape(local_rows, HEADS, HEAD_DIM)
    new_key = blocks[:, :, query_cols : query_cols + kv_cols].reshape(
        local_rows, KV_HEADS, HEAD_DIM
    )
    new_value = (
        blocks[:, :, query_cols + kv_cols :]
        .reshape(local_rows, KV_HEADS, HEAD_DIM)
        .astype(jnp.bfloat16)
    )
    queries = rotate(queries, lengths).astype(jnp.bfloat16)
    new_key = rotate(new_key, lengths).astype(jnp.bfloat16)
    attended = attend(queries, new_key, new_value, cache_keys, cache_values, lengths)
    head_block = lax.all_to_all(attended, "tp", split_axis=1, concat_axis=0, tiled=True)
    attn_terms = jnp.dot(
        lax.all_gather(head_block, "role", axis=0, tiled=True),
        w_output,
        preferred_element_type=jnp.float32,
    )
    attn = lax.psum_scatter(
        attn_terms.astype(jnp.bfloat16), "tp", scatter_dimension=0, tiled=True
    ).astype(jnp.float32)
    middle_own = (residual.astype(jnp.float32) + live_own * attn).astype(jnp.bfloat16)
    middle = lax.all_gather(middle_own, "tp", axis=0, tiled=True)
    ffn = feed_forward(middle, ffn_gain, w_gate, w_up, w_down)
    return (middle_own.astype(jnp.float32) + live_own * ffn).astype(jnp.bfloat16)


LANES = 128
MIB = 2**20
COVER = (100, 100, 100, 100, 1, 1, 1, 1, 1, 1)
CHUNK = 512


def exchange_fits(residual, w_query, w_key, w_gate):
    tp_count, role_count = lax.axis_size("tp"), lax.axis_size("role")
    return (
        tp_count == KV_HEADS
        and role_count == 4
        and residual.shape[0] % 8 == 0
        and w_query.shape[1] == GROUP * LANES
        and w_key.shape[1] == LANES
        and w_gate.shape[1] % (2 * LANES) == 0
    )


def swap(value, axis, distance):
    count = lax.axis_size(axis)
    return lax.ppermute(value, axis, [(i, i ^ distance) for i in range(count)])


def in_vmem(value):
    return pltpu.with_memory_space_constraint(value, pltpu.VMEM)


def call(kernel, outs, args, scratch=(), limit=4 * MIB, smem=0, cost=0):
    specs = [pl.BlockSpec(memory_space=pltpu.SMEM)] * smem
    specs += [pl.BlockSpec(memory_space=pltpu.VMEM)] * (len(args) - smem)
    return pl.pallas_call(
        kernel,
        out_shape=outs,
        in_specs=specs,
        out_specs=[pl.BlockSpec(memory_space=pltpu.VMEM)] * len(outs),
        scratch_shapes=list(scratch),
        compiler_params=pltpu.CompilerParams(vmem_limit_bytes=limit),
        cost_estimate=pl.CostEstimate(flops=cost * 10**9, bytes_accessed=MIB, transcendentals=0),
    )(*args)


def split_three(column):
    first = column.astype(jnp.bfloat16)
    left = column - first.astype(jnp.float32)
    second = left.astype(jnp.bfloat16)
    third = (left - second.astype(jnp.float32)).astype(jnp.bfloat16)
    lane = lax.broadcasted_iota(jnp.int32, (column.shape[0], LANES), 1)
    wide = jnp.where(lane == 0, first.astype(jnp.float32), 0.0)
    wide = jnp.where(lane == 1, second.astype(jnp.float32), wide)
    return jnp.where(lane == 2, third.astype(jnp.float32), wide).astype(jnp.bfloat16)


def angle_kernel(lengths_ref, cosine_ref, sine_ref):
    count, width = cosine_ref.shape
    lane = lax.broadcasted_iota(jnp.int32, (1, width), 1)
    step = lax.rem(lane, width // 2).astype(jnp.float32)
    frequency = jnp.exp(step * (-2.0 / width * math.log(rope_base)))
    angles = jnp.concatenate(
        [lengths_ref[i].astype(jnp.float32) * frequency for i in range(count)], axis=0
    )
    cosine_ref[...] = jnp.cos(angles)
    sine = jnp.sin(angles)
    sine_ref[...] = jnp.where(lane < width // 2, -sine, sine)


def project_kernel(_, *refs):
    *block_refs, gain_ref, wq_ref, wk_ref, wv_ref, out_ref, rows_ref, sums_ref, packed_ref = refs
    place = lax.axis_index("tp")
    own = block_refs[0].shape[0]
    for k, block_ref in enumerate(block_refs):
        start = pl.multiple_of((place ^ k) * own, own)
        rows_ref[pl.ds(start, own), :] = block_ref[...].astype(jnp.float32)
    rows = rows_ref[...]
    squares = jnp.sum(rows * rows, axis=1, keepdims=True)
    scaled = (rows * gain_ref[...]).astype(jnp.bfloat16)
    count = rows.shape[0]
    groups = 0
    for w_ref in (wq_ref, wk_ref, wv_ref):
        product = jnp.dot(scaled, w_ref[...], preferred_element_type=jnp.float32)
        for at in range(0, w_ref.shape[1], LANES):
            sums_ref[groups * count : (groups + 1) * count, :] = product[:, at : at + LANES]
            groups += 1
    sums_ref[groups * count :, :] = split_three(squares).astype(jnp.float32)
    groups += 1
    devices, depth, _ = out_ref.shape
    each = count // devices
    queries = wq_ref.shape[1] // LANES
    packed_ref[...] = jnp.zeros_like(packed_ref)
    for n in range(each):
        for g in range(groups):
            row = packed_row(n, g, each, queries, groups)
            packed_ref[pl.ds(row, devices, stride=depth), :] = sums_ref[
                pl.ds(g * count + n, devices, stride=each), :
            ]
    out_ref[...] = packed_ref[...].reshape(out_ref.shape).astype(jnp.bfloat16)


def packed_row(n, g, each, queries, groups):
    if g < queries:
        return n * queries + g
    return each * queries + n * (groups - queries) + g - queries


def attend_kernel(
    lengths_ref, got_ref, cosine_ref, sine_ref, keys_ref, values_ref, out_ref
):
    tp_count = KV_HEADS
    devices, depth, width = got_ref.shape
    each, window, _ = keys_ref.shape
    groups = GROUP + 3
    total = jnp.sum(
        got_ref[...].astype(jnp.float32).reshape(devices // tp_count, tp_count, depth, width),
        axis=0,
    )
    factor = HEAD_DIM ** (-0.5)
    scores, own_scores, own_values = [], [], []
    for n in range(each):
        cosine, sine = cosine_ref[n : n + 1, :], sine_ref[n : n + 1, :]
        tail = packed_row(n, GROUP, each, GROUP, groups)
        squares = jnp.sum(total[0, tail + 2 : tail + 3, :], axis=1, keepdims=True)
        inverse = lax.rsqrt(squares / D + epsilon)
        usable = lax.broadcasted_iota(jnp.int32, (GROUP, window), 1) < lengths_ref[n]
        for h in range(tp_count):
            query = total[h, n * GROUP : (n + 1) * GROUP, :] * inverse
            key = total[h, tail : tail + 1, :] * inverse
            query = query * cosine + pltpu.roll(query, width // 2, 1) * sine
            key = key * cosine + pltpu.roll(key, width // 2, 1) * sine
            query = query.astype(jnp.bfloat16)
            key = key.astype(jnp.bfloat16).astype(jnp.float32)
            score = lax.dot_general(
                query,
                keys_ref[n, :, h * width : (h + 1) * width],
                (((1,), (1,)), ((), ())),
                preferred_element_type=jnp.float32,
            )
            scores.append(jnp.where(usable, score * factor, -jnp.inf))
            own_scores.append(
                jnp.sum(query.astype(jnp.float32) * key, axis=1, keepdims=True) * factor
            )
            value = (total[h, tail + 1 : tail + 2, :] * inverse).astype(jnp.bfloat16)
            own_values.append(value.astype(jnp.float32))
    scores, own_scores = jnp.concatenate(scores, axis=0), jnp.concatenate(own_scores, axis=0)
    highest = jnp.maximum(jnp.max(scores, axis=1, keepdims=True), own_scores)
    weights, own_weights = jnp.exp(scores - highest), jnp.exp(own_scores - highest)
    denominator = jnp.sum(weights, axis=1, keepdims=True) + own_weights
    chances = (weights / denominator).astype(jnp.bfloat16)
    own_chances = (own_weights / denominator).astype(jnp.bfloat16).astype(jnp.float32)
    for n in range(each):
        for h in range(tp_count):
            at = (n * tp_count + h) * GROUP
            attended = jnp.dot(
                chances[at : at + GROUP],
                values_ref[n, :, h * width : (h + 1) * width],
                preferred_element_type=jnp.float32,
            )
            attended = attended + own_chances[at : at + GROUP] * own_values[n * tp_count + h]
            for r in range(devices // tp_count):
                out_ref[r * tp_count + h, n * GROUP : (n + 1) * GROUP, :] = attended.astype(
                    jnp.bfloat16
                )


def output_kernel(heads_ref, w_ref, *refs):
    *out_refs, heads_wide_ref, rows_ref = refs
    place = lax.axis_index("tp")
    own = out_refs[0].shape[0]
    groups = w_ref.shape[0] // LANES
    heads_wide_ref[...] = heads_ref[...].astype(jnp.float32).reshape(heads_wide_ref.shape)
    attended = jnp.concatenate(
        [heads_wide_ref[pl.ds(g, rows_ref.shape[0], stride=groups), :] for g in range(groups)],
        axis=1,
    ).astype(jnp.bfloat16)
    rows_ref[...] = jnp.dot(attended, w_ref[...], preferred_element_type=jnp.float32)
    for k, out_ref in enumerate(out_refs):
        start = pl.multiple_of((place ^ k) * own, own)
        out_ref[...] = rows_ref[pl.ds(start, own), :].astype(jnp.bfloat16)


def add_kernel(served_ref, stream_ref, *refs):
    *term_refs, out_ref = refs
    own = stream_ref.shape[0]
    start = lax.axis_index("tp") * own
    row = lax.broadcasted_iota(jnp.int32, (own, LANES), 0)
    live = jnp.zeros((own, LANES), jnp.int32)
    for i in range(own):
        live = jnp.where(row == i, served_ref[start + i], live)
    live = live.astype(jnp.float32)[:, :1]
    total = term_refs[0][...].astype(jnp.float32)
    for term_ref in term_refs[1:]:
        total = total + term_ref[...].astype(jnp.float32)
    out_ref[...] = (stream_ref[...].astype(jnp.float32) + live * total).astype(
        jnp.bfloat16
    )


def gate_send_kernel(*refs):
    *block_refs, gain_ref, w_ref, scaled_ref, tail_ref, send_ref = refs
    rows = jnp.concatenate([ref[...].astype(jnp.float32) for ref in block_refs], axis=0)
    squares = jnp.sum(rows * rows, axis=1, keepdims=True)
    scaled = (rows * gain_ref[...]).astype(jnp.bfloat16)
    scaled_ref[...] = scaled
    half = lax.rem(lax.axis_index("role"), 2)
    one_half(scaled, w_ref, send_ref, 1 - half)
    tail = split_three(squares)
    send_ref[:, w_ref.shape[1] // 2 :] = tail
    tail_ref[...] = tail.astype(jnp.float32)


def send_kernel(scaled_ref, w_ref, send_ref):
    half = lax.rem(lax.axis_index("role"), 2)
    one_half(scaled_ref[...], w_ref, send_ref, 1 - half)


def keep_kernel(scaled_ref, w_ref, keep_ref):
    half = lax.rem(lax.axis_index("role"), 2)
    one_half(scaled_ref[...], w_ref, keep_ref, half)


def one_half(scaled, w_ref, out_ref, side):
    width = w_ref.shape[1] // 2
    for at in range(0, width, CHUNK):
        size = min(CHUNK, width - at)
        start = pl.multiple_of(side * width + at, LANES)
        out_ref[:, at : at + size] = jnp.dot(
            scaled, w_ref[:, pl.ds(start, size)], preferred_element_type=jnp.float32
        ).astype(out_ref.dtype)


def pair_gate_kernel(keep_ref, tail_ref, got_ref, out_ref):
    wide = keep_ref.shape[1]
    out_ref[:, :wide] = (keep_ref[...] + got_ref[:, :wide].astype(jnp.float32)).astype(
        jnp.bfloat16
    )
    squares = jnp.sum(
        tail_ref[...] + got_ref[:, wide:].astype(jnp.float32), axis=1, keepdims=True
    )
    out_ref[:, wide:] = split_three(squares)


def pair_up_kernel(keep_ref, got_ref, out_ref):
    out_ref[...] = (keep_ref[...] + got_ref[...].astype(jnp.float32)).astype(jnp.bfloat16)


def hidden_kernel(gate_ref, gate_got_ref, up_ref, up_got_ref, out_ref):
    width = out_ref.shape[1]
    squares = jnp.sum(
        gate_ref[:, width:].astype(jnp.float32) + gate_got_ref[:, width:].astype(jnp.float32),
        axis=1,
        keepdims=True,
    )
    inverse = lax.rsqrt(squares / D + epsilon)
    gate = gate_ref[:, :width].astype(jnp.float32) + gate_got_ref[:, :width].astype(jnp.float32)
    up = up_ref[...].astype(jnp.float32) + up_got_ref[...].astype(jnp.float32)
    gate, up = gate * inverse, up * inverse
    out_ref[...] = (gate / (1.0 + jnp.exp(-gate)) * up).astype(jnp.bfloat16)


def down_own_kernel(own_ref, w_ref, rows_ref):
    half = lax.rem(lax.axis_index("role"), 2)
    width = own_ref.shape[1]
    mine = pl.ds(pl.multiple_of(half * width, LANES), width)
    for at in range(0, w_ref.shape[1], CHUNK):
        part = slice(at, min(at + CHUNK, w_ref.shape[1]))
        rows_ref[:, part] = jnp.dot(
            own_ref[...], w_ref[mine, part], preferred_element_type=jnp.float32
        )


def down_kernel(other_ref, w_ref, rows_ref, *out_refs):
    half = lax.rem(lax.axis_index("role"), 2)
    width = other_ref.shape[1]
    theirs = pl.ds(pl.multiple_of((1 - half) * width, LANES), width)
    own = out_refs[0].shape[0]
    for at in range(0, w_ref.shape[1], CHUNK):
        part = slice(at, min(at + CHUNK, w_ref.shape[1]))
        rows = rows_ref[:, part] + jnp.dot(
            other_ref[...], w_ref[theirs, part], preferred_element_type=jnp.float32
        )
        for k, out_ref in enumerate(out_refs):
            out_ref[:, part] = rows[k * own : (k + 1) * own].astype(jnp.bfloat16)


def local_exchange(
    residual,
    attn_gain,
    w_query,
    w_key,
    w_value,
    w_output,
    cache_keys,
    cache_values,
    lengths,
    served,
    ffn_gain,
    w_gate,
    w_up,
    w_down,
):
    if not exchange_fits(residual, w_query, w_key, w_gate):
        return local(
            residual,
            attn_gain,
            w_query,
            w_key,
            w_value,
            w_output,
            cache_keys,
            cache_values,
            lengths,
            served,
            ffn_gain,
            w_gate,
            w_up,
            w_down,
        )
    tp_count, role_count = lax.axis_size("tp"), lax.axis_size("role")
    devices = tp_count * role_count
    own, features = residual.shape
    rows = own * tp_count
    each = rows // devices
    block = jax.ShapeDtypeStruct((own, features), jnp.bfloat16)

    table = jax.ShapeDtypeStruct((each, HEAD_DIM), jnp.float32)
    cosine, sine = call(angle_kernel, [table] * 2, [lengths], smem=1, cost=COVER[0])
    blocks = [residual] + [swap(residual, "tp", k) for k in range(1, tp_count)]
    payload = w_query.shape[1] + 2 * w_key.shape[1] + LANES
    depth = -(-each * payload // (LANES * 8)) * 8
    (sums,) = call(
        project_kernel,
        [jax.ShapeDtypeStruct((devices, depth, LANES), jnp.bfloat16)],
        [cosine, *blocks, attn_gain[None, :], in_vmem(w_query), in_vmem(w_key), in_vmem(w_value)],
        scratch=[
            pltpu.VMEM((rows, features), jnp.float32),
            pltpu.VMEM((rows * payload // LANES, LANES), jnp.float32),
            pltpu.VMEM((devices * depth, LANES), jnp.float32),
        ],
        cost=COVER[1],
    )
    parts = lax.all_to_all(sums, ("role", "tp"), 0, 0)
    (heads,) = call(
        attend_kernel,
        [jax.ShapeDtypeStruct((devices, each * GROUP, LANES), jnp.bfloat16)],
        [lengths, parts, cosine, sine, in_vmem(cache_keys), in_vmem(cache_values)],
        smem=1,
        cost=COVER[2],
    )
    heads = lax.all_to_all(heads, ("role", "tp"), 0, 0)
    terms = call(
        output_kernel,
        [block] * tp_count,
        [heads, in_vmem(w_output)],
        scratch=[
            pltpu.VMEM((rows * GROUP, LANES), jnp.float32),
            pltpu.VMEM((rows, features), jnp.float32),
        ],
        cost=COVER[3],
    )
    terms = [terms[0]] + [swap(terms[k], "tp", k) for k in range(1, tp_count)]
    (middle,) = call(add_kernel, [block], [served, residual, *terms], smem=1)

    blocks = [middle] + [swap(middle, "tp", k) for k in range(1, tp_count)]
    width = w_gate.shape[1] // 2
    wide = width + LANES
    half_f32 = jax.ShapeDtypeStruct((rows, width), jnp.float32)
    half_bf16 = jax.ShapeDtypeStruct((rows, width), jnp.bfloat16)
    wide_bf16 = jax.ShapeDtypeStruct((rows, wide), jnp.bfloat16)
    w_gate, w_up, w_down = in_vmem(w_gate), in_vmem(w_up), in_vmem(w_down)
    scaled, tail, gate_send = call(
        gate_send_kernel,
        [
            jax.ShapeDtypeStruct((rows, features), jnp.bfloat16),
            jax.ShapeDtypeStruct((rows, LANES), jnp.float32),
            wide_bf16,
        ],
        [*blocks, ffn_gain[None, :], w_gate],
        cost=COVER[4],
    )
    gate_got = swap(gate_send, "role", 1)
    (gate,) = call(keep_kernel, [half_f32], [scaled, w_gate], cost=COVER[5])
    (gate,) = call(pair_gate_kernel, [wide_bf16], [gate, tail, gate_got])
    (up_send,) = call(send_kernel, [half_bf16], [scaled, w_up], cost=COVER[6])
    up_got = swap(up_send, "role", 1)
    (up,) = call(keep_kernel, [half_f32], [scaled, w_up], cost=COVER[7])
    (up,) = call(pair_up_kernel, [half_bf16], [up, up_got])
    gate_got, up_got = swap(gate, "role", 2), swap(up, "role", 2)
    (hidden,) = call(
        hidden_kernel,
        [half_bf16],
        [gate, gate_got, up, up_got],
    )
    other = swap(hidden, "role", 1)
    (down,) = call(
        down_own_kernel,
        [jax.ShapeDtypeStruct((rows, features), jnp.float32)],
        [hidden, w_down],
        cost=COVER[8],
    )
    terms = call(down_kernel, [block] * tp_count, [other, w_down, down], cost=COVER[9])
    terms = [terms[0]] + [swap(terms[k], "tp", k) for k in range(1, tp_count)]
    return call(add_kernel, [block], [served, middle, *terms], smem=1)[0]


def solution(mesh):
    return jax.shard_map(
        local_exchange,
        mesh=mesh,
        in_specs=(
            P(("groups", "tp"), "role"),
            P("role"),
            P("role", "tp"),
            P("role", "tp"),
            P("role", "tp"),
            P("tp", "role"),
            P(("groups", "role", "tp"), None, None),
            P(("groups", "role", "tp"), None, None),
            P(("groups", "role", "tp")),
            P("groups"),
            P("role"),
            P("role", "tp"),
            P("role", "tp"),
            P("tp", "role"),
        ),
        out_specs=P(("groups", "tp"), "role"),
        check_vma=False,
    )
```

```python
import math

import jax
import jax.numpy as jnp
from jax import lax
from jax.experimental import pallas as pl
from jax.experimental.pallas import tpu as pltpu
from jax.sharding import PartitionSpec as P

D = 8192
HEADS = 32
KV_HEADS = 4
HEAD_DIM = 128
WINDOW = 256
GROUP = 8


epsilon = 1e-05
rope_base = 500000.0


def rotate(vectors, positions):
    halfway = vectors.shape[-1] // 2
    frequency = jnp.power(
        jnp.float32(rope_base), -jnp.arange(halfway, dtype=jnp.float32) * 2.0 / vectors.shape[-1]
    )
    angles = positions.astype(jnp.float32)[:, None, None] * frequency[None, None, :]
    cosine = jnp.cos(angles)
    sine_part = jnp.sin(angles)
    leading = vectors[..., :halfway]
    trailing = vectors[..., halfway:]
    return jnp.concatenate(
        [leading * cosine - trailing * sine_part, trailing * cosine + leading * sine_part], axis=-1
    )


def attend(queries, new_key, new_value, keys, values, lengths):
    batch_rows = queries.shape[0]
    factor = HEAD_DIM ** (-0.5)
    grouped = queries.reshape(batch_rows, KV_HEADS, GROUP, HEAD_DIM)
    key_blocks = keys.reshape(batch_rows, WINDOW, KV_HEADS, HEAD_DIM)
    value_blocks = values.reshape(batch_rows, WINDOW, KV_HEADS, HEAD_DIM)
    scores = (
        jnp.einsum("nkgd,nwkd->nkgw", grouped, key_blocks, preferred_element_type=jnp.float32)
        * factor
    )
    self_score = (
        jnp.einsum("nkgd,nkd->nkg", grouped, new_key, preferred_element_type=jnp.float32) * factor
    )
    usable = jnp.arange(WINDOW, dtype=jnp.int32)[None, :] < lengths[:, None]
    scores = jnp.where(usable[:, None, None, :], scores, -jnp.inf)
    highest = jnp.maximum(jnp.max(scores, axis=-1), self_score)
    weights = jnp.exp(scores - highest[..., None])
    self_weight = jnp.exp(self_score - highest)
    denominator = jnp.sum(weights, axis=-1) + self_weight
    chances = (weights / denominator[..., None]).astype(jnp.bfloat16)
    self_chance = (self_weight / denominator).astype(jnp.bfloat16)
    attended = jnp.einsum(
        "nkgw,nwkd->nkgd", chances, value_blocks, preferred_element_type=jnp.float32
    )
    attended = (
        attended
        + self_chance.astype(jnp.float32)[..., None] * new_value.astype(jnp.float32)[:, :, None, :]
    )
    return attended.reshape(batch_rows, HEADS * HEAD_DIM).astype(jnp.bfloat16)


def feed_forward(middle, ffn_gain, w_gate, w_up, w_down):
    widened = middle.astype(jnp.float32)
    squares = lax.psum(jnp.sum(widened * widened, axis=1), "role")
    inverse = lax.rsqrt(squares / D + epsilon)
    mid_normed = (widened * inverse[:, None] * ffn_gain[None, :]).astype(jnp.bfloat16)
    gate_part = jnp.dot(mid_normed, w_gate, preferred_element_type=jnp.float32)
    up_part = jnp.dot(mid_normed, w_up, preferred_element_type=jnp.float32)
    gate_total, up_total = (
        lax.psum(gate_part.astype(jnp.bfloat16), "role").astype(jnp.float32),
        lax.psum(up_part.astype(jnp.bfloat16), "role").astype(jnp.float32),
    )
    hidden = (jax.nn.silu(gate_total) * up_total).astype(jnp.bfloat16)
    down_terms = jnp.dot(hidden, w_down, preferred_element_type=jnp.float32)
    return lax.psum_scatter(
        down_terms.astype(jnp.bfloat16), "tp", scatter_dimension=0, tiled=True
    ).astype(jnp.float32)


def local(
    residual,
    attn_gain,
    w_query,
    w_key,
    w_value,
    w_output,
    cache_keys,
    cache_values,
    lengths,
    served,
    ffn_gain,
    w_gate,
    w_up,
    w_down,
):
    own_rows = residual.shape[0]
    tp_count = lax.axis_size("tp")
    row_start = lax.axis_index("tp") * own_rows
    live_own = lax.dynamic_slice_in_dim(served, row_start, own_rows, 0).astype(jnp.float32)[:, None]
    rows_all = lax.all_gather(residual, "tp", axis=0, tiled=True)
    widened = rows_all.astype(jnp.float32)
    squares = lax.psum(jnp.sum(widened * widened, axis=1), "role")
    inverse = lax.rsqrt(squares / D + epsilon)
    normed = (widened * inverse[:, None] * attn_gain[None, :]).astype(jnp.bfloat16)
    partial_value = jnp.concatenate(
        [
            jnp.dot(normed, w_query, preferred_element_type=jnp.float32),
            jnp.dot(normed, w_key, preferred_element_type=jnp.float32),
            jnp.dot(normed, w_value, preferred_element_type=jnp.float32),
        ],
        axis=1,
    )
    summed = lax.psum_scatter(
        partial_value.astype(jnp.bfloat16), "role", scatter_dimension=0, tiled=True
    ).astype(jnp.float32)
    gathered = lax.all_to_all(
        summed.astype(jnp.bfloat16), "tp", split_axis=0, concat_axis=1, tiled=True
    ).astype(summed.dtype)
    local_rows = gathered.shape[0]
    query_cols = w_query.shape[1]
    kv_cols = w_key.shape[1]
    blocks = gathered.reshape(local_rows, tp_count, query_cols + 2 * kv_cols)
    queries = blocks[:, :, :query_cols].reshape(local_rows, HEADS, HEAD_DIM)
    new_key = blocks[:, :, query_cols : query_cols + kv_cols].reshape(
        local_rows, KV_HEADS, HEAD_DIM
    )
    new_value = (
        blocks[:, :, query_cols + kv_cols :]
        .reshape(local_rows, KV_HEADS, HEAD_DIM)
        .astype(jnp.bfloat16)
    )
    queries = rotate(queries, lengths).astype(jnp.bfloat16)
    new_key = rotate(new_key, lengths).astype(jnp.bfloat16)
    attended = attend(queries, new_key, new_value, cache_keys, cache_values, lengths)
    head_block = lax.all_to_all(attended, "tp", split_axis=1, concat_axis=0, tiled=True)
    attn_terms = jnp.dot(
        lax.all_gather(head_block, "role", axis=0, tiled=True),
        w_output,
        preferred_element_type=jnp.float32,
    )
    attn = lax.psum_scatter(
        attn_terms.astype(jnp.bfloat16), "tp", scatter_dimension=0, tiled=True
    ).astype(jnp.float32)
    middle_own = (residual.astype(jnp.float32) + live_own * attn).astype(jnp.bfloat16)
    middle = lax.all_gather(middle_own, "tp", axis=0, tiled=True)
    ffn = feed_forward(middle, ffn_gain, w_gate, w_up, w_down)
    return (middle_own.astype(jnp.float32) + live_own * ffn).astype(jnp.bfloat16)


LANES = 128
MIB = 2**20
COVER = (100, 100, 100, 1, 1, 1, 1, 1, 1, 1)
CHUNK = 512


def exchange_fits(residual, w_query, w_key, w_gate):
    tp_count, role_count = lax.axis_size("tp"), lax.axis_size("role")
    return (
        tp_count == KV_HEADS
        and role_count == 4
        and residual.shape[0] % 8 == 0
        and w_query.shape[1] == GROUP * LANES
        and w_key.shape[1] == LANES
        and w_gate.shape[1] % (2 * LANES) == 0
    )


def swap(value, axis, distance):
    count = lax.axis_size(axis)
    return lax.ppermute(value, axis, [(i, i ^ distance) for i in range(count)])


def in_vmem(value):
    return pltpu.with_memory_space_constraint(value, pltpu.VMEM)


def call(kernel, outs, args, scratch=(), limit=4 * MIB, smem=0, cost=0):
    specs = [pl.BlockSpec(memory_space=pltpu.SMEM)] * smem
    specs += [pl.BlockSpec(memory_space=pltpu.VMEM)] * (len(args) - smem)
    return pl.pallas_call(
        kernel,
        out_shape=outs,
        in_specs=specs,
        out_specs=[pl.BlockSpec(memory_space=pltpu.VMEM)] * len(outs),
        scratch_shapes=list(scratch),
        compiler_params=pltpu.CompilerParams(vmem_limit_bytes=limit),
        cost_estimate=pl.CostEstimate(flops=cost * 10**9, bytes_accessed=MIB, transcendentals=0),
    )(*args)


def split_three(column):
    first = column.astype(jnp.bfloat16)
    left = column - first.astype(jnp.float32)
    second = left.astype(jnp.bfloat16)
    third = (left - second.astype(jnp.float32)).astype(jnp.bfloat16)
    lane = lax.broadcasted_iota(jnp.int32, (column.shape[0], LANES), 1)
    wide = jnp.where(lane == 0, first.astype(jnp.float32), 0.0)
    wide = jnp.where(lane == 1, second.astype(jnp.float32), wide)
    return jnp.where(lane == 2, third.astype(jnp.float32), wide).astype(jnp.bfloat16)


def angle_kernel(lengths_ref, cosine_ref, sine_ref):
    count, width = cosine_ref.shape
    lane = lax.broadcasted_iota(jnp.int32, (1, width), 1)
    step = lax.rem(lane, width // 2).astype(jnp.float32)
    frequency = jnp.exp(step * (-2.0 / width * math.log(rope_base)))
    angles = jnp.concatenate(
        [lengths_ref[i].astype(jnp.float32) * frequency for i in range(count)], axis=0
    )
    cosine_ref[...] = jnp.cos(angles)
    sine = jnp.sin(angles)
    sine_ref[...] = jnp.where(lane < width // 2, -sine, sine)


def project_kernel(_, *refs):
    *block_refs, gain_ref, wq_ref, wk_ref, wv_ref, out_ref, stream_ref = refs[:-3]
    rows_ref, sums_ref, packed_ref = refs[-3:]
    place = lax.axis_index("tp")
    own = block_refs[0].shape[0]
    for k, block_ref in enumerate(block_refs):
        start = pl.multiple_of((place ^ k) * own, own)
        rows_ref[pl.ds(start, own), :] = block_ref[...].astype(jnp.float32)
    rows = rows_ref[...]
    stream_ref[...] = rows.astype(jnp.bfloat16)
    squares = jnp.sum(rows * rows, axis=1, keepdims=True)
    scaled = (rows * gain_ref[...]).astype(jnp.bfloat16)
    count = rows.shape[0]
    groups = 0
    for w_ref in (wq_ref, wk_ref, wv_ref):
        product = jnp.dot(scaled, w_ref[...], preferred_element_type=jnp.float32)
        for at in range(0, w_ref.shape[1], LANES):
            sums_ref[groups * count : (groups + 1) * count, :] = product[:, at : at + LANES]
            groups += 1
    sums_ref[groups * count :, :] = split_three(squares).astype(jnp.float32)
    groups += 1
    devices, depth, _ = out_ref.shape
    each = count // devices
    queries = wq_ref.shape[1] // LANES
    packed_ref[...] = jnp.zeros_like(packed_ref)
    for n in range(each):
        for g in range(groups):
            row = packed_row(n, g, each, queries, groups)
            packed_ref[pl.ds(row, devices, stride=depth), :] = sums_ref[
                pl.ds(g * count + n, devices, stride=each), :
            ]
    out_ref[...] = packed_ref[...].reshape(out_ref.shape).astype(jnp.bfloat16)


def packed_row(n, g, each, queries, groups):
    if g < queries:
        return n * queries + g
    return each * queries + n * (groups - queries) + g - queries


def attend_kernel(
    lengths_ref, got_ref, cosine_ref, sine_ref, keys_ref, values_ref, out_ref
):
    tp_count = KV_HEADS
    devices, depth, width = got_ref.shape
    each, window, _ = keys_ref.shape
    groups = GROUP + 3
    total = jnp.sum(
        got_ref[...].astype(jnp.float32).reshape(devices // tp_count, tp_count, depth, width),
        axis=0,
    )
    factor = HEAD_DIM ** (-0.5)
    scores, own_scores, own_values = [], [], []
    for n in range(each):
        cosine, sine = cosine_ref[n : n + 1, :], sine_ref[n : n + 1, :]
        tail = packed_row(n, GROUP, each, GROUP, groups)
        squares = jnp.sum(total[0, tail + 2 : tail + 3, :], axis=1, keepdims=True)
        inverse = lax.rsqrt(squares / D + epsilon)
        usable = lax.broadcasted_iota(jnp.int32, (GROUP, window), 1) < lengths_ref[n]
        for h in range(tp_count):
            query = total[h, n * GROUP : (n + 1) * GROUP, :] * inverse
            key = total[h, tail : tail + 1, :] * inverse
            query = query * cosine + pltpu.roll(query, width // 2, 1) * sine
            key = key * cosine + pltpu.roll(key, width // 2, 1) * sine
            query = query.astype(jnp.bfloat16)
            key = key.astype(jnp.bfloat16).astype(jnp.float32)
            score = lax.dot_general(
                query,
                keys_ref[n, :, h * width : (h + 1) * width],
                (((1,), (1,)), ((), ())),
                preferred_element_type=jnp.float32,
            )
            scores.append(jnp.where(usable, score * factor, -jnp.inf))
            own_scores.append(
                jnp.sum(query.astype(jnp.float32) * key, axis=1, keepdims=True) * factor
            )
            value = (total[h, tail + 1 : tail + 2, :] * inverse).astype(jnp.bfloat16)
            own_values.append(value.astype(jnp.float32))
    scores, own_scores = jnp.concatenate(scores, axis=0), jnp.concatenate(own_scores, axis=0)
    highest = jnp.maximum(jnp.max(scores, axis=1, keepdims=True), own_scores)
    weights, own_weights = jnp.exp(scores - highest), jnp.exp(own_scores - highest)
    denominator = jnp.sum(weights, axis=1, keepdims=True) + own_weights
    chances = (weights / denominator).astype(jnp.bfloat16)
    own_chances = (own_weights / denominator).astype(jnp.bfloat16).astype(jnp.float32)
    for n in range(each):
        for h in range(tp_count):
            at = (n * tp_count + h) * GROUP
            attended = jnp.dot(
                chances[at : at + GROUP],
                values_ref[n, :, h * width : (h + 1) * width],
                preferred_element_type=jnp.float32,
            )
            attended = attended + own_chances[at : at + GROUP] * own_values[n * tp_count + h]
            for r in range(devices // tp_count):
                out_ref[r * tp_count + h, n * GROUP : (n + 1) * GROUP, :] = attended.astype(
                    jnp.bfloat16
                )


def output_kernel(heads_ref, w_ref, *refs):
    *out_refs, heads_wide_ref = refs
    count = sum(ref.shape[0] for ref in out_refs)
    groups = w_ref.shape[0] // LANES
    heads_wide_ref[...] = heads_ref[...].astype(jnp.float32).reshape(heads_wide_ref.shape)
    attended = jnp.concatenate(
        [heads_wide_ref[pl.ds(g, count, stride=groups), :] for g in range(groups)], axis=1
    ).astype(jnp.bfloat16)
    for at in range(0, w_ref.shape[1], CHUNK):
        part = slice(at, min(at + CHUNK, w_ref.shape[1]))
        rows = jnp.dot(attended, w_ref[:, part], preferred_element_type=jnp.float32)
        start = 0
        for out_ref in out_refs:
            out_ref[:, part] = rows[start : start + out_ref.shape[0]].astype(jnp.bfloat16)
            start += out_ref.shape[0]


def add_kernel(served_ref, stream_ref, *refs):
    *term_refs, out_ref = refs
    own = stream_ref.shape[0]
    start = lax.axis_index("tp") * own
    row = lax.broadcasted_iota(jnp.int32, (own, LANES), 0)
    live = jnp.zeros((own, LANES), jnp.int32)
    for i in range(own):
        live = jnp.where(row == i, served_ref[start + i], live)
    live = live.astype(jnp.float32)[:, :1]
    total = term_refs[0][...].astype(jnp.float32)
    for term_ref in term_refs[1:]:
        total = total + term_ref[...].astype(jnp.float32)
    out_ref[...] = (stream_ref[...].astype(jnp.float32) + live * total).astype(
        jnp.bfloat16
    )


def gate_send_kernel(*refs):
    served_ref, stream_ref, *term_refs, gain_ref, w_ref = refs[:-5]
    scaled_ref, tail_ref, send_ref, middle_ref, rows_ref = refs[-5:]
    count = stream_ref.shape[0]
    row = lax.broadcasted_iota(jnp.int32, (count, count), 0)
    column = lax.broadcasted_iota(jnp.int32, (count, count), 1)
    live = jnp.sum(
        jnp.where(row == column, served_ref[...], 0).astype(jnp.float32), axis=1, keepdims=True
    )
    pieces = len(term_refs) // 2
    attn = jnp.concatenate(
        [
            term_refs[2 * i][...].astype(jnp.float32) + term_refs[2 * i + 1][...].astype(jnp.float32)
            for i in range(pieces)
        ],
        axis=0,
    )
    rows = (stream_ref[...].astype(jnp.float32) + live * attn).astype(jnp.bfloat16)
    rows = rows.astype(jnp.float32)
    rows_ref[...] = rows
    own = middle_ref.shape[0]
    start = pl.multiple_of(lax.axis_index("tp") * own, own)
    middle_ref[...] = rows_ref[pl.ds(start, own), :].astype(jnp.bfloat16)
    squares = jnp.sum(rows * rows, axis=1, keepdims=True)
    scaled = (rows * gain_ref[...]).astype(jnp.bfloat16)
    scaled_ref[...] = scaled
    half = lax.rem(lax.axis_index("role"), 2)
    one_half(scaled, w_ref, send_ref, 1 - half)
    tail = split_three(squares)
    send_ref[:, w_ref.shape[1] // 2 :] = tail
    tail_ref[...] = tail.astype(jnp.float32)


def send_kernel(scaled_ref, w_ref, send_ref):
    half = lax.rem(lax.axis_index("role"), 2)
    one_half(scaled_ref[...], w_ref, send_ref, 1 - half)


def keep_kernel(scaled_ref, w_ref, keep_ref):
    half = lax.rem(lax.axis_index("role"), 2)
    one_half(scaled_ref[...], w_ref, keep_ref, half)


def one_half(scaled, w_ref, out_ref, side):
    width = w_ref.shape[1] // 2
    for at in range(0, width, CHUNK):
        size = min(CHUNK, width - at)
        start = pl.multiple_of(side * width + at, LANES)
        out_ref[:, at : at + size] = jnp.dot(
            scaled, w_ref[:, pl.ds(start, size)], preferred_element_type=jnp.float32
        ).astype(out_ref.dtype)


def pair_gate_kernel(keep_ref, tail_ref, got_ref, out_ref):
    wide = keep_ref.shape[1]
    out_ref[:, :wide] = (keep_ref[...] + got_ref[:, :wide].astype(jnp.float32)).astype(
        jnp.bfloat16
    )
    squares = jnp.sum(
        tail_ref[...] + got_ref[:, wide:].astype(jnp.float32), axis=1, keepdims=True
    )
    out_ref[:, wide:] = split_three(squares)


def pair_kernel(keep_ref, got_ref, out_ref):
    out_ref[...] = (keep_ref[...].astype(jnp.float32) + got_ref[...].astype(jnp.float32)).astype(jnp.bfloat16)


def hidden_kernel(gate_ref, gate_got_ref, up_ref, up_got_ref, out_ref):
    width = out_ref.shape[1]
    squares = jnp.sum(
        gate_ref[:, width:].astype(jnp.float32) + gate_got_ref[:, width:].astype(jnp.float32),
        axis=1,
        keepdims=True,
    )
    inverse = lax.rsqrt(squares / D + epsilon)
    gate = gate_ref[:, :width].astype(jnp.float32) + gate_got_ref[:, :width].astype(jnp.float32)
    up = up_ref[...].astype(jnp.float32) + up_got_ref[...].astype(jnp.float32)
    gate, up = gate * inverse, up * inverse
    out_ref[...] = (gate / (1.0 + jnp.exp(-gate)) * up).astype(jnp.bfloat16)


def down_own_kernel(own_ref, w_ref, rows_ref):
    half = lax.rem(lax.axis_index("role"), 2)
    width = own_ref.shape[1]
    mine = pl.ds(pl.multiple_of(half * width, LANES), width)
    for at in range(0, w_ref.shape[1], CHUNK):
        part = slice(at, min(at + CHUNK, w_ref.shape[1]))
        rows_ref[:, part] = jnp.dot(
            own_ref[...], w_ref[mine, part], preferred_element_type=jnp.float32
        )


def down_kernel(other_ref, w_ref, rows_ref, *refs):
    *out_refs, total_ref = refs
    half = lax.rem(lax.axis_index("role"), 2)
    place = lax.axis_index("tp")
    width = other_ref.shape[1]
    theirs = pl.ds(pl.multiple_of((1 - half) * width, LANES), width)
    own = out_refs[0].shape[0]
    for at in range(0, w_ref.shape[1], CHUNK):
        part = slice(at, min(at + CHUNK, w_ref.shape[1]))
        total_ref[:, part] = rows_ref[:, part] + jnp.dot(
            other_ref[...], w_ref[theirs, part], preferred_element_type=jnp.float32
        )
    for k, out_ref in enumerate(out_refs):
        start = pl.multiple_of((place ^ k) * own, own)
        out_ref[...] = total_ref[pl.ds(start, own), :].astype(jnp.bfloat16)


def local_exchange(
    residual,
    attn_gain,
    w_query,
    w_key,
    w_value,
    w_output,
    cache_keys,
    cache_values,
    lengths,
    served,
    ffn_gain,
    w_gate,
    w_up,
    w_down,
):
    if not exchange_fits(residual, w_query, w_key, w_gate):
        return local(
            residual,
            attn_gain,
            w_query,
            w_key,
            w_value,
            w_output,
            cache_keys,
            cache_values,
            lengths,
            served,
            ffn_gain,
            w_gate,
            w_up,
            w_down,
        )
    tp_count, role_count = lax.axis_size("tp"), lax.axis_size("role")
    devices = tp_count * role_count
    own, features = residual.shape
    rows = own * tp_count
    each = rows // devices
    block = jax.ShapeDtypeStruct((own, features), jnp.bfloat16)

    table = jax.ShapeDtypeStruct((each, HEAD_DIM), jnp.float32)
    cosine, sine = call(angle_kernel, [table] * 2, [lengths], smem=1, cost=COVER[0])
    others = {k: swap(residual, "tp", k) for k in reversed(range(1, tp_count))}
    blocks = [residual] + [others[k] for k in range(1, tp_count)]
    payload = w_query.shape[1] + 2 * w_key.shape[1] + LANES
    depth = -(-each * payload // (LANES * 8)) * 8
    sums, stream = call(
        project_kernel,
        [
            jax.ShapeDtypeStruct((devices, depth, LANES), jnp.bfloat16),
            jax.ShapeDtypeStruct((rows, features), jnp.bfloat16),
        ],
        [cosine, *blocks, attn_gain[None, :], in_vmem(w_query), in_vmem(w_key), in_vmem(w_value)],
        scratch=[
            pltpu.VMEM((rows, features), jnp.float32),
            pltpu.VMEM((rows * payload // LANES, LANES), jnp.float32),
            pltpu.VMEM((devices * depth, LANES), jnp.float32),
        ],
        cost=COVER[1],
    )
    parts = lax.all_to_all(sums, ("role", "tp"), 0, 0)
    (heads,) = call(
        attend_kernel,
        [jax.ShapeDtypeStruct((devices, each * GROUP, LANES), jnp.bfloat16)],
        [lengths, parts, cosine, sine, in_vmem(cache_keys), in_vmem(cache_values)],
        smem=1,
        cost=COVER[2],
    )
    heads = lax.all_to_all(heads, ("role", "tp"), 0, 0)
    pieces = 2
    piece = jax.ShapeDtypeStruct((rows // pieces, features), jnp.bfloat16)
    attn = call(
        output_kernel,
        [piece] * pieces,
        [heads, in_vmem(w_output)],
        scratch=[pltpu.VMEM((rows * GROUP, LANES), jnp.float32)],
        cost=COVER[3],
    )
    terms = []
    near = [swap(value, "tp", 1) for value in attn]
    for value, got in zip(attn, near):
        (paired,) = call(pair_kernel, [piece], [value, got])
        terms += [paired, swap(paired, "tp", 2)]
    width = w_gate.shape[1] // 2
    wide = width + LANES
    half_f32 = jax.ShapeDtypeStruct((rows, width), jnp.float32)
    half_bf16 = jax.ShapeDtypeStruct((rows, width), jnp.bfloat16)
    wide_bf16 = jax.ShapeDtypeStruct((rows, wide), jnp.bfloat16)
    w_gate, w_up, w_down = in_vmem(w_gate), in_vmem(w_up), in_vmem(w_down)
    scaled, tail, gate_send, middle = call(
        gate_send_kernel,
        [
            jax.ShapeDtypeStruct((rows, features), jnp.bfloat16),
            jax.ShapeDtypeStruct((rows, LANES), jnp.float32),
            wide_bf16,
            block,
        ],
        [served[None, :], stream, *terms, ffn_gain[None, :], w_gate],
        scratch=[pltpu.VMEM((rows, features), jnp.float32)],
        cost=COVER[4],
    )
    gate_got = swap(gate_send, "role", 1)
    (gate,) = call(keep_kernel, [half_f32], [scaled, w_gate], cost=COVER[5])
    (gate,) = call(pair_gate_kernel, [wide_bf16], [gate, tail, gate_got])
    (up_send,) = call(send_kernel, [half_bf16], [scaled, w_up], cost=COVER[6])
    up_got = swap(up_send, "role", 1)
    (up,) = call(keep_kernel, [half_f32], [scaled, w_up], cost=COVER[7])
    (up,) = call(pair_kernel, [half_bf16], [up, up_got])
    gate_got, up_got = swap(gate, "role", 2), swap(up, "role", 2)
    (hidden,) = call(
        hidden_kernel,
        [half_bf16],
        [gate, gate_got, up, up_got],
    )
    other = swap(hidden, "role", 1)
    (down,) = call(
        down_own_kernel,
        [jax.ShapeDtypeStruct((rows, features), jnp.float32)],
        [hidden, w_down],
        cost=COVER[8],
    )
    terms = call(
        down_kernel,
        [block] * tp_count,
        [other, w_down, down],
        scratch=[pltpu.VMEM((rows, features), jnp.float32)],
        cost=COVER[9],
    )
    terms = [terms[0]] + [swap(terms[k], "tp", k) for k in range(1, tp_count)]
    return call(add_kernel, [block], [served, middle, *terms], smem=1)[0]


def solution(mesh):
    return jax.shard_map(
        local_exchange,
        mesh=mesh,
        in_specs=(
            P(("groups", "tp"), "role"),
            P("role"),
            P("role", "tp"),
            P("role", "tp"),
            P("role", "tp"),
            P("tp", "role"),
            P(("groups", "role", "tp"), None, None),
            P(("groups", "role", "tp"), None, None),
            P(("groups", "role", "tp")),
            P("groups"),
            P("role"),
            P("role", "tp"),
            P("role", "tp"),
            P("tp", "role"),
        ),
        out_specs=P(("groups", "tp"), "role"),
        check_vma=False,
    )
```

```python
import functools
import math

import jax
import jax.numpy as jnp
from jax import lax
from jax.experimental import pallas as pl
from jax.experimental.pallas import tpu as pltpu
from jax.sharding import PartitionSpec as P

D = 8192
HEADS = 32
KV_HEADS = 4
HEAD_DIM = 128
WINDOW = 256
GROUP = 8


epsilon = 1e-05
rope_base = 500000.0


def rotate(vectors, positions):
    halfway = vectors.shape[-1] // 2
    frequency = jnp.power(
        jnp.float32(rope_base), -jnp.arange(halfway, dtype=jnp.float32) * 2.0 / vectors.shape[-1]
    )
    angles = positions.astype(jnp.float32)[:, None, None] * frequency[None, None, :]
    cosine = jnp.cos(angles)
    sine_part = jnp.sin(angles)
    leading = vectors[..., :halfway]
    trailing = vectors[..., halfway:]
    return jnp.concatenate(
        [leading * cosine - trailing * sine_part, trailing * cosine + leading * sine_part], axis=-1
    )


def attend(queries, new_key, new_value, keys, values, lengths):
    batch_rows = queries.shape[0]
    factor = HEAD_DIM ** (-0.5)
    grouped = queries.reshape(batch_rows, KV_HEADS, GROUP, HEAD_DIM)
    key_blocks = keys.reshape(batch_rows, WINDOW, KV_HEADS, HEAD_DIM)
    value_blocks = values.reshape(batch_rows, WINDOW, KV_HEADS, HEAD_DIM)
    scores = (
        jnp.einsum("nkgd,nwkd->nkgw", grouped, key_blocks, preferred_element_type=jnp.float32)
        * factor
    )
    self_score = (
        jnp.einsum("nkgd,nkd->nkg", grouped, new_key, preferred_element_type=jnp.float32) * factor
    )
    usable = jnp.arange(WINDOW, dtype=jnp.int32)[None, :] < lengths[:, None]
    scores = jnp.where(usable[:, None, None, :], scores, -jnp.inf)
    highest = jnp.maximum(jnp.max(scores, axis=-1), self_score)
    weights = jnp.exp(scores - highest[..., None])
    self_weight = jnp.exp(self_score - highest)
    denominator = jnp.sum(weights, axis=-1) + self_weight
    chances = (weights / denominator[..., None]).astype(jnp.bfloat16)
    self_chance = (self_weight / denominator).astype(jnp.bfloat16)
    attended = jnp.einsum(
        "nkgw,nwkd->nkgd", chances, value_blocks, preferred_element_type=jnp.float32
    )
    attended = (
        attended
        + self_chance.astype(jnp.float32)[..., None] * new_value.astype(jnp.float32)[:, :, None, :]
    )
    return attended.reshape(batch_rows, HEADS * HEAD_DIM).astype(jnp.bfloat16)


def feed_forward(middle, ffn_gain, w_gate, w_up, w_down):
    widened = middle.astype(jnp.float32)
    squares = lax.psum(jnp.sum(widened * widened, axis=1), "role")
    inverse = lax.rsqrt(squares / D + epsilon)
    mid_normed = (widened * inverse[:, None] * ffn_gain[None, :]).astype(jnp.bfloat16)
    gate_part = jnp.dot(mid_normed, w_gate, preferred_element_type=jnp.float32)
    up_part = jnp.dot(mid_normed, w_up, preferred_element_type=jnp.float32)
    gate_total, up_total = (
        lax.psum(gate_part.astype(jnp.bfloat16), "role").astype(jnp.float32),
        lax.psum(up_part.astype(jnp.bfloat16), "role").astype(jnp.float32),
    )
    hidden = (jax.nn.silu(gate_total) * up_total).astype(jnp.bfloat16)
    down_terms = jnp.dot(hidden, w_down, preferred_element_type=jnp.float32)
    return lax.psum_scatter(
        down_terms.astype(jnp.bfloat16), "tp", scatter_dimension=0, tiled=True
    ).astype(jnp.float32)


def local(
    residual,
    attn_gain,
    w_query,
    w_key,
    w_value,
    w_output,
    cache_keys,
    cache_values,
    lengths,
    served,
    ffn_gain,
    w_gate,
    w_up,
    w_down,
):
    own_rows = residual.shape[0]
    tp_count = lax.axis_size("tp")
    row_start = lax.axis_index("tp") * own_rows
    live_own = lax.dynamic_slice_in_dim(served, row_start, own_rows, 0).astype(jnp.float32)[:, None]
    rows_all = lax.all_gather(residual, "tp", axis=0, tiled=True)
    widened = rows_all.astype(jnp.float32)
    squares = lax.psum(jnp.sum(widened * widened, axis=1), "role")
    inverse = lax.rsqrt(squares / D + epsilon)
    normed = (widened * inverse[:, None] * attn_gain[None, :]).astype(jnp.bfloat16)
    partial_value = jnp.concatenate(
        [
            jnp.dot(normed, w_query, preferred_element_type=jnp.float32),
            jnp.dot(normed, w_key, preferred_element_type=jnp.float32),
            jnp.dot(normed, w_value, preferred_element_type=jnp.float32),
        ],
        axis=1,
    )
    summed = lax.psum_scatter(
        partial_value.astype(jnp.bfloat16), "role", scatter_dimension=0, tiled=True
    ).astype(jnp.float32)
    gathered = lax.all_to_all(
        summed.astype(jnp.bfloat16), "tp", split_axis=0, concat_axis=1, tiled=True
    ).astype(summed.dtype)
    local_rows = gathered.shape[0]
    query_cols = w_query.shape[1]
    kv_cols = w_key.shape[1]
    blocks = gathered.reshape(local_rows, tp_count, query_cols + 2 * kv_cols)
    queries = blocks[:, :, :query_cols].reshape(local_rows, HEADS, HEAD_DIM)
    new_key = blocks[:, :, query_cols : query_cols + kv_cols].reshape(
        local_rows, KV_HEADS, HEAD_DIM
    )
    new_value = (
        blocks[:, :, query_cols + kv_cols :]
        .reshape(local_rows, KV_HEADS, HEAD_DIM)
        .astype(jnp.bfloat16)
    )
    queries = rotate(queries, lengths).astype(jnp.bfloat16)
    new_key = rotate(new_key, lengths).astype(jnp.bfloat16)
    attended = attend(queries, new_key, new_value, cache_keys, cache_values, lengths)
    head_block = lax.all_to_all(attended, "tp", split_axis=1, concat_axis=0, tiled=True)
    attn_terms = jnp.dot(
        lax.all_gather(head_block, "role", axis=0, tiled=True),
        w_output,
        preferred_element_type=jnp.float32,
    )
    attn = lax.psum_scatter(
        attn_terms.astype(jnp.bfloat16), "tp", scatter_dimension=0, tiled=True
    ).astype(jnp.float32)
    middle_own = (residual.astype(jnp.float32) + live_own * attn).astype(jnp.bfloat16)
    middle = lax.all_gather(middle_own, "tp", axis=0, tiled=True)
    ffn = feed_forward(middle, ffn_gain, w_gate, w_up, w_down)
    return (middle_own.astype(jnp.float32) + live_own * ffn).astype(jnp.bfloat16)


LANES = 128
MIB = 2**20
COVER = (100, 100, 100, 1, 10, 10, 10, 1, 1, 1)
CHUNK = 512
FIRST_PART = 57


def exchange_fits(residual, w_query, w_key, w_gate):
    tp_count, role_count = lax.axis_size("tp"), lax.axis_size("role")
    return (
        tp_count == KV_HEADS
        and role_count == 4
        and residual.shape[0] % 8 == 0
        and w_query.shape[1] == GROUP * LANES
        and w_key.shape[1] == LANES
        and w_gate.shape[1] % (4 * LANES) == 0
        and w_gate.shape[1] >= 8 * LANES
    )


def swap(value, axis, distance):
    count = lax.axis_size(axis)
    return lax.ppermute(value, axis, [(i, i ^ distance) for i in range(count)])


def in_vmem(value):
    return pltpu.with_memory_space_constraint(value, pltpu.VMEM)


def call(kernel, outs, args, scratch=(), limit=4 * MIB, smem=0, cost=0):
    specs = [pl.BlockSpec(memory_space=pltpu.SMEM)] * smem
    specs += [pl.BlockSpec(memory_space=pltpu.VMEM)] * (len(args) - smem)
    return pl.pallas_call(
        kernel,
        out_shape=outs,
        in_specs=specs,
        out_specs=[pl.BlockSpec(memory_space=pltpu.VMEM)] * len(outs),
        scratch_shapes=list(scratch),
        compiler_params=pltpu.CompilerParams(vmem_limit_bytes=limit),
        cost_estimate=pl.CostEstimate(flops=cost * 10**9, bytes_accessed=MIB, transcendentals=0),
    )(*args)


def split_three(column):
    first = column.astype(jnp.bfloat16)
    left = column - first.astype(jnp.float32)
    second = left.astype(jnp.bfloat16)
    third = (left - second.astype(jnp.float32)).astype(jnp.bfloat16)
    lane = lax.broadcasted_iota(jnp.int32, (column.shape[0], LANES), 1)
    wide = jnp.where(lane == 0, first.astype(jnp.float32), 0.0)
    wide = jnp.where(lane == 1, second.astype(jnp.float32), wide)
    return jnp.where(lane == 2, third.astype(jnp.float32), wide).astype(jnp.bfloat16)


def angle_kernel(lengths_ref, cosine_ref, sine_ref):
    count, width = cosine_ref.shape
    lane = lax.broadcasted_iota(jnp.int32, (1, width), 1)
    step = lax.rem(lane, width // 2).astype(jnp.float32)
    frequency = jnp.exp(step * (-2.0 / width * math.log(rope_base)))
    angles = jnp.concatenate(
        [lengths_ref[i].astype(jnp.float32) * frequency for i in range(count)], axis=0
    )
    cosine_ref[...] = jnp.cos(angles)
    sine = jnp.sin(angles)
    sine_ref[...] = jnp.where(lane < width // 2, -sine, sine)


def project_kernel(_, *refs):
    *block_refs, gain_ref, wq_ref, wk_ref, wv_ref, out_ref, stream_ref = refs[:-3]
    rows_ref, sums_ref, packed_ref = refs[-3:]
    place = lax.axis_index("tp")
    own = block_refs[0].shape[0]
    for k, block_ref in enumerate(block_refs):
        start = pl.multiple_of((place ^ k) * own, own)
        rows_ref[pl.ds(start, own), :] = block_ref[...].astype(jnp.float32)
    rows = rows_ref[...]
    stream_ref[...] = rows.astype(jnp.bfloat16)
    squares = jnp.sum(rows * rows, axis=1, keepdims=True)
    scaled = (rows * gain_ref[...]).astype(jnp.bfloat16)
    count = rows.shape[0]
    groups = 0
    for w_ref in (wq_ref, wk_ref, wv_ref):
        product = jnp.dot(scaled, w_ref[...], preferred_element_type=jnp.float32)
        for at in range(0, w_ref.shape[1], LANES):
            sums_ref[groups * count : (groups + 1) * count, :] = product[:, at : at + LANES]
            groups += 1
    sums_ref[groups * count :, :] = split_three(squares).astype(jnp.float32)
    groups += 1
    devices, depth, _ = out_ref.shape
    each = count // devices
    queries = wq_ref.shape[1] // LANES
    packed_ref[...] = jnp.zeros_like(packed_ref)
    for n in range(each):
        for g in range(groups):
            row = packed_row(n, g, each, queries, groups)
            packed_ref[pl.ds(row, devices, stride=depth), :] = sums_ref[
                pl.ds(g * count + n, devices, stride=each), :
            ]
    out_ref[...] = packed_ref[...].reshape(out_ref.shape).astype(jnp.bfloat16)


def packed_row(n, g, each, queries, groups):
    if g < queries:
        return n * queries + g
    return each * queries + n * (groups - queries) + g - queries


def attend_kernel(
    lengths_ref, got_ref, cosine_ref, sine_ref, keys_ref, values_ref, out_ref
):
    tp_count = KV_HEADS
    devices, depth, width = got_ref.shape
    each, window, _ = keys_ref.shape
    groups = GROUP + 3
    total = jnp.sum(
        got_ref[...].astype(jnp.float32).reshape(devices // tp_count, tp_count, depth, width),
        axis=0,
    )
    factor = HEAD_DIM ** (-0.5)
    scores, own_scores, own_values = [], [], []
    for n in range(each):
        cosine, sine = cosine_ref[n : n + 1, :], sine_ref[n : n + 1, :]
        tail = packed_row(n, GROUP, each, GROUP, groups)
        squares = jnp.sum(total[0, tail + 2 : tail + 3, :], axis=1, keepdims=True)
        inverse = lax.rsqrt(squares / D + epsilon)
        usable = lax.broadcasted_iota(jnp.int32, (GROUP, window), 1) < lengths_ref[n]
        for h in range(tp_count):
            query = total[h, n * GROUP : (n + 1) * GROUP, :] * inverse
            key = total[h, tail : tail + 1, :] * inverse
            query = query * cosine + pltpu.roll(query, width // 2, 1) * sine
            key = key * cosine + pltpu.roll(key, width // 2, 1) * sine
            query = query.astype(jnp.bfloat16)
            key = key.astype(jnp.bfloat16).astype(jnp.float32)
            score = lax.dot_general(
                query,
                keys_ref[n, :, h * width : (h + 1) * width],
                (((1,), (1,)), ((), ())),
                preferred_element_type=jnp.float32,
            )
            scores.append(jnp.where(usable, score * factor, -jnp.inf))
            own_scores.append(
                jnp.sum(query.astype(jnp.float32) * key, axis=1, keepdims=True) * factor
            )
            value = (total[h, tail + 1 : tail + 2, :] * inverse).astype(jnp.bfloat16)
            own_values.append(value.astype(jnp.float32))
    scores, own_scores = jnp.concatenate(scores, axis=0), jnp.concatenate(own_scores, axis=0)
    highest = jnp.maximum(jnp.max(scores, axis=1, keepdims=True), own_scores)
    weights, own_weights = jnp.exp(scores - highest), jnp.exp(own_scores - highest)
    denominator = jnp.sum(weights, axis=1, keepdims=True) + own_weights
    chances = (weights / denominator).astype(jnp.bfloat16)
    own_chances = (own_weights / denominator).astype(jnp.bfloat16).astype(jnp.float32)
    for n in range(each):
        for h in range(tp_count):
            at = (n * tp_count + h) * GROUP
            attended = jnp.dot(
                chances[at : at + GROUP],
                values_ref[n, :, h * width : (h + 1) * width],
                preferred_element_type=jnp.float32,
            )
            attended = attended + own_chances[at : at + GROUP] * own_values[n * tp_count + h]
            for r in range(devices // tp_count):
                out_ref[r * tp_count + h, n * GROUP : (n + 1) * GROUP, :] = attended.astype(
                    jnp.bfloat16
                )


def output_kernel(heads_ref, w_ref, *refs):
    *out_refs, heads_wide_ref = refs
    count = sum(ref.shape[0] for ref in out_refs)
    groups = w_ref.shape[0] // LANES
    heads_wide_ref[...] = heads_ref[...].astype(jnp.float32).reshape(heads_wide_ref.shape)
    attended = jnp.concatenate(
        [heads_wide_ref[pl.ds(g, count, stride=groups), :] for g in range(groups)], axis=1
    ).astype(jnp.bfloat16)
    for at in range(0, w_ref.shape[1], CHUNK):
        part = slice(at, min(at + CHUNK, w_ref.shape[1]))
        rows = jnp.dot(attended, w_ref[:, part], preferred_element_type=jnp.float32)
        start = 0
        for out_ref in out_refs:
            out_ref[:, part] = rows[start : start + out_ref.shape[0]].astype(jnp.bfloat16)
            start += out_ref.shape[0]


def add_kernel(served_ref, stream_ref, *refs):
    *term_refs, out_ref = refs
    own = stream_ref.shape[0]
    start = lax.axis_index("tp") * own
    row = lax.broadcasted_iota(jnp.int32, (own, LANES), 0)
    live = jnp.zeros((own, LANES), jnp.int32)
    for i in range(own):
        live = jnp.where(row == i, served_ref[start + i], live)
    live = live.astype(jnp.float32)[:, :1]
    total = term_refs[0][...].astype(jnp.float32)
    for term_ref in term_refs[1:]:
        total = total + term_ref[...].astype(jnp.float32)
    out_ref[...] = (stream_ref[...].astype(jnp.float32) + live * total).astype(
        jnp.bfloat16
    )


def middle_kernel(*refs):
    served_ref, stream_ref, *term_refs, gain_ref, wg_ref, wu_ref = refs[:-5]
    scaled_ref, tail_ref, send_ref, middle_ref, rows_ref = refs[-5:]
    count = stream_ref.shape[0]
    row = lax.broadcasted_iota(jnp.int32, (count, count), 0)
    column = lax.broadcasted_iota(jnp.int32, (count, count), 1)
    live = jnp.sum(
        jnp.where(row == column, served_ref[...], 0).astype(jnp.float32), axis=1, keepdims=True
    )
    pieces = len(term_refs) // 2
    attn = jnp.concatenate(
        [
            term_refs[2 * i][...].astype(jnp.float32) + term_refs[2 * i + 1][...].astype(jnp.float32)
            for i in range(pieces)
        ],
        axis=0,
    )
    rows = (stream_ref[...].astype(jnp.float32) + live * attn).astype(jnp.bfloat16)
    rows = rows.astype(jnp.float32)
    rows_ref[...] = rows
    own = middle_ref.shape[0]
    start = pl.multiple_of(lax.axis_index("tp") * own, own)
    middle_ref[...] = rows_ref[pl.ds(start, own), :].astype(jnp.bfloat16)
    squares = jnp.sum(rows * rows, axis=1, keepdims=True)
    scaled_ref[...] = (rows * gain_ref[...]).astype(jnp.bfloat16)
    half = lax.rem(lax.axis_index("role"), 2)
    size = (send_ref.shape[1] - LANES) // 2
    piece_dots(scaled_ref, wg_ref, wu_ref, send_ref, 1 - half, 0, size)
    tail = split_three(squares)
    send_ref[:, 2 * size :] = tail
    tail_ref[...] = tail.astype(jnp.float32)


def piece_kernel(theirs, begin, size, scaled_ref, wg_ref, wu_ref, *refs):
    half = lax.rem(lax.axis_index("role"), 2)
    side = 1 - half if theirs else half
    piece_dots(scaled_ref, wg_ref, wu_ref, refs[-1], side, begin, size)


def piece_dots(scaled_ref, wg_ref, wu_ref, out_ref, side, begin, size):
    scaled = scaled_ref[...]
    first = side * (wg_ref.shape[1] // 2) + begin
    for w_ref, base in ((wg_ref, 0), (wu_ref, size)):
        for at in range(0, size, CHUNK):
            step = min(CHUNK, size - at)
            start = pl.multiple_of(first + at, LANES)
            out_ref[:, base + at : base + at + step] = jnp.dot(
                scaled, w_ref[:, pl.ds(start, step)], preferred_element_type=jnp.float32
            ).astype(out_ref.dtype)


def pair_tail_kernel(keep_ref, tail_ref, got_ref, out_ref):
    wide = keep_ref.shape[1]
    out_ref[:, :wide] = (keep_ref[...] + got_ref[:, :wide].astype(jnp.float32)).astype(
        jnp.bfloat16
    )
    squares = jnp.sum(
        tail_ref[...] + got_ref[:, wide:].astype(jnp.float32), axis=1, keepdims=True
    )
    out_ref[:, wide:] = split_three(squares)


def pair_kernel(keep_ref, got_ref, out_ref):
    out_ref[...] = (
        keep_ref[...].astype(jnp.float32) + got_ref[...].astype(jnp.float32)
    ).astype(jnp.bfloat16)


def first_hidden_kernel(own_ref, got_ref, hidden_ref, inverse_ref):
    wide = 2 * hidden_ref.shape[1]
    squares = jnp.sum(
        own_ref[:, wide:].astype(jnp.float32) + got_ref[:, wide:].astype(jnp.float32),
        axis=1,
        keepdims=True,
    )
    inverse = lax.rsqrt(squares / D + epsilon)
    inverse_ref[...] = jnp.broadcast_to(inverse, inverse_ref.shape)
    gated(own_ref, got_ref, inverse, hidden_ref)


def hidden_kernel(own_ref, got_ref, inverse_ref, _, hidden_ref):
    gated(own_ref, got_ref, inverse_ref[:, :1], hidden_ref)


def gated(own_ref, got_ref, inverse, hidden_ref):
    size = hidden_ref.shape[1]
    total = own_ref[:, : 2 * size].astype(jnp.float32) + got_ref[:, : 2 * size].astype(jnp.float32)
    total = total * inverse
    gate, up = total[:, :size], total[:, size:]
    hidden_ref[...] = (gate / (1.0 + jnp.exp(-gate)) * up).astype(jnp.bfloat16)


def down_dots(theirs, begin, hidden_ref, w_ref, part):
    half = lax.rem(lax.axis_index("role"), 2)
    side = 1 - half if theirs else half
    start = pl.multiple_of(side * (w_ref.shape[0] // 2) + begin, LANES)
    return jnp.dot(
        hidden_ref[...],
        w_ref[pl.ds(start, hidden_ref.shape[1]), part],
        preferred_element_type=jnp.float32,
    )


def chunks(width):
    return [slice(at, min(at + CHUNK, width)) for at in range(0, width, CHUNK)]


def down_kernel(theirs, begin, hidden_ref, w_ref, *refs):
    *before_refs, rows_ref = refs
    for part in chunks(w_ref.shape[1]):
        rows = down_dots(theirs, begin, hidden_ref, w_ref, part)
        for before_ref in before_refs:
            rows = rows + before_ref[:, part]
        rows_ref[:, part] = rows


def last_down_kernel(theirs, begin, hidden_ref, w_ref, before_ref, *refs):
    *out_refs, rows_ref = refs
    place = lax.axis_index("tp")
    own = out_refs[0].shape[0]
    for part in chunks(w_ref.shape[1]):
        rows_ref[:, part] = before_ref[:, part] + down_dots(
            theirs, begin, hidden_ref, w_ref, part
        )
    for k, out_ref in enumerate(out_refs):
        start = pl.multiple_of((place ^ k) * own, own)
        out_ref[...] = rows_ref[pl.ds(start, own), :].astype(jnp.bfloat16)


def local_exchange(
    residual,
    attn_gain,
    w_query,
    w_key,
    w_value,
    w_output,
    cache_keys,
    cache_values,
    lengths,
    served,
    ffn_gain,
    w_gate,
    w_up,
    w_down,
):
    if not exchange_fits(residual, w_query, w_key, w_gate):
        return local(
            residual,
            attn_gain,
            w_query,
            w_key,
            w_value,
            w_output,
            cache_keys,
            cache_values,
            lengths,
            served,
            ffn_gain,
            w_gate,
            w_up,
            w_down,
        )
    tp_count, role_count = lax.axis_size("tp"), lax.axis_size("role")
    devices = tp_count * role_count
    own, features = residual.shape
    rows = own * tp_count
    each = rows // devices
    block = jax.ShapeDtypeStruct((own, features), jnp.bfloat16)

    table = jax.ShapeDtypeStruct((each, HEAD_DIM), jnp.float32)
    cosine, sine = call(angle_kernel, [table] * 2, [lengths], smem=1, cost=COVER[0])
    others = {k: swap(residual, "tp", k) for k in reversed(range(1, tp_count))}
    blocks = [residual] + [others[k] for k in range(1, tp_count)]
    payload = w_query.shape[1] + 2 * w_key.shape[1] + LANES
    depth = -(-each * payload // (LANES * 8)) * 8
    sums, stream = call(
        project_kernel,
        [
            jax.ShapeDtypeStruct((devices, depth, LANES), jnp.bfloat16),
            jax.ShapeDtypeStruct((rows, features), jnp.bfloat16),
        ],
        [cosine, *blocks, attn_gain[None, :], in_vmem(w_query), in_vmem(w_key), in_vmem(w_value)],
        scratch=[
            pltpu.VMEM((rows, features), jnp.float32),
            pltpu.VMEM((rows * payload // LANES, LANES), jnp.float32),
            pltpu.VMEM((devices * depth, LANES), jnp.float32),
        ],
        cost=COVER[1],
    )
    parts = lax.all_to_all(sums, ("role", "tp"), 0, 0)
    (heads,) = call(
        attend_kernel,
        [jax.ShapeDtypeStruct((devices, each * GROUP, LANES), jnp.bfloat16)],
        [lengths, parts, cosine, sine, in_vmem(cache_keys), in_vmem(cache_values)],
        smem=1,
        cost=COVER[2],
    )
    heads = lax.all_to_all(heads, ("role", "tp"), 0, 0)
    pieces = 2
    piece = jax.ShapeDtypeStruct((rows // pieces, features), jnp.bfloat16)
    attn = call(
        output_kernel,
        [piece] * pieces,
        [heads, in_vmem(w_output)],
        scratch=[pltpu.VMEM((rows * GROUP, LANES), jnp.float32)],
        cost=COVER[3],
    )
    terms = []
    near = [swap(value, "tp", 1) for value in attn]
    for value, got in zip(attn, near):
        (paired,) = call(pair_kernel, [piece], [value, got])
        terms += [paired, swap(paired, "tp", 2)]
    width = w_gate.shape[1] // 2
    first = -(-width * FIRST_PART // (100 * 2 * LANES)) * 2 * LANES
    sizes = (first, width - first)
    w_gate, w_up, w_down = in_vmem(w_gate), in_vmem(w_up), in_vmem(w_down)
    rows_f32 = jax.ShapeDtypeStruct((rows, features), jnp.float32)
    row_scratch = pltpu.VMEM((rows, features), jnp.float32)

    def wide(size, dtype, more=0):
        return jax.ShapeDtypeStruct((rows, 2 * size + more), dtype)

    def half_of(piece):
        return jax.ShapeDtypeStruct((rows, sizes[piece]), jnp.bfloat16)

    scaled, tail, send, middle = call(
        middle_kernel,
        [
            jax.ShapeDtypeStruct((rows, features), jnp.bfloat16),
            jax.ShapeDtypeStruct((rows, LANES), jnp.float32),
            wide(sizes[0], jnp.bfloat16, LANES),
            block,
        ],
        [served[None, :], stream, *terms, ffn_gain[None, :], w_gate, w_up],
        scratch=[row_scratch],
        cost=COVER[4],
    )
    got = swap(send, "role", 1)
    (keep,) = call(
        functools.partial(piece_kernel, False, 0, sizes[0]),
        [wide(sizes[0], jnp.float32)],
        [scaled, w_gate, w_up],
        cost=COVER[5],
    )
    (chip_0,) = call(
        pair_tail_kernel, [wide(sizes[0], jnp.bfloat16, LANES)], [keep, tail, got]
    )
    far_0 = swap(chip_0, "role", 2)
    (send,) = call(
        functools.partial(piece_kernel, True, sizes[0], sizes[1]),
        [wide(sizes[1], jnp.bfloat16)],
        [scaled, w_gate, w_up, chip_0],
        cost=COVER[6],
    )
    got = swap(send, "role", 1)
    (keep,) = call(
        functools.partial(piece_kernel, False, sizes[0], sizes[1]),
        [wide(sizes[1], jnp.float32)],
        [scaled, w_gate, w_up],
        cost=COVER[7],
    )
    (chip_1,) = call(pair_kernel, [wide(sizes[1], jnp.bfloat16)], [keep, got])
    far_1 = swap(chip_1, "role", 2)
    hidden, inverse = call(
        first_hidden_kernel,
        [half_of(0), jax.ShapeDtypeStruct((rows, LANES), jnp.float32)],
        [chip_0, far_0],
    )
    other = swap(hidden, "role", 1)
    (down,) = call(
        functools.partial(down_kernel, False, 0), [rows_f32], [hidden, w_down], cost=COVER[8]
    )
    (down,) = call(
        functools.partial(down_kernel, True, 0), [rows_f32], [other, w_down, down], cost=COVER[8]
    )
    (hidden,) = call(hidden_kernel, [half_of(1)], [chip_1, far_1, inverse, down])
    other = swap(hidden, "role", 1)
    (down,) = call(
        functools.partial(down_kernel, False, sizes[0]),
        [rows_f32],
        [hidden, w_down, down],
        cost=COVER[9],
    )
    terms = call(
        functools.partial(last_down_kernel, True, sizes[0]),
        [block] * tp_count,
        [other, w_down, down],
        scratch=[row_scratch],
        cost=COVER[9],
    )
    terms = [terms[0]] + [swap(terms[k], "tp", k) for k in range(1, tp_count)]
    return call(add_kernel, [block], [served, middle, *terms], smem=1)[0]


def solution(mesh):
    return jax.shard_map(
        local_exchange,
        mesh=mesh,
        in_specs=(
            P(("groups", "tp"), "role"),
            P("role"),
            P("role", "tp"),
            P("role", "tp"),
            P("role", "tp"),
            P("tp", "role"),
            P(("groups", "role", "tp"), None, None),
            P(("groups", "role", "tp"), None, None),
            P(("groups", "role", "tp")),
            P("groups"),
            P("role"),
            P("role", "tp"),
            P("role", "tp"),
            P("tp", "role"),
        ),
        out_specs=P(("groups", "tp"), "role"),
        check_vma=False,
    )
```

```python
import functools
import math

import jax
import jax.numpy as jnp
from jax import lax
from jax.experimental import pallas as pl
from jax.experimental.pallas import tpu as pltpu
from jax.sharding import PartitionSpec as P

D = 8192
HEADS = 32
KV_HEADS = 4
HEAD_DIM = 128
WINDOW = 256
GROUP = 8


epsilon = 1e-05
rope_base = 500000.0


def rotate(vectors, positions):
    halfway = vectors.shape[-1] // 2
    frequency = jnp.power(
        jnp.float32(rope_base), -jnp.arange(halfway, dtype=jnp.float32) * 2.0 / vectors.shape[-1]
    )
    angles = positions.astype(jnp.float32)[:, None, None] * frequency[None, None, :]
    cosine = jnp.cos(angles)
    sine_part = jnp.sin(angles)
    leading = vectors[..., :halfway]
    trailing = vectors[..., halfway:]
    return jnp.concatenate(
        [leading * cosine - trailing * sine_part, trailing * cosine + leading * sine_part], axis=-1
    )


def attend(queries, new_key, new_value, keys, values, lengths):
    batch_rows = queries.shape[0]
    factor = HEAD_DIM ** (-0.5)
    grouped = queries.reshape(batch_rows, KV_HEADS, GROUP, HEAD_DIM)
    key_blocks = keys.reshape(batch_rows, WINDOW, KV_HEADS, HEAD_DIM)
    value_blocks = values.reshape(batch_rows, WINDOW, KV_HEADS, HEAD_DIM)
    scores = (
        jnp.einsum("nkgd,nwkd->nkgw", grouped, key_blocks, preferred_element_type=jnp.float32)
        * factor
    )
    self_score = (
        jnp.einsum("nkgd,nkd->nkg", grouped, new_key, preferred_element_type=jnp.float32) * factor
    )
    usable = jnp.arange(WINDOW, dtype=jnp.int32)[None, :] < lengths[:, None]
    scores = jnp.where(usable[:, None, None, :], scores, -jnp.inf)
    highest = jnp.maximum(jnp.max(scores, axis=-1), self_score)
    weights = jnp.exp(scores - highest[..., None])
    self_weight = jnp.exp(self_score - highest)
    denominator = jnp.sum(weights, axis=-1) + self_weight
    chances = (weights / denominator[..., None]).astype(jnp.bfloat16)
    self_chance = (self_weight / denominator).astype(jnp.bfloat16)
    attended = jnp.einsum(
        "nkgw,nwkd->nkgd", chances, value_blocks, preferred_element_type=jnp.float32
    )
    attended = (
        attended
        + self_chance.astype(jnp.float32)[..., None] * new_value.astype(jnp.float32)[:, :, None, :]
    )
    return attended.reshape(batch_rows, HEADS * HEAD_DIM).astype(jnp.bfloat16)


def feed_forward(middle, ffn_gain, w_gate, w_up, w_down):
    widened = middle.astype(jnp.float32)
    squares = lax.psum(jnp.sum(widened * widened, axis=1), "role")
    inverse = lax.rsqrt(squares / D + epsilon)
    mid_normed = (widened * inverse[:, None] * ffn_gain[None, :]).astype(jnp.bfloat16)
    gate_part = jnp.dot(mid_normed, w_gate, preferred_element_type=jnp.float32)
    up_part = jnp.dot(mid_normed, w_up, preferred_element_type=jnp.float32)
    gate_total, up_total = (
        lax.psum(gate_part.astype(jnp.bfloat16), "role").astype(jnp.float32),
        lax.psum(up_part.astype(jnp.bfloat16), "role").astype(jnp.float32),
    )
    hidden = (jax.nn.silu(gate_total) * up_total).astype(jnp.bfloat16)
    down_terms = jnp.dot(hidden, w_down, preferred_element_type=jnp.float32)
    return lax.psum_scatter(
        down_terms.astype(jnp.bfloat16), "tp", scatter_dimension=0, tiled=True
    ).astype(jnp.float32)


def local(
    residual,
    attn_gain,
    w_query,
    w_key,
    w_value,
    w_output,
    cache_keys,
    cache_values,
    lengths,
    served,
    ffn_gain,
    w_gate,
    w_up,
    w_down,
):
    own_rows = residual.shape[0]
    tp_count = lax.axis_size("tp")
    row_start = lax.axis_index("tp") * own_rows
    live_own = lax.dynamic_slice_in_dim(served, row_start, own_rows, 0).astype(jnp.float32)[:, None]
    rows_all = lax.all_gather(residual, "tp", axis=0, tiled=True)
    widened = rows_all.astype(jnp.float32)
    squares = lax.psum(jnp.sum(widened * widened, axis=1), "role")
    inverse = lax.rsqrt(squares / D + epsilon)
    normed = (widened * inverse[:, None] * attn_gain[None, :]).astype(jnp.bfloat16)
    partial_value = jnp.concatenate(
        [
            jnp.dot(normed, w_query, preferred_element_type=jnp.float32),
            jnp.dot(normed, w_key, preferred_element_type=jnp.float32),
            jnp.dot(normed, w_value, preferred_element_type=jnp.float32),
        ],
        axis=1,
    )
    summed = lax.psum_scatter(
        partial_value.astype(jnp.bfloat16), "role", scatter_dimension=0, tiled=True
    ).astype(jnp.float32)
    gathered = lax.all_to_all(
        summed.astype(jnp.bfloat16), "tp", split_axis=0, concat_axis=1, tiled=True
    ).astype(summed.dtype)
    local_rows = gathered.shape[0]
    query_cols = w_query.shape[1]
    kv_cols = w_key.shape[1]
    blocks = gathered.reshape(local_rows, tp_count, query_cols + 2 * kv_cols)
    queries = blocks[:, :, :query_cols].reshape(local_rows, HEADS, HEAD_DIM)
    new_key = blocks[:, :, query_cols : query_cols + kv_cols].reshape(
        local_rows, KV_HEADS, HEAD_DIM
    )
    new_value = (
        blocks[:, :, query_cols + kv_cols :]
        .reshape(local_rows, KV_HEADS, HEAD_DIM)
        .astype(jnp.bfloat16)
    )
    queries = rotate(queries, lengths).astype(jnp.bfloat16)
    new_key = rotate(new_key, lengths).astype(jnp.bfloat16)
    attended = attend(queries, new_key, new_value, cache_keys, cache_values, lengths)
    head_block = lax.all_to_all(attended, "tp", split_axis=1, concat_axis=0, tiled=True)
    attn_terms = jnp.dot(
        lax.all_gather(head_block, "role", axis=0, tiled=True),
        w_output,
        preferred_element_type=jnp.float32,
    )
    attn = lax.psum_scatter(
        attn_terms.astype(jnp.bfloat16), "tp", scatter_dimension=0, tiled=True
    ).astype(jnp.float32)
    middle_own = (residual.astype(jnp.float32) + live_own * attn).astype(jnp.bfloat16)
    middle = lax.all_gather(middle_own, "tp", axis=0, tiled=True)
    ffn = feed_forward(middle, ffn_gain, w_gate, w_up, w_down)
    return (middle_own.astype(jnp.float32) + live_own * ffn).astype(jnp.bfloat16)


LANES = 128
MIB = 2**20
COVER = (100, 100, 1, 1, 1, 1, 1, 1, 1, 1)
CHUNK = 512
FIRST_PART = 57


def exchange_fits(residual, w_query, w_key, w_gate):
    tp_count, role_count = lax.axis_size("tp"), lax.axis_size("role")
    return (
        tp_count == KV_HEADS
        and role_count == 4
        and residual.shape[0] % 8 == 0
        and w_query.shape[1] == GROUP * LANES
        and w_key.shape[1] == LANES
        and w_gate.shape[1] % (4 * LANES) == 0
        and w_gate.shape[1] >= 8 * LANES
    )


def swap(value, axis, distance):
    count = lax.axis_size(axis)
    return lax.ppermute(value, axis, [(i, i ^ distance) for i in range(count)])


def in_vmem(value):
    return pltpu.with_memory_space_constraint(value, pltpu.VMEM)


def call(kernel, outs, args, scratch=(), limit=4 * MIB, smem=0, cost=0):
    specs = [pl.BlockSpec(memory_space=pltpu.SMEM)] * smem
    specs += [pl.BlockSpec(memory_space=pltpu.VMEM)] * (len(args) - smem)
    return pl.pallas_call(
        kernel,
        out_shape=outs,
        in_specs=specs,
        out_specs=[pl.BlockSpec(memory_space=pltpu.VMEM)] * len(outs),
        scratch_shapes=list(scratch),
        compiler_params=pltpu.CompilerParams(vmem_limit_bytes=limit),
        cost_estimate=pl.CostEstimate(flops=cost * 10**9, bytes_accessed=MIB, transcendentals=0),
    )(*args)


def split_three(column):
    first = column.astype(jnp.bfloat16)
    left = column - first.astype(jnp.float32)
    second = left.astype(jnp.bfloat16)
    third = (left - second.astype(jnp.float32)).astype(jnp.bfloat16)
    lane = lax.broadcasted_iota(jnp.int32, (column.shape[0], LANES), 1)
    wide = jnp.where(lane == 0, first.astype(jnp.float32), 0.0)
    wide = jnp.where(lane == 1, second.astype(jnp.float32), wide)
    return jnp.where(lane == 2, third.astype(jnp.float32), wide).astype(jnp.bfloat16)


def angle_kernel(lengths_ref, cosine_ref, sine_ref):
    count, width = cosine_ref.shape
    lane = lax.broadcasted_iota(jnp.int32, (1, width), 1)
    step = lax.rem(lane, width // 2).astype(jnp.float32)
    frequency = jnp.exp(step * (-2.0 / width * math.log(rope_base)))
    angles = jnp.concatenate(
        [lengths_ref[i].astype(jnp.float32) * frequency for i in range(count)], axis=0
    )
    cosine_ref[...] = jnp.cos(angles)
    sine = jnp.sin(angles)
    sine_ref[...] = jnp.where(lane < width // 2, -sine, sine)


def project_kernel(_, *refs):
    *block_refs, gain_ref, wq_ref, wk_ref, wv_ref, out_ref, stream_ref = refs[:-3]
    rows_ref, sums_ref, packed_ref = refs[-3:]
    place = lax.axis_index("tp")
    own = block_refs[0].shape[0]
    for k, block_ref in enumerate(block_refs):
        start = pl.multiple_of((place ^ k) * own, own)
        rows_ref[pl.ds(start, own), :] = block_ref[...].astype(jnp.float32)
    rows = rows_ref[...]
    stream_ref[...] = rows.astype(jnp.bfloat16)
    squares = jnp.sum(rows * rows, axis=1, keepdims=True)
    scaled = (rows * gain_ref[...]).astype(jnp.bfloat16)
    count = rows.shape[0]
    groups = 0
    for w_ref in (wq_ref, wk_ref, wv_ref):
        product = jnp.dot(scaled, w_ref[...], preferred_element_type=jnp.float32)
        for at in range(0, w_ref.shape[1], LANES):
            sums_ref[groups * count : (groups + 1) * count, :] = product[:, at : at + LANES]
            groups += 1
    sums_ref[groups * count :, :] = split_three(squares).astype(jnp.float32)
    groups += 1
    devices, depth, _ = out_ref.shape
    each = count // devices
    queries = wq_ref.shape[1] // LANES
    packed_ref[...] = jnp.zeros_like(packed_ref)
    for n in range(each):
        for g in range(groups):
            row = packed_row(n, g, each, queries, groups)
            packed_ref[pl.ds(row, devices, stride=depth), :] = sums_ref[
                pl.ds(g * count + n, devices, stride=each), :
            ]
    out_ref[...] = packed_ref[...].reshape(out_ref.shape).astype(jnp.bfloat16)


def packed_row(n, g, each, queries, groups):
    if g < queries:
        return n * queries + g
    return each * queries + n * (groups - queries) + g - queries


def attend_kernel(
    lengths_ref, got_ref, cosine_ref, sine_ref, keys_ref, values_ref, out_ref
):
    tp_count = KV_HEADS
    devices, depth, width = got_ref.shape
    each, window, _ = keys_ref.shape
    groups = GROUP + 3
    total = jnp.sum(
        got_ref[...].astype(jnp.float32).reshape(devices // tp_count, tp_count, depth, width),
        axis=0,
    )
    factor = HEAD_DIM ** (-0.5)
    scores, own_scores, own_values = [], [], []
    for n in range(each):
        cosine, sine = cosine_ref[n : n + 1, :], sine_ref[n : n + 1, :]
        tail = packed_row(n, GROUP, each, GROUP, groups)
        squares = jnp.sum(total[0, tail + 2 : tail + 3, :], axis=1, keepdims=True)
        inverse = lax.rsqrt(squares / D + epsilon)
        usable = lax.broadcasted_iota(jnp.int32, (GROUP, window), 1) < lengths_ref[n]
        for h in range(tp_count):
            query = total[h, n * GROUP : (n + 1) * GROUP, :] * inverse
            key = total[h, tail : tail + 1, :] * inverse
            query = query * cosine + pltpu.roll(query, width // 2, 1) * sine
            key = key * cosine + pltpu.roll(key, width // 2, 1) * sine
            query = query.astype(jnp.bfloat16)
            key = key.astype(jnp.bfloat16).astype(jnp.float32)
            score = lax.dot_general(
                query,
                keys_ref[n, :, h * width : (h + 1) * width],
                (((1,), (1,)), ((), ())),
                preferred_element_type=jnp.float32,
            )
            scores.append(jnp.where(usable, score * factor, -jnp.inf))
            own_scores.append(
                jnp.sum(query.astype(jnp.float32) * key, axis=1, keepdims=True) * factor
            )
            value = (total[h, tail + 1 : tail + 2, :] * inverse).astype(jnp.bfloat16)
            own_values.append(value.astype(jnp.float32))
    scores, own_scores = jnp.concatenate(scores, axis=0), jnp.concatenate(own_scores, axis=0)
    highest = jnp.maximum(jnp.max(scores, axis=1, keepdims=True), own_scores)
    weights, own_weights = jnp.exp(scores - highest), jnp.exp(own_scores - highest)
    denominator = jnp.sum(weights, axis=1, keepdims=True) + own_weights
    chances = (weights / denominator).astype(jnp.bfloat16)
    own_chances = (own_weights / denominator).astype(jnp.bfloat16).astype(jnp.float32)
    for n in range(each):
        for h in range(tp_count):
            at = (n * tp_count + h) * GROUP
            attended = jnp.dot(
                chances[at : at + GROUP],
                values_ref[n, :, h * width : (h + 1) * width],
                preferred_element_type=jnp.float32,
            )
            attended = attended + own_chances[at : at + GROUP] * own_values[n * tp_count + h]
            for r in range(devices // tp_count):
                out_ref[r * tp_count + h, n * GROUP : (n + 1) * GROUP, :] = attended.astype(
                    jnp.bfloat16
                )


def output_kernel(heads_ref, w_ref, *refs):
    *out_refs, heads_wide_ref = refs
    count = sum(ref.shape[0] for ref in out_refs)
    groups = w_ref.shape[0] // LANES
    heads_wide_ref[...] = heads_ref[...].astype(jnp.float32).reshape(heads_wide_ref.shape)
    attended = jnp.concatenate(
        [heads_wide_ref[pl.ds(g, count, stride=groups), :] for g in range(groups)], axis=1
    ).astype(jnp.bfloat16)
    for at in range(0, w_ref.shape[1], CHUNK):
        part = slice(at, min(at + CHUNK, w_ref.shape[1]))
        rows = jnp.dot(attended, w_ref[:, part], preferred_element_type=jnp.float32)
        start = 0
        for out_ref in out_refs:
            out_ref[:, part] = rows[start : start + out_ref.shape[0]].astype(jnp.bfloat16)
            start += out_ref.shape[0]


def add_kernel(served_ref, stream_ref, *refs):
    *term_refs, out_ref = refs
    own = stream_ref.shape[0]
    start = lax.axis_index("tp") * own
    row = lax.broadcasted_iota(jnp.int32, (own, LANES), 0)
    live = jnp.zeros((own, LANES), jnp.int32)
    for i in range(own):
        live = jnp.where(row == i, served_ref[start + i], live)
    live = live.astype(jnp.float32)[:, :1]
    total = term_refs[0][...].astype(jnp.float32)
    for term_ref in term_refs[1:]:
        total = total + term_ref[...].astype(jnp.float32)
    out_ref[...] = (stream_ref[...].astype(jnp.float32) + live * total).astype(
        jnp.bfloat16
    )


def middle_kernel(*refs):
    served_ref, stream_ref, *term_refs, gain_ref, wg_ref, wu_ref, _ = refs[:-5]
    scaled_ref, tail_ref, send_ref, middle_ref, rows_ref = refs[-5:]
    count = stream_ref.shape[0]
    row = lax.broadcasted_iota(jnp.int32, (count, count), 0)
    column = lax.broadcasted_iota(jnp.int32, (count, count), 1)
    live = jnp.sum(
        jnp.where(row == column, served_ref[...], 0).astype(jnp.float32), axis=1, keepdims=True
    )
    pieces = len(term_refs) // 2
    attn = jnp.concatenate(
        [
            term_refs[2 * i][...].astype(jnp.float32) + term_refs[2 * i + 1][...].astype(jnp.float32)
            for i in range(pieces)
        ],
        axis=0,
    )
    rows = (stream_ref[...].astype(jnp.float32) + live * attn).astype(jnp.bfloat16)
    rows = rows.astype(jnp.float32)
    rows_ref[...] = rows
    own = middle_ref.shape[0]
    start = pl.multiple_of(lax.axis_index("tp") * own, own)
    middle_ref[...] = rows_ref[pl.ds(start, own), :].astype(jnp.bfloat16)
    squares = jnp.sum(rows * rows, axis=1, keepdims=True)
    scaled_ref[...] = (rows * gain_ref[...]).astype(jnp.bfloat16)
    half = lax.rem(lax.axis_index("role"), 2)
    size = (send_ref.shape[1] - LANES) // 2
    piece_dots(scaled_ref, wg_ref, wu_ref, send_ref, 1 - half, 0, size)
    tail = split_three(squares)
    send_ref[:, 2 * size :] = tail
    tail_ref[...] = tail.astype(jnp.float32)


def piece_kernel(theirs, begin, size, scaled_ref, wg_ref, wu_ref, *refs):
    half = lax.rem(lax.axis_index("role"), 2)
    side = 1 - half if theirs else half
    piece_dots(scaled_ref, wg_ref, wu_ref, refs[-1], side, begin, size)


def piece_dots(scaled_ref, wg_ref, wu_ref, out_ref, side, begin, size):
    scaled = scaled_ref[...]
    first = side * (wg_ref.shape[1] // 2) + begin
    for w_ref, base in ((wg_ref, 0), (wu_ref, size)):
        for at in range(0, size, CHUNK):
            step = min(CHUNK, size - at)
            start = pl.multiple_of(first + at, LANES)
            out_ref[:, base + at : base + at + step] = jnp.dot(
                scaled, w_ref[:, pl.ds(start, step)], preferred_element_type=jnp.float32
            ).astype(out_ref.dtype)


def pair_tail_kernel(keep_ref, tail_ref, got_ref, out_ref):
    wide = keep_ref.shape[1]
    out_ref[:, :wide] = (keep_ref[...] + got_ref[:, :wide].astype(jnp.float32)).astype(
        jnp.bfloat16
    )
    squares = jnp.sum(
        tail_ref[...] + got_ref[:, wide:].astype(jnp.float32), axis=1, keepdims=True
    )
    out_ref[:, wide:] = split_three(squares)


def pair_kernel(keep_ref, got_ref, out_ref):
    out_ref[...] = (
        keep_ref[...].astype(jnp.float32) + got_ref[...].astype(jnp.float32)
    ).astype(jnp.bfloat16)


def first_hidden_kernel(own_ref, got_ref, hidden_ref, inverse_ref):
    wide = 2 * hidden_ref.shape[1]
    squares = jnp.sum(
        own_ref[:, wide:].astype(jnp.float32) + got_ref[:, wide:].astype(jnp.float32),
        axis=1,
        keepdims=True,
    )
    inverse = lax.rsqrt(squares / D + epsilon)
    inverse_ref[...] = jnp.broadcast_to(inverse, inverse_ref.shape)
    gated(own_ref, got_ref, inverse, hidden_ref)


def hidden_kernel(own_ref, got_ref, inverse_ref, _, hidden_ref):
    gated(own_ref, got_ref, inverse_ref[:, :1], hidden_ref)


def gated(own_ref, got_ref, inverse, hidden_ref):
    size = hidden_ref.shape[1]
    total = own_ref[:, : 2 * size].astype(jnp.float32) + got_ref[:, : 2 * size].astype(jnp.float32)
    total = total * inverse
    gate, up = total[:, :size], total[:, size:]
    hidden_ref[...] = (gate / (1.0 + jnp.exp(-gate)) * up).astype(jnp.bfloat16)


def down_dots(theirs, begin, hidden_ref, w_ref, part):
    half = lax.rem(lax.axis_index("role"), 2)
    side = 1 - half if theirs else half
    start = pl.multiple_of(side * (w_ref.shape[0] // 2) + begin, LANES)
    return jnp.dot(
        hidden_ref[...],
        w_ref[pl.ds(start, hidden_ref.shape[1]), part],
        preferred_element_type=jnp.float32,
    )


def chunks(width):
    return [slice(at, min(at + CHUNK, width)) for at in range(0, width, CHUNK)]


def down_kernel(theirs, begin, hidden_ref, w_ref, *refs):
    *before_refs, rows_ref = refs
    for part in chunks(w_ref.shape[1]):
        rows = down_dots(theirs, begin, hidden_ref, w_ref, part)
        for before_ref in before_refs:
            rows = rows + before_ref[:, part]
        rows_ref[:, part] = rows


def last_down_kernel(theirs, begin, hidden_ref, w_ref, before_ref, *refs):
    *out_refs, rows_ref = refs
    place = lax.axis_index("tp")
    own = out_refs[0].shape[0]
    for part in chunks(w_ref.shape[1]):
        rows_ref[:, part] = before_ref[:, part] + down_dots(
            theirs, begin, hidden_ref, w_ref, part
        )
    for k, out_ref in enumerate(out_refs):
        start = pl.multiple_of((place ^ k) * own, own)
        out_ref[...] = rows_ref[pl.ds(start, own), :].astype(jnp.bfloat16)


def local_exchange(
    residual,
    attn_gain,
    w_query,
    w_key,
    w_value,
    w_output,
    cache_keys,
    cache_values,
    lengths,
    served,
    ffn_gain,
    w_gate,
    w_up,
    w_down,
):
    if not exchange_fits(residual, w_query, w_key, w_gate):
        return local(
            residual,
            attn_gain,
            w_query,
            w_key,
            w_value,
            w_output,
            cache_keys,
            cache_values,
            lengths,
            served,
            ffn_gain,
            w_gate,
            w_up,
            w_down,
        )
    tp_count, role_count = lax.axis_size("tp"), lax.axis_size("role")
    devices = tp_count * role_count
    own, features = residual.shape
    rows = own * tp_count
    each = rows // devices
    block = jax.ShapeDtypeStruct((own, features), jnp.bfloat16)

    table = jax.ShapeDtypeStruct((each, HEAD_DIM), jnp.float32)
    cosine, sine = call(angle_kernel, [table] * 2, [lengths], smem=1, cost=COVER[0])
    others = {k: swap(residual, "tp", k) for k in reversed(range(1, tp_count))}
    blocks = [residual] + [others[k] for k in range(1, tp_count)]
    payload = w_query.shape[1] + 2 * w_key.shape[1] + LANES
    depth = -(-each * payload // (LANES * 8)) * 8
    sums, stream = call(
        project_kernel,
        [
            jax.ShapeDtypeStruct((devices, depth, LANES), jnp.bfloat16),
            jax.ShapeDtypeStruct((rows, features), jnp.bfloat16),
        ],
        [cosine, *blocks, attn_gain[None, :], in_vmem(w_query), in_vmem(w_key), in_vmem(w_value)],
        scratch=[
            pltpu.VMEM((rows, features), jnp.float32),
            pltpu.VMEM((rows * payload // LANES, LANES), jnp.float32),
            pltpu.VMEM((devices * depth, LANES), jnp.float32),
        ],
        cost=COVER[1],
    )
    parts = lax.all_to_all(sums, ("role", "tp"), 0, 0)
    (heads,) = call(
        attend_kernel,
        [jax.ShapeDtypeStruct((devices, each * GROUP, LANES), jnp.bfloat16)],
        [lengths, parts, cosine, sine, in_vmem(cache_keys), in_vmem(cache_values)],
        smem=1,
        cost=COVER[2],
    )
    heads = lax.all_to_all(heads, ("role", "tp"), 0, 0)
    pieces = 2
    piece = jax.ShapeDtypeStruct((rows // pieces, features), jnp.bfloat16)
    attn = call(
        output_kernel,
        [piece] * pieces,
        [heads, in_vmem(w_output)],
        scratch=[pltpu.VMEM((rows * GROUP, LANES), jnp.float32)],
        cost=COVER[3],
    )
    terms = []
    near = [swap(value, "tp", 1) for value in attn]
    for value, got in zip(attn, near):
        (paired,) = call(pair_kernel, [piece], [value, got])
        terms += [paired, swap(paired, "tp", 2)]
    width = w_gate.shape[1] // 2
    first = -(-width * FIRST_PART // (100 * 2 * LANES)) * 2 * LANES
    sizes = (first, width - first)
    w_gate, w_up, w_down = in_vmem(w_gate), in_vmem(w_up), in_vmem(w_down)
    rows_f32 = jax.ShapeDtypeStruct((rows, features), jnp.float32)
    row_scratch = pltpu.VMEM((rows, features), jnp.float32)

    def wide(size, dtype, more=0):
        return jax.ShapeDtypeStruct((rows, 2 * size + more), dtype)

    def half_of(piece):
        return jax.ShapeDtypeStruct((rows, sizes[piece]), jnp.bfloat16)

    scaled, tail, send, middle = call(
        middle_kernel,
        [
            jax.ShapeDtypeStruct((rows, features), jnp.bfloat16),
            jax.ShapeDtypeStruct((rows, LANES), jnp.float32),
            wide(sizes[0], jnp.bfloat16, LANES),
            block,
        ],
        [served[None, :], stream, *terms, ffn_gain[None, :], w_gate, w_up, w_down],
        scratch=[row_scratch],
        cost=COVER[4],
    )
    got = swap(send, "role", 1)
    (keep,) = call(
        functools.partial(piece_kernel, False, 0, sizes[0]),
        [wide(sizes[0], jnp.float32)],
        [scaled, w_gate, w_up],
        cost=COVER[5],
    )
    (chip_0,) = call(
        pair_tail_kernel, [wide(sizes[0], jnp.bfloat16, LANES)], [keep, tail, got]
    )
    far_0 = swap(chip_0, "role", 2)
    (send,) = call(
        functools.partial(piece_kernel, True, sizes[0], sizes[1]),
        [wide(sizes[1], jnp.bfloat16)],
        [scaled, w_gate, w_up, chip_0],
        cost=COVER[6],
    )
    got = swap(send, "role", 1)
    (keep,) = call(
        functools.partial(piece_kernel, False, sizes[0], sizes[1]),
        [wide(sizes[1], jnp.float32)],
        [scaled, w_gate, w_up],
        cost=COVER[7],
    )
    (chip_1,) = call(pair_kernel, [wide(sizes[1], jnp.bfloat16)], [keep, got])
    far_1 = swap(chip_1, "role", 2)
    hidden, inverse = call(
        first_hidden_kernel,
        [half_of(0), jax.ShapeDtypeStruct((rows, LANES), jnp.float32)],
        [chip_0, far_0],
    )
    other = swap(hidden, "role", 1)
    (down,) = call(
        functools.partial(down_kernel, False, 0), [rows_f32], [hidden, w_down], cost=COVER[8]
    )
    (down,) = call(
        functools.partial(down_kernel, True, 0), [rows_f32], [other, w_down, down], cost=COVER[8]
    )
    (hidden,) = call(hidden_kernel, [half_of(1)], [chip_1, far_1, inverse, down])
    other = swap(hidden, "role", 1)
    (down,) = call(
        functools.partial(down_kernel, False, sizes[0]),
        [rows_f32],
        [hidden, w_down, down],
        cost=COVER[9],
    )
    terms = call(
        functools.partial(last_down_kernel, True, sizes[0]),
        [block] * tp_count,
        [other, w_down, down],
        scratch=[row_scratch],
        cost=COVER[9],
    )
    terms = [terms[0]] + [swap(terms[k], "tp", k) for k in range(1, tp_count)]
    return call(add_kernel, [block], [served, middle, *terms], smem=1)[0]


def solution(mesh):
    return jax.shard_map(
        local_exchange,
        mesh=mesh,
        in_specs=(
            P(("groups", "tp"), "role"),
            P("role"),
            P("role", "tp"),
            P("role", "tp"),
            P("role", "tp"),
            P("tp", "role"),
            P(("groups", "role", "tp"), None, None),
            P(("groups", "role", "tp"), None, None),
            P(("groups", "role", "tp")),
            P("groups"),
            P("role"),
            P("role", "tp"),
            P("role", "tp"),
            P("tp", "role"),
        ),
        out_specs=P(("groups", "tp"), "role"),
        check_vma=False,
    )
```

```python
import functools
import math

import jax
import jax.numpy as jnp
from jax import lax
from jax.experimental import pallas as pl
from jax.experimental.pallas import tpu as pltpu
from jax.sharding import PartitionSpec as P

D = 8192
HEADS = 32
KV_HEADS = 4
HEAD_DIM = 128
WINDOW = 256
GROUP = 8


epsilon = 1e-05
rope_base = 500000.0


def rotate(vectors, positions):
    halfway = vectors.shape[-1] // 2
    frequency = jnp.power(
        jnp.float32(rope_base), -jnp.arange(halfway, dtype=jnp.float32) * 2.0 / vectors.shape[-1]
    )
    angles = positions.astype(jnp.float32)[:, None, None] * frequency[None, None, :]
    cosine = jnp.cos(angles)
    sine_part = jnp.sin(angles)
    leading = vectors[..., :halfway]
    trailing = vectors[..., halfway:]
    return jnp.concatenate(
        [leading * cosine - trailing * sine_part, trailing * cosine + leading * sine_part], axis=-1
    )


def attend(queries, new_key, new_value, keys, values, lengths):
    batch_rows = queries.shape[0]
    factor = HEAD_DIM ** (-0.5)
    grouped = queries.reshape(batch_rows, KV_HEADS, GROUP, HEAD_DIM)
    key_blocks = keys.reshape(batch_rows, WINDOW, KV_HEADS, HEAD_DIM)
    value_blocks = values.reshape(batch_rows, WINDOW, KV_HEADS, HEAD_DIM)
    scores = (
        jnp.einsum("nkgd,nwkd->nkgw", grouped, key_blocks, preferred_element_type=jnp.float32)
        * factor
    )
    self_score = (
        jnp.einsum("nkgd,nkd->nkg", grouped, new_key, preferred_element_type=jnp.float32) * factor
    )
    usable = jnp.arange(WINDOW, dtype=jnp.int32)[None, :] < lengths[:, None]
    scores = jnp.where(usable[:, None, None, :], scores, -jnp.inf)
    highest = jnp.maximum(jnp.max(scores, axis=-1), self_score)
    weights = jnp.exp(scores - highest[..., None])
    self_weight = jnp.exp(self_score - highest)
    denominator = jnp.sum(weights, axis=-1) + self_weight
    chances = (weights / denominator[..., None]).astype(jnp.bfloat16)
    self_chance = (self_weight / denominator).astype(jnp.bfloat16)
    attended = jnp.einsum(
        "nkgw,nwkd->nkgd", chances, value_blocks, preferred_element_type=jnp.float32
    )
    attended = (
        attended
        + self_chance.astype(jnp.float32)[..., None] * new_value.astype(jnp.float32)[:, :, None, :]
    )
    return attended.reshape(batch_rows, HEADS * HEAD_DIM).astype(jnp.bfloat16)


def feed_forward(middle, ffn_gain, w_gate, w_up, w_down):
    widened = middle.astype(jnp.float32)
    squares = lax.psum(jnp.sum(widened * widened, axis=1), "role")
    inverse = lax.rsqrt(squares / D + epsilon)
    mid_normed = (widened * inverse[:, None] * ffn_gain[None, :]).astype(jnp.bfloat16)
    gate_part = jnp.dot(mid_normed, w_gate, preferred_element_type=jnp.float32)
    up_part = jnp.dot(mid_normed, w_up, preferred_element_type=jnp.float32)
    gate_total, up_total = (
        lax.psum(gate_part.astype(jnp.bfloat16), "role").astype(jnp.float32),
        lax.psum(up_part.astype(jnp.bfloat16), "role").astype(jnp.float32),
    )
    hidden = (jax.nn.silu(gate_total) * up_total).astype(jnp.bfloat16)
    down_terms = jnp.dot(hidden, w_down, preferred_element_type=jnp.float32)
    return lax.psum_scatter(
        down_terms.astype(jnp.bfloat16), "tp", scatter_dimension=0, tiled=True
    ).astype(jnp.float32)


def local(
    residual,
    attn_gain,
    w_query,
    w_key,
    w_value,
    w_output,
    cache_keys,
    cache_values,
    lengths,
    served,
    ffn_gain,
    w_gate,
    w_up,
    w_down,
):
    own_rows = residual.shape[0]
    tp_count = lax.axis_size("tp")
    row_start = lax.axis_index("tp") * own_rows
    live_own = lax.dynamic_slice_in_dim(served, row_start, own_rows, 0).astype(jnp.float32)[:, None]
    rows_all = lax.all_gather(residual, "tp", axis=0, tiled=True)
    widened = rows_all.astype(jnp.float32)
    squares = lax.psum(jnp.sum(widened * widened, axis=1), "role")
    inverse = lax.rsqrt(squares / D + epsilon)
    normed = (widened * inverse[:, None] * attn_gain[None, :]).astype(jnp.bfloat16)
    partial_value = jnp.concatenate(
        [
            jnp.dot(normed, w_query, preferred_element_type=jnp.float32),
            jnp.dot(normed, w_key, preferred_element_type=jnp.float32),
            jnp.dot(normed, w_value, preferred_element_type=jnp.float32),
        ],
        axis=1,
    )
    summed = lax.psum_scatter(
        partial_value.astype(jnp.bfloat16), "role", scatter_dimension=0, tiled=True
    ).astype(jnp.float32)
    gathered = lax.all_to_all(
        summed.astype(jnp.bfloat16), "tp", split_axis=0, concat_axis=1, tiled=True
    ).astype(summed.dtype)
    local_rows = gathered.shape[0]
    query_cols = w_query.shape[1]
    kv_cols = w_key.shape[1]
    blocks = gathered.reshape(local_rows, tp_count, query_cols + 2 * kv_cols)
    queries = blocks[:, :, :query_cols].reshape(local_rows, HEADS, HEAD_DIM)
    new_key = blocks[:, :, query_cols : query_cols + kv_cols].reshape(
        local_rows, KV_HEADS, HEAD_DIM
    )
    new_value = (
        blocks[:, :, query_cols + kv_cols :]
        .reshape(local_rows, KV_HEADS, HEAD_DIM)
        .astype(jnp.bfloat16)
    )
    queries = rotate(queries, lengths).astype(jnp.bfloat16)
    new_key = rotate(new_key, lengths).astype(jnp.bfloat16)
    attended = attend(queries, new_key, new_value, cache_keys, cache_values, lengths)
    head_block = lax.all_to_all(attended, "tp", split_axis=1, concat_axis=0, tiled=True)
    attn_terms = jnp.dot(
        lax.all_gather(head_block, "role", axis=0, tiled=True),
        w_output,
        preferred_element_type=jnp.float32,
    )
    attn = lax.psum_scatter(
        attn_terms.astype(jnp.bfloat16), "tp", scatter_dimension=0, tiled=True
    ).astype(jnp.float32)
    middle_own = (residual.astype(jnp.float32) + live_own * attn).astype(jnp.bfloat16)
    middle = lax.all_gather(middle_own, "tp", axis=0, tiled=True)
    ffn = feed_forward(middle, ffn_gain, w_gate, w_up, w_down)
    return (middle_own.astype(jnp.float32) + live_own * ffn).astype(jnp.bfloat16)


LANES = 128
MIB = 2**20
COVER = (100, 100, 100, 1, 10, 10, 10, 1, 1, 1)
CHUNK = 512
PARTS = (16, 16)
STEPS = (1, 2)
FIRST_PART = 57


def exchange_fits(residual, w_query, w_key, w_gate):
    tp_count, role_count = lax.axis_size("tp"), lax.axis_size("role")
    return (
        tp_count == KV_HEADS
        and role_count == 4
        and residual.shape[0] % 8 == 0
        and w_query.shape[1] == GROUP * LANES
        and w_key.shape[1] == LANES
        and w_gate.shape[1] % (4 * LANES) == 0
        and w_gate.shape[1] >= 8 * LANES
    )


def swap(value, axis, distance):
    count = lax.axis_size(axis)
    return lax.ppermute(value, axis, [(i, i ^ distance) for i in range(count)])


def in_vmem(value):
    return pltpu.with_memory_space_constraint(value, pltpu.VMEM)


def call(kernel, outs, args, scratch=(), limit=4 * MIB, smem=0, cost=0):
    specs = [pl.BlockSpec(memory_space=pltpu.SMEM)] * smem
    specs += [pl.BlockSpec(memory_space=pltpu.VMEM)] * (len(args) - smem)
    return pl.pallas_call(
        kernel,
        out_shape=outs,
        in_specs=specs,
        out_specs=[pl.BlockSpec(memory_space=pltpu.VMEM)] * len(outs),
        scratch_shapes=list(scratch),
        compiler_params=pltpu.CompilerParams(vmem_limit_bytes=limit),
        cost_estimate=pl.CostEstimate(flops=cost * 10**9, bytes_accessed=MIB, transcendentals=0),
    )(*args)


def split_three(column):
    first = column.astype(jnp.bfloat16)
    left = column - first.astype(jnp.float32)
    second = left.astype(jnp.bfloat16)
    third = (left - second.astype(jnp.float32)).astype(jnp.bfloat16)
    lane = lax.broadcasted_iota(jnp.int32, (column.shape[0], LANES), 1)
    wide = jnp.where(lane == 0, first.astype(jnp.float32), 0.0)
    wide = jnp.where(lane == 1, second.astype(jnp.float32), wide)
    return jnp.where(lane == 2, third.astype(jnp.float32), wide).astype(jnp.bfloat16)


def angle_kernel(lengths_ref, cosine_ref, sine_ref):
    count, width = cosine_ref.shape
    lane = lax.broadcasted_iota(jnp.int32, (1, width), 1)
    step = lax.rem(lane, width // 2).astype(jnp.float32)
    frequency = jnp.exp(step * (-2.0 / width * math.log(rope_base)))
    angles = jnp.concatenate(
        [lengths_ref[i].astype(jnp.float32) * frequency for i in range(count)], axis=0
    )
    cosine_ref[...] = jnp.cos(angles)
    sine = jnp.sin(angles)
    sine_ref[...] = jnp.where(lane < width // 2, -sine, sine)


def project_kernel(_, *refs):
    *block_refs, gain_ref, wq_ref, wk_ref, wv_ref, out_ref, stream_ref = refs[:-3]
    rows_ref, sums_ref, packed_ref = refs[-3:]
    place = lax.axis_index("tp")
    own = block_refs[0].shape[0]
    for k, block_ref in enumerate(block_refs):
        start = pl.multiple_of((place ^ k) * own, own)
        rows_ref[pl.ds(start, own), :] = block_ref[...].astype(jnp.float32)
    rows = rows_ref[...]
    stream_ref[...] = rows.astype(jnp.bfloat16)
    squares = jnp.sum(rows * rows, axis=1, keepdims=True)
    scaled = (rows * gain_ref[...]).astype(jnp.bfloat16)
    count = rows.shape[0]
    groups = 0
    for w_ref in (wq_ref, wk_ref, wv_ref):
        product = jnp.dot(scaled, w_ref[...], preferred_element_type=jnp.float32)
        for at in range(0, w_ref.shape[1], LANES):
            sums_ref[groups * count : (groups + 1) * count, :] = product[:, at : at + LANES]
            groups += 1
    sums_ref[groups * count :, :] = split_three(squares).astype(jnp.float32)
    groups += 1
    devices, depth, _ = out_ref.shape
    each = count // devices
    queries = wq_ref.shape[1] // LANES
    packed_ref[...] = jnp.zeros_like(packed_ref)
    for n in range(each):
        for g in range(groups):
            row = packed_row(n, g, each, queries, groups)
            packed_ref[pl.ds(row, devices, stride=depth), :] = sums_ref[
                pl.ds(g * count + n, devices, stride=each), :
            ]
    out_ref[...] = packed_ref[...].reshape(out_ref.shape).astype(jnp.bfloat16)


def packed_row(n, g, each, queries, groups):
    if g < queries:
        return n * queries + g
    return each * queries + n * (groups - queries) + g - queries


def attend_kernel(
    lengths_ref, got_ref, cosine_ref, sine_ref, keys_ref, values_ref, out_ref
):
    tp_count = KV_HEADS
    devices, depth, width = got_ref.shape
    each, window, _ = keys_ref.shape
    groups = GROUP + 3
    total = jnp.sum(
        got_ref[...].astype(jnp.float32).reshape(devices // tp_count, tp_count, depth, width),
        axis=0,
    )
    factor = HEAD_DIM ** (-0.5)
    scores, own_scores, own_values = [], [], []
    for n in range(each):
        cosine, sine = cosine_ref[n : n + 1, :], sine_ref[n : n + 1, :]
        tail = packed_row(n, GROUP, each, GROUP, groups)
        squares = jnp.sum(total[0, tail + 2 : tail + 3, :], axis=1, keepdims=True)
        inverse = lax.rsqrt(squares / D + epsilon)
        usable = lax.broadcasted_iota(jnp.int32, (GROUP, window), 1) < lengths_ref[n]
        for h in range(tp_count):
            query = total[h, n * GROUP : (n + 1) * GROUP, :] * inverse
            key = total[h, tail : tail + 1, :] * inverse
            query = query * cosine + pltpu.roll(query, width // 2, 1) * sine
            key = key * cosine + pltpu.roll(key, width // 2, 1) * sine
            query = query.astype(jnp.bfloat16)
            key = key.astype(jnp.bfloat16).astype(jnp.float32)
            score = lax.dot_general(
                query,
                keys_ref[n, :, h * width : (h + 1) * width],
                (((1,), (1,)), ((), ())),
                preferred_element_type=jnp.float32,
            )
            scores.append(jnp.where(usable, score * factor, -jnp.inf))
            own_scores.append(
                jnp.sum(query.astype(jnp.float32) * key, axis=1, keepdims=True) * factor
            )
            value = (total[h, tail + 1 : tail + 2, :] * inverse).astype(jnp.bfloat16)
            own_values.append(value.astype(jnp.float32))
    scores, own_scores = jnp.concatenate(scores, axis=0), jnp.concatenate(own_scores, axis=0)
    highest = jnp.maximum(jnp.max(scores, axis=1, keepdims=True), own_scores)
    weights, own_weights = jnp.exp(scores - highest), jnp.exp(own_scores - highest)
    denominator = jnp.sum(weights, axis=1, keepdims=True) + own_weights
    chances = (weights / denominator).astype(jnp.bfloat16)
    own_chances = (own_weights / denominator).astype(jnp.bfloat16).astype(jnp.float32)
    for n in range(each):
        for h in range(tp_count):
            at = (n * tp_count + h) * GROUP
            attended = jnp.dot(
                chances[at : at + GROUP],
                values_ref[n, :, h * width : (h + 1) * width],
                preferred_element_type=jnp.float32,
            )
            attended = attended + own_chances[at : at + GROUP] * own_values[n * tp_count + h]
            for r in range(devices // tp_count):
                out_ref[r * tp_count + h, n * GROUP : (n + 1) * GROUP, :] = attended.astype(
                    jnp.bfloat16
                )


def output_kernel(heads_ref, w_ref, *refs):
    *out_refs, heads_wide_ref = refs
    count = sum(ref.shape[0] for ref in out_refs)
    groups = w_ref.shape[0] // LANES
    heads_wide_ref[...] = heads_ref[...].astype(jnp.float32).reshape(heads_wide_ref.shape)
    attended = jnp.concatenate(
        [heads_wide_ref[pl.ds(g, count, stride=groups), :] for g in range(groups)], axis=1
    ).astype(jnp.bfloat16)
    for at in range(0, w_ref.shape[1], CHUNK):
        part = slice(at, min(at + CHUNK, w_ref.shape[1]))
        rows = jnp.dot(attended, w_ref[:, part], preferred_element_type=jnp.float32)
        start = 0
        for out_ref in out_refs:
            out_ref[:, part] = rows[start : start + out_ref.shape[0]].astype(jnp.bfloat16)
            start += out_ref.shape[0]


def add_kernel(served_ref, stream_ref, *refs):
    *term_refs, out_ref = refs
    own = stream_ref.shape[0]
    start = lax.axis_index("tp") * own
    row = lax.broadcasted_iota(jnp.int32, (own, LANES), 0)
    live = jnp.zeros((own, LANES), jnp.int32)
    for i in range(own):
        live = jnp.where(row == i, served_ref[start + i], live)
    live = live.astype(jnp.float32)[:, :1]
    total = term_refs[0][...].astype(jnp.float32)
    for term_ref in term_refs[1:]:
        total = total + term_ref[...].astype(jnp.float32)
    out_ref[...] = (stream_ref[...].astype(jnp.float32) + live * total).astype(
        jnp.bfloat16
    )


def middle_kernel(*refs):
    served_ref, stream_ref, *term_refs, gain_ref, wg_ref, wu_ref = refs[:-7]
    scaled_ref, tail_ref, send_ref, middle_ref, live_ref, rows_ref, live_rows_ref = refs[-7:]
    count = stream_ref.shape[0]
    row = lax.broadcasted_iota(jnp.int32, (count, count), 0)
    column = lax.broadcasted_iota(jnp.int32, (count, count), 1)
    live = jnp.sum(
        jnp.where(row == column, served_ref[...], 0).astype(jnp.float32), axis=1, keepdims=True
    )
    pieces = len(term_refs) // 2
    attn = jnp.concatenate(
        [
            term_refs[2 * i][...].astype(jnp.float32) + term_refs[2 * i + 1][...].astype(jnp.float32)
            for i in range(pieces)
        ],
        axis=0,
    )
    rows = (stream_ref[...].astype(jnp.float32) + live * attn).astype(jnp.bfloat16)
    rows = rows.astype(jnp.float32)
    rows_ref[...] = rows
    own = middle_ref.shape[0]
    start = pl.multiple_of(lax.axis_index("tp") * own, own)
    middle_ref[...] = rows_ref[pl.ds(start, own), :].astype(jnp.bfloat16)
    live_rows_ref[...] = jnp.broadcast_to(live, live_rows_ref.shape)
    live_ref[...] = live_rows_ref[pl.ds(start, own), :]
    squares = jnp.sum(rows * rows, axis=1, keepdims=True)
    scaled_ref[...] = (rows * gain_ref[...]).astype(jnp.bfloat16)
    half = lax.rem(lax.axis_index("role"), 2)
    size = (send_ref.shape[1] - LANES) // 2
    piece_dots(scaled_ref, wg_ref, wu_ref, send_ref, 1 - half, 0, size)
    tail = split_three(squares)
    send_ref[:, 2 * size :] = tail
    tail_ref[...] = tail.astype(jnp.float32)


def piece_kernel(theirs, begin, size, scaled_ref, wg_ref, wu_ref, *refs):
    half = lax.rem(lax.axis_index("role"), 2)
    side = 1 - half if theirs else half
    piece_dots(scaled_ref, wg_ref, wu_ref, refs[-1], side, begin, size)


def piece_dots(scaled_ref, wg_ref, wu_ref, out_ref, side, begin, size):
    scaled = scaled_ref[...]
    first = side * (wg_ref.shape[1] // 2) + begin
    for w_ref, base in ((wg_ref, 0), (wu_ref, size)):
        for at in range(0, size, CHUNK):
            step = min(CHUNK, size - at)
            start = pl.multiple_of(first + at, LANES)
            out_ref[:, base + at : base + at + step] = jnp.dot(
                scaled, w_ref[:, pl.ds(start, step)], preferred_element_type=jnp.float32
            ).astype(out_ref.dtype)


def pair_tail_kernel(keep_ref, tail_ref, got_ref, out_ref):
    wide = keep_ref.shape[1]
    out_ref[:, :wide] = (keep_ref[...] + got_ref[:, :wide].astype(jnp.float32)).astype(
        jnp.bfloat16
    )
    squares = jnp.sum(
        tail_ref[...] + got_ref[:, wide:].astype(jnp.float32), axis=1, keepdims=True
    )
    out_ref[:, wide:] = split_three(squares)


def pair_kernel(keep_ref, got_ref, out_ref):
    out_ref[...] = (
        keep_ref[...].astype(jnp.float32) + got_ref[...].astype(jnp.float32)
    ).astype(jnp.bfloat16)


def first_hidden_kernel(own_ref, got_ref, hidden_ref, inverse_ref):
    wide = 2 * hidden_ref.shape[1]
    squares = jnp.sum(
        own_ref[:, wide:].astype(jnp.float32) + got_ref[:, wide:].astype(jnp.float32),
        axis=1,
        keepdims=True,
    )
    inverse = lax.rsqrt(squares / D + epsilon)
    inverse_ref[...] = jnp.broadcast_to(inverse, inverse_ref.shape)
    gated(own_ref, got_ref, inverse, hidden_ref)


def hidden_kernel(own_ref, got_ref, inverse_ref, _, hidden_ref):
    gated(own_ref, got_ref, inverse_ref[:, :1], hidden_ref)


def gated(own_ref, got_ref, inverse, hidden_ref):
    size = hidden_ref.shape[1]
    total = own_ref[:, : 2 * size].astype(jnp.float32) + got_ref[:, : 2 * size].astype(jnp.float32)
    total = total * inverse
    gate, up = total[:, :size], total[:, size:]
    hidden_ref[...] = (gate / (1.0 + jnp.exp(-gate)) * up).astype(jnp.bfloat16)


def down_dots(theirs, begin, hidden_ref, w_ref, part):
    half = lax.rem(lax.axis_index("role"), 2)
    side = 1 - half if theirs else half
    start = pl.multiple_of(side * (w_ref.shape[0] // 2) + begin, LANES)
    return jnp.dot(
        hidden_ref[...],
        w_ref[pl.ds(start, hidden_ref.shape[1]), part],
        preferred_element_type=jnp.float32,
    )


def chunks(width):
    return [slice(at, min(at + CHUNK, width)) for at in range(0, width, CHUNK)]


def down_kernel(theirs, begin, hidden_ref, w_ref, *refs):
    *before_refs, rows_ref = refs
    for part in chunks(w_ref.shape[1]):
        rows = down_dots(theirs, begin, hidden_ref, w_ref, part)
        for before_ref in before_refs:
            rows = rows + before_ref[:, part]
        rows_ref[:, part] = rows


def last_down_kernel(theirs, begin, hidden_ref, w_ref, before_ref, *refs):
    *out_refs, rows_ref = refs
    place = lax.axis_index("tp")
    own = out_refs[0].shape[0]
    for part in chunks(w_ref.shape[1]):
        rows_ref[:, part] = before_ref[:, part] + down_dots(
            theirs, begin, hidden_ref, w_ref, part
        )
    for k, out_ref in enumerate(out_refs):
        start = pl.multiple_of((place ^ k) * own, own)
        out_ref[...] = rows_ref[pl.ds(start, own), :].astype(jnp.bfloat16)


def local_exchange(
    residual,
    attn_gain,
    w_query,
    w_key,
    w_value,
    w_output,
    cache_keys,
    cache_values,
    lengths,
    served,
    ffn_gain,
    w_gate,
    w_up,
    w_down,
):
    if not exchange_fits(residual, w_query, w_key, w_gate):
        return local(
            residual,
            attn_gain,
            w_query,
            w_key,
            w_value,
            w_output,
            cache_keys,
            cache_values,
            lengths,
            served,
            ffn_gain,
            w_gate,
            w_up,
            w_down,
        )
    tp_count, role_count = lax.axis_size("tp"), lax.axis_size("role")
    devices = tp_count * role_count
    own, features = residual.shape
    rows = own * tp_count
    each = rows // devices
    block = jax.ShapeDtypeStruct((own, features), jnp.bfloat16)

    table = jax.ShapeDtypeStruct((each, HEAD_DIM), jnp.float32)
    cosine, sine = call(angle_kernel, [table] * 2, [lengths], smem=1, cost=COVER[0])
    others = {k: swap(residual, "tp", k) for k in reversed(range(1, tp_count))}
    blocks = [residual] + [others[k] for k in range(1, tp_count)]
    payload = w_query.shape[1] + 2 * w_key.shape[1] + LANES
    depth = -(-each * payload // (LANES * 8)) * 8
    sums, stream = call(
        project_kernel,
        [
            jax.ShapeDtypeStruct((devices, depth, LANES), jnp.bfloat16),
            jax.ShapeDtypeStruct((rows, features), jnp.bfloat16),
        ],
        [cosine, *blocks, attn_gain[None, :], in_vmem(w_query), in_vmem(w_key), in_vmem(w_value)],
        scratch=[
            pltpu.VMEM((rows, features), jnp.float32),
            pltpu.VMEM((rows * payload // LANES, LANES), jnp.float32),
            pltpu.VMEM((devices * depth, LANES), jnp.float32),
        ],
        cost=COVER[1],
    )
    parts = lax.all_to_all(sums, ("role", "tp"), 0, 0)
    (heads,) = call(
        attend_kernel,
        [jax.ShapeDtypeStruct((devices, each * GROUP, LANES), jnp.bfloat16)],
        [lengths, parts, cosine, sine, in_vmem(cache_keys), in_vmem(cache_values)],
        smem=1,
        cost=COVER[2],
    )
    heads = lax.all_to_all(heads, ("role", "tp"), 0, 0)
    near, far = STEPS
    pieces = [jax.ShapeDtypeStruct((rows * part // 32, features), jnp.bfloat16) for part in PARTS]
    attn = call(
        output_kernel,
        pieces,
        [heads, in_vmem(w_output)],
        scratch=[pltpu.VMEM((rows * GROUP, LANES), jnp.float32)],
        cost=COVER[3],
    )
    terms = []
    got = [swap(value, "tp", near) for value in attn]
    for value, arrived, piece in zip(attn, got, pieces):
        (paired,) = call(pair_kernel, [piece], [value, arrived])
        terms += [paired, swap(paired, "tp", far)]
    width = w_gate.shape[1] // 2
    first = -(-width * FIRST_PART // (100 * 2 * LANES)) * 2 * LANES
    sizes = (first, width - first)
    w_gate, w_up, w_down = in_vmem(w_gate), in_vmem(w_up), in_vmem(w_down)
    rows_f32 = jax.ShapeDtypeStruct((rows, features), jnp.float32)
    row_scratch = pltpu.VMEM((rows, features), jnp.float32)

    def wide(size, dtype, more=0):
        return jax.ShapeDtypeStruct((rows, 2 * size + more), dtype)

    def half_of(piece):
        return jax.ShapeDtypeStruct((rows, sizes[piece]), jnp.bfloat16)

    scaled, tail, send, middle, live = call(
        middle_kernel,
        [
            jax.ShapeDtypeStruct((rows, features), jnp.bfloat16),
            jax.ShapeDtypeStruct((rows, LANES), jnp.float32),
            wide(sizes[0], jnp.bfloat16, LANES),
            block,
            jax.ShapeDtypeStruct((own, LANES), jnp.float32),
        ],
        [served[None, :], stream, *terms, ffn_gain[None, :], w_gate, w_up],
        scratch=[row_scratch, pltpu.VMEM((rows, LANES), jnp.float32)],
        cost=COVER[4],
    )
    got = swap(send, "role", 1)
    (keep,) = call(
        functools.partial(piece_kernel, False, 0, sizes[0]),
        [wide(sizes[0], jnp.float32)],
        [scaled, w_gate, w_up],
        cost=COVER[5],
    )
    (chip_0,) = call(
        pair_tail_kernel, [wide(sizes[0], jnp.bfloat16, LANES)], [keep, tail, got]
    )
    far_0 = swap(chip_0, "role", 2)
    (send,) = call(
        functools.partial(piece_kernel, True, sizes[0], sizes[1]),
        [wide(sizes[1], jnp.bfloat16)],
        [scaled, w_gate, w_up, chip_0],
        cost=COVER[6],
    )
    got = swap(send, "role", 1)
    (keep,) = call(
        functools.partial(piece_kernel, False, sizes[0], sizes[1]),
        [wide(sizes[1], jnp.float32)],
        [scaled, w_gate, w_up],
        cost=COVER[7],
    )
    (chip_1,) = call(pair_kernel, [wide(sizes[1], jnp.bfloat16)], [keep, got])
    far_1 = swap(chip_1, "role", 2)
    hidden, inverse = call(
        first_hidden_kernel,
        [half_of(0), jax.ShapeDtypeStruct((rows, LANES), jnp.float32)],
        [chip_0, far_0],
    )
    other = swap(hidden, "role", 1)
    (down,) = call(
        functools.partial(down_kernel, False, 0), [rows_f32], [hidden, w_down], cost=COVER[8]
    )
    (down,) = call(
        functools.partial(down_kernel, True, 0), [rows_f32], [other, w_down, down], cost=COVER[8]
    )
    (hidden,) = call(hidden_kernel, [half_of(1)], [chip_1, far_1, inverse, down])
    other = swap(hidden, "role", 1)
    (down,) = call(
        functools.partial(down_kernel, False, sizes[0]),
        [rows_f32],
        [hidden, w_down, down],
        cost=COVER[9],
    )
    terms = call(
        functools.partial(last_down_kernel, True, sizes[0]),
        [block] * tp_count,
        [other, w_down, down],
        scratch=[row_scratch],
        cost=COVER[9],
    )
    terms = [terms[0]] + [swap(terms[k], "tp", k) for k in range(1, tp_count)]
    ffn = terms[0].astype(jnp.float32)
    for term in terms[1:]:
        ffn = ffn + term.astype(jnp.float32)
    return (middle.astype(jnp.float32) + live[:, :1] * ffn).astype(jnp.bfloat16)


def solution(mesh):
    return jax.shard_map(
        local_exchange,
        mesh=mesh,
        in_specs=(
            P(("groups", "tp"), "role"),
            P("role"),
            P("role", "tp"),
            P("role", "tp"),
            P("role", "tp"),
            P("tp", "role"),
            P(("groups", "role", "tp"), None, None),
            P(("groups", "role", "tp"), None, None),
            P(("groups", "role", "tp")),
            P("groups"),
            P("role"),
            P("role", "tp"),
            P("role", "tp"),
            P("tp", "role"),
        ),
        out_specs=P(("groups", "tp"), "role"),
        check_vma=False,
    )
```

```python
import functools
import math

import jax
import jax.numpy as jnp
from jax import lax
from jax.experimental import pallas as pl
from jax.experimental.pallas import tpu as pltpu
from jax.sharding import PartitionSpec as P


D = 8192
HEADS = 32
KV_HEADS = 4
HEAD_DIM = 128
WINDOW = 256
GROUP = 8


epsilon = 1e-05
rope_base = 500000.0


def rotate(vectors, positions):
    halfway = vectors.shape[-1] // 2
    frequency = jnp.power(
        jnp.float32(rope_base), -jnp.arange(halfway, dtype=jnp.float32) * 2.0 / vectors.shape[-1]
    )
    angles = positions.astype(jnp.float32)[:, None, None] * frequency[None, None, :]
    cosine = jnp.cos(angles)
    sine_part = jnp.sin(angles)
    leading = vectors[..., :halfway]
    trailing = vectors[..., halfway:]
    return jnp.concatenate(
        [leading * cosine - trailing * sine_part, trailing * cosine + leading * sine_part], axis=-1
    )


def attend(queries, new_key, new_value, keys, values, lengths):
    batch_rows = queries.shape[0]
    factor = HEAD_DIM ** (-0.5)
    grouped = queries.reshape(batch_rows, KV_HEADS, GROUP, HEAD_DIM)
    key_blocks = keys.reshape(batch_rows, WINDOW, KV_HEADS, HEAD_DIM)
    value_blocks = values.reshape(batch_rows, WINDOW, KV_HEADS, HEAD_DIM)
    scores = (
        jnp.einsum("nkgd,nwkd->nkgw", grouped, key_blocks, preferred_element_type=jnp.float32)
        * factor
    )
    self_score = (
        jnp.einsum("nkgd,nkd->nkg", grouped, new_key, preferred_element_type=jnp.float32) * factor
    )
    usable = jnp.arange(WINDOW, dtype=jnp.int32)[None, :] < lengths[:, None]
    scores = jnp.where(usable[:, None, None, :], scores, -jnp.inf)
    highest = jnp.maximum(jnp.max(scores, axis=-1), self_score)
    weights = jnp.exp(scores - highest[..., None])
    self_weight = jnp.exp(self_score - highest)
    denominator = jnp.sum(weights, axis=-1) + self_weight
    chances = (weights / denominator[..., None]).astype(jnp.bfloat16)
    self_chance = (self_weight / denominator).astype(jnp.bfloat16)
    attended = jnp.einsum(
        "nkgw,nwkd->nkgd", chances, value_blocks, preferred_element_type=jnp.float32
    )
    attended = (
        attended
        + self_chance.astype(jnp.float32)[..., None] * new_value.astype(jnp.float32)[:, :, None, :]
    )
    return attended.reshape(batch_rows, HEADS * HEAD_DIM).astype(jnp.bfloat16)


def feed_forward(middle, ffn_gain, w_gate, w_up, w_down):
    widened = middle.astype(jnp.float32)
    squares = lax.psum(jnp.sum(widened * widened, axis=1), "role")
    inverse = lax.rsqrt(squares / D + epsilon)
    mid_normed = (widened * inverse[:, None] * ffn_gain[None, :]).astype(jnp.bfloat16)
    gate_part = jnp.dot(mid_normed, w_gate, preferred_element_type=jnp.float32)
    up_part = jnp.dot(mid_normed, w_up, preferred_element_type=jnp.float32)
    gate_total, up_total = (
        lax.psum(gate_part.astype(jnp.bfloat16), "role").astype(jnp.float32),
        lax.psum(up_part.astype(jnp.bfloat16), "role").astype(jnp.float32),
    )
    hidden = (jax.nn.silu(gate_total) * up_total).astype(jnp.bfloat16)
    down_terms = jnp.dot(hidden, w_down, preferred_element_type=jnp.float32)
    return lax.psum_scatter(
        down_terms.astype(jnp.bfloat16), "tp", scatter_dimension=0, tiled=True
    ).astype(jnp.float32)


def local(
    residual,
    attn_gain,
    w_query,
    w_key,
    w_value,
    w_output,
    cache_keys,
    cache_values,
    lengths,
    served,
    ffn_gain,
    w_gate,
    w_up,
    w_down,
):
    own_rows = residual.shape[0]
    tp_count = lax.axis_size("tp")
    row_start = lax.axis_index("tp") * own_rows
    live_own = lax.dynamic_slice_in_dim(served, row_start, own_rows, 0).astype(jnp.float32)[:, None]
    rows_all = lax.all_gather(residual, "tp", axis=0, tiled=True)
    widened = rows_all.astype(jnp.float32)
    squares = lax.psum(jnp.sum(widened * widened, axis=1), "role")
    inverse = lax.rsqrt(squares / D + epsilon)
    normed = (widened * inverse[:, None] * attn_gain[None, :]).astype(jnp.bfloat16)
    partial_value = jnp.concatenate(
        [
            jnp.dot(normed, w_query, preferred_element_type=jnp.float32),
            jnp.dot(normed, w_key, preferred_element_type=jnp.float32),
            jnp.dot(normed, w_value, preferred_element_type=jnp.float32),
        ],
        axis=1,
    )
    summed = lax.psum_scatter(
        partial_value.astype(jnp.bfloat16), "role", scatter_dimension=0, tiled=True
    ).astype(jnp.float32)
    gathered = lax.all_to_all(
        summed.astype(jnp.bfloat16), "tp", split_axis=0, concat_axis=1, tiled=True
    ).astype(summed.dtype)
    local_rows = gathered.shape[0]
    query_cols = w_query.shape[1]
    kv_cols = w_key.shape[1]
    blocks = gathered.reshape(local_rows, tp_count, query_cols + 2 * kv_cols)
    queries = blocks[:, :, :query_cols].reshape(local_rows, HEADS, HEAD_DIM)
    new_key = blocks[:, :, query_cols : query_cols + kv_cols].reshape(
        local_rows, KV_HEADS, HEAD_DIM
    )
    new_value = (
        blocks[:, :, query_cols + kv_cols :]
        .reshape(local_rows, KV_HEADS, HEAD_DIM)
        .astype(jnp.bfloat16)
    )
    queries = rotate(queries, lengths).astype(jnp.bfloat16)
    new_key = rotate(new_key, lengths).astype(jnp.bfloat16)
    attended = attend(queries, new_key, new_value, cache_keys, cache_values, lengths)
    head_block = lax.all_to_all(attended, "tp", split_axis=1, concat_axis=0, tiled=True)
    attn_terms = jnp.dot(
        lax.all_gather(head_block, "role", axis=0, tiled=True),
        w_output,
        preferred_element_type=jnp.float32,
    )
    attn = lax.psum_scatter(
        attn_terms.astype(jnp.bfloat16), "tp", scatter_dimension=0, tiled=True
    ).astype(jnp.float32)
    middle_own = (residual.astype(jnp.float32) + live_own * attn).astype(jnp.bfloat16)
    middle = lax.all_gather(middle_own, "tp", axis=0, tiled=True)
    ffn = feed_forward(middle, ffn_gain, w_gate, w_up, w_down)
    return (middle_own.astype(jnp.float32) + live_own * ffn).astype(jnp.bfloat16)


LANES = 128
MIB = 2**20
COVER = (100, 1, 1, 1, 10, 10, 10, 1, 1, 1)
CHUNK = 512
FIRST_PART = 57


def exchange_fits(residual, w_query, w_key, w_gate):
    tp_count, role_count = lax.axis_size("tp"), lax.axis_size("role")
    return (
        tp_count == KV_HEADS
        and role_count == 4
        and residual.shape[0] % 8 == 0
        and residual.shape[1] % (2 * LANES) == 0
        and w_query.shape[1] == GROUP * LANES
        and w_key.shape[1] == LANES
        and w_gate.shape[1] % (4 * LANES) == 0
        and w_gate.shape[1] >= 8 * LANES
    )


def swap(value, axis, distance):
    count = lax.axis_size(axis)
    return lax.ppermute(value, axis, [(i, i ^ distance) for i in range(count)])


def in_vmem(value):
    return pltpu.with_memory_space_constraint(value, pltpu.VMEM)


def call(kernel, outs, args, scratch=(), limit=4 * MIB, smem=0, cost=0):
    specs = [pl.BlockSpec(memory_space=pltpu.SMEM)] * smem
    specs += [pl.BlockSpec(memory_space=pltpu.VMEM)] * (len(args) - smem)
    return pl.pallas_call(
        kernel,
        out_shape=outs,
        in_specs=specs,
        out_specs=[pl.BlockSpec(memory_space=pltpu.VMEM)] * len(outs),
        scratch_shapes=list(scratch),
        compiler_params=pltpu.CompilerParams(vmem_limit_bytes=limit),
        cost_estimate=pl.CostEstimate(flops=cost * 10**9, bytes_accessed=MIB, transcendentals=0),
    )(*args)


def split_three(column):
    first = column.astype(jnp.bfloat16)
    left = column - first.astype(jnp.float32)
    second = left.astype(jnp.bfloat16)
    third = (left - second.astype(jnp.float32)).astype(jnp.bfloat16)
    lane = lax.broadcasted_iota(jnp.int32, (column.shape[0], LANES), 1)
    wide = jnp.where(lane == 0, first.astype(jnp.float32), 0.0)
    wide = jnp.where(lane == 1, second.astype(jnp.float32), wide)
    return jnp.where(lane == 2, third.astype(jnp.float32), wide).astype(jnp.bfloat16)


def angle_kernel(lengths_ref, cosine_ref, sine_ref):
    count, width = cosine_ref.shape
    lane = lax.broadcasted_iota(jnp.int32, (1, width), 1)
    step = lax.rem(lane, width // 2).astype(jnp.float32)
    frequency = jnp.exp(step * (-2.0 / width * math.log(rope_base)))
    angles = jnp.concatenate(
        [lengths_ref[i].astype(jnp.float32) * frequency for i in range(count)], axis=0
    )
    cosine_ref[...] = jnp.cos(angles)
    sine = jnp.sin(angles)
    sine_ref[...] = jnp.where(lane < width // 2, -sine, sine)


def project_kernel(_, *refs):
    *block_refs, gain_ref, wq_ref, wk_ref, wv_ref, out_ref, stream_ref = refs[:-3]
    rows_ref, sums_ref, packed_ref = refs[-3:]
    place = lax.axis_index("tp")
    own = block_refs[0].shape[0]
    for k, block_ref in enumerate(block_refs):
        start = pl.multiple_of((place ^ k) * own, own)
        rows_ref[pl.ds(start, own), :] = block_ref[...].astype(jnp.float32)
    rows = rows_ref[...]
    stream_ref[...] = rows.astype(jnp.bfloat16)
    squares = jnp.sum(rows * rows, axis=1, keepdims=True)
    scaled = (rows * gain_ref[...]).astype(jnp.bfloat16)
    count = rows.shape[0]
    groups = 0
    for w_ref in (wq_ref, wk_ref, wv_ref):
        product = jnp.dot(scaled, w_ref[...], preferred_element_type=jnp.float32)
        for at in range(0, w_ref.shape[1], LANES):
            sums_ref[groups * count : (groups + 1) * count, :] = product[:, at : at + LANES]
            groups += 1
    sums_ref[groups * count :, :] = split_three(squares).astype(jnp.float32)
    groups += 1
    devices, depth, _ = out_ref.shape
    each = count // devices
    queries = wq_ref.shape[1] // LANES
    packed_ref[...] = jnp.zeros_like(packed_ref)
    for n in range(each):
        for g in range(groups):
            row = packed_row(n, g, each, queries, groups)
            packed_ref[pl.ds(row, devices, stride=depth), :] = sums_ref[
                pl.ds(g * count + n, devices, stride=each), :
            ]
    out_ref[...] = packed_ref[...].reshape(out_ref.shape).astype(jnp.bfloat16)


def packed_row(n, g, each, queries, groups):
    if g < queries:
        return n * queries + g
    return each * queries + n * (groups - queries) + g - queries


def attend_kernel(
    lengths_ref, got_ref, cosine_ref, sine_ref, keys_ref, values_ref, out_ref
):
    tp_count = KV_HEADS
    devices, depth, width = got_ref.shape
    each, window, _ = keys_ref.shape
    groups = GROUP + 3
    total = jnp.sum(
        got_ref[...].astype(jnp.float32).reshape(devices // tp_count, tp_count, depth, width),
        axis=0,
    )
    factor = HEAD_DIM ** (-0.5)
    scores, own_scores, own_values = [], [], []
    for n in range(each):
        cosine, sine = cosine_ref[n : n + 1, :], sine_ref[n : n + 1, :]
        tail = packed_row(n, GROUP, each, GROUP, groups)
        squares = jnp.sum(total[0, tail + 2 : tail + 3, :], axis=1, keepdims=True)
        inverse = lax.rsqrt(squares / D + epsilon)
        usable = lax.broadcasted_iota(jnp.int32, (GROUP, window), 1) < lengths_ref[n]
        for h in range(tp_count):
            query = total[h, n * GROUP : (n + 1) * GROUP, :]
            key = total[h, tail : tail + 1, :]
            query = query * cosine + pltpu.roll(query, width // 2, 1) * sine
            key = key * cosine + pltpu.roll(key, width // 2, 1) * sine
            query = query.astype(jnp.bfloat16)
            key = key.astype(jnp.bfloat16).astype(jnp.float32)
            score = lax.dot_general(
                query,
                keys_ref[n, :, h * width : (h + 1) * width],
                (((1,), (1,)), ((), ())),
                preferred_element_type=jnp.float32,
            )
            scores.append(jnp.where(usable, score * (inverse * factor), -jnp.inf))
            own_scores.append(
                jnp.sum(query.astype(jnp.float32) * key, axis=1, keepdims=True)
                * (inverse * inverse * factor)
            )
            value = (total[h, tail + 1 : tail + 2, :] * inverse).astype(jnp.bfloat16)
            own_values.append(value.astype(jnp.float32))
    scores, own_scores = jnp.concatenate(scores, axis=0), jnp.concatenate(own_scores, axis=0)
    highest = jnp.maximum(jnp.max(scores, axis=1, keepdims=True), own_scores)
    weights, own_weights = jnp.exp(scores - highest), jnp.exp(own_scores - highest)
    denominator = jnp.sum(weights, axis=1, keepdims=True) + own_weights
    chances = weights.astype(jnp.bfloat16)
    for n in range(each):
        for h in range(tp_count):
            at = (n * tp_count + h) * GROUP
            attended = jnp.dot(
                chances[at : at + GROUP],
                values_ref[n, :, h * width : (h + 1) * width],
                preferred_element_type=jnp.float32,
            )
            attended = attended + own_weights[at : at + GROUP] * own_values[n * tp_count + h]
            attended = attended / denominator[at : at + GROUP]
            for r in range(devices // tp_count):
                out_ref[r * tp_count + h, n * GROUP : (n + 1) * GROUP, :] = attended.astype(
                    jnp.bfloat16
                )


def output_kernel(heads_ref, w_ref, attended_ref, out_ref, heads_wide_ref):
    count = attended_ref.shape[0]
    groups = w_ref.shape[0] // LANES
    heads_wide_ref[...] = heads_ref[...].astype(jnp.float32).reshape(heads_wide_ref.shape)
    for g in range(groups):
        attended_ref[:, g * LANES : (g + 1) * LANES] = heads_wide_ref[
            pl.ds(g, count, stride=groups), :
        ].astype(jnp.bfloat16)
    output_dots(attended_ref, w_ref, out_ref, 0)


def more_output_kernel(begin, attended_ref, w_ref, out_ref):
    output_dots(attended_ref, w_ref, out_ref, begin)


def output_dots(attended_ref, w_ref, out_ref, begin):
    for part in chunks(out_ref.shape[1]):
        out_ref[:, part] = jnp.dot(
            attended_ref[...],
            w_ref[:, begin + part.start : begin + part.stop],
            preferred_element_type=jnp.float32,
        ).astype(jnp.bfloat16)


def live_column(served_ref, count):
    row = lax.broadcasted_iota(jnp.int32, (count, count), 0)
    column = lax.broadcasted_iota(jnp.int32, (count, count), 1)
    return jnp.sum(
        jnp.where(row == column, served_ref[...], 0).astype(jnp.float32), axis=1, keepdims=True
    )


def middle_part(live, stream_ref, term_refs, gain_ref, at, middle_ref, rows_ref):
    width = term_refs[0].shape[1]
    part = slice(at, at + width)
    attn = term_refs[0][...].astype(jnp.float32) + term_refs[1][...].astype(jnp.float32)
    rows = (stream_ref[:, part].astype(jnp.float32) + live * attn).astype(jnp.bfloat16)
    rows = rows.astype(jnp.float32)
    rows_ref[...] = rows
    own = middle_ref.shape[0]
    start = pl.multiple_of(lax.axis_index("tp") * own, own)
    middle_ref[...] = rows_ref[pl.ds(start, own), :].astype(jnp.bfloat16)
    squares = jnp.sum(rows * rows, axis=1, keepdims=True)
    return (rows * gain_ref[:, part]).astype(jnp.bfloat16), squares


def middle_kernel(*refs):
    served_ref, stream_ref, here_ref, far_ref, gain_ref, wg_ref, wu_ref, *refs = refs
    scaled_ref, squares_ref, partial_ref, middle_ref, live_ref, rows_ref, live_rows_ref = refs
    live = live_column(served_ref, stream_ref.shape[0])
    own = middle_ref.shape[0]
    start = pl.multiple_of(lax.axis_index("tp") * own, own)
    live_rows_ref[...] = jnp.broadcast_to(live, live_rows_ref.shape)
    live_ref[...] = live_rows_ref[pl.ds(start, own), :]
    scaled_ref[...], squares = middle_part(
        live, stream_ref, (here_ref, far_ref), gain_ref, 0, middle_ref, rows_ref
    )
    squares_ref[...] = jnp.broadcast_to(squares, squares_ref.shape)
    part_dots(scaled_ref, wg_ref, wu_ref, partial_ref, 0, ())


def more_middle_kernel(*refs):
    served_ref, stream_ref, here_ref, far_ref, gain_ref, wg_ref, wu_ref, *refs = refs
    before_ref, squares_ref, partial_ref, scaled_ref, tail_ref, send_ref, middle_ref, rows_ref = refs
    live = live_column(served_ref, stream_ref.shape[0])
    width = before_ref.shape[1]
    scaled, squares = middle_part(
        live, stream_ref, (here_ref, far_ref), gain_ref, width, middle_ref, rows_ref
    )
    scaled_ref[:, :width] = before_ref[...]
    scaled_ref[:, width:] = scaled
    wide = partial_ref.shape[1]
    part_dots(scaled_ref, wg_ref, wu_ref, send_ref, width, (partial_ref,))
    tail = split_three(squares + squares_ref[:, :1])
    send_ref[:, wide:] = tail
    tail_ref[...] = tail.astype(jnp.float32)


def part_dots(scaled_ref, wg_ref, wu_ref, out_ref, at, before_refs):
    side = 1 - lax.rem(lax.axis_index("role"), 2)
    size = out_ref.shape[1] // (4 * LANES) * 2 * LANES
    depth = scaled_ref.shape[1] - at
    scaled = scaled_ref[:, at:]
    for w_ref, base in ((wg_ref, 0), (wu_ref, size)):
        for step in range(0, size, CHUNK):
            count = min(CHUNK, size - step)
            start = pl.multiple_of(side * (w_ref.shape[1] // 2) + step, LANES)
            part = slice(base + step, base + step + count)
            product = jnp.dot(
                scaled,
                w_ref[at : at + depth, pl.ds(start, count)],
                preferred_element_type=jnp.float32,
            )
            for before_ref in before_refs:
                product = product + before_ref[:, part]
            out_ref[:, part] = product.astype(out_ref.dtype)


def piece_kernel(theirs, begin, size, scaled_ref, wg_ref, wu_ref, *refs):
    half = lax.rem(lax.axis_index("role"), 2)
    side = 1 - half if theirs else half
    piece_dots(scaled_ref, wg_ref, wu_ref, refs[-1], side, begin, size)


def piece_dots(scaled_ref, wg_ref, wu_ref, out_ref, side, begin, size):
    scaled = scaled_ref[...]
    first = side * (wg_ref.shape[1] // 2) + begin
    for w_ref, base in ((wg_ref, 0), (wu_ref, size)):
        for at in range(0, size, CHUNK):
            step = min(CHUNK, size - at)
            start = pl.multiple_of(first + at, LANES)
            out_ref[:, base + at : base + at + step] = jnp.dot(
                scaled, w_ref[:, pl.ds(start, step)], preferred_element_type=jnp.float32
            ).astype(out_ref.dtype)


def pair_tail_kernel(keep_ref, tail_ref, got_ref, out_ref):
    wide = keep_ref.shape[1]
    out_ref[:, :wide] = (keep_ref[...] + got_ref[:, :wide].astype(jnp.float32)).astype(
        jnp.bfloat16
    )
    squares = jnp.sum(
        tail_ref[...] + got_ref[:, wide:].astype(jnp.float32), axis=1, keepdims=True
    )
    out_ref[:, wide:] = split_three(squares)


def pair_kernel(keep_ref, got_ref, out_ref):
    out_ref[...] = (
        keep_ref[...].astype(jnp.float32) + got_ref[...].astype(jnp.float32)
    ).astype(jnp.bfloat16)


def first_hidden_kernel(own_ref, got_ref, hidden_ref, inverse_ref):
    wide = 2 * hidden_ref.shape[1]
    squares = jnp.sum(
        own_ref[:, wide:].astype(jnp.float32) + got_ref[:, wide:].astype(jnp.float32),
        axis=1,
        keepdims=True,
    )
    inverse = lax.rsqrt(squares / D + epsilon)
    inverse_ref[...] = jnp.broadcast_to(inverse, inverse_ref.shape)
    gated(own_ref, got_ref, inverse, hidden_ref)


def hidden_kernel(own_ref, got_ref, inverse_ref, _, hidden_ref):
    gated(own_ref, got_ref, inverse_ref[:, :1], hidden_ref)


def gated(own_ref, got_ref, inverse, hidden_ref):
    size = hidden_ref.shape[1]
    total = own_ref[:, : 2 * size].astype(jnp.float32) + got_ref[:, : 2 * size].astype(jnp.float32)
    total = total * inverse
    gate, up = total[:, :size], total[:, size:]
    hidden_ref[...] = (gate / (1.0 + jnp.exp(-gate)) * up).astype(jnp.bfloat16)


def down_dots(theirs, begin, hidden_ref, w_ref, part):
    half = lax.rem(lax.axis_index("role"), 2)
    side = 1 - half if theirs else half
    start = pl.multiple_of(side * (w_ref.shape[0] // 2) + begin, LANES)
    return jnp.dot(
        hidden_ref[...],
        w_ref[pl.ds(start, hidden_ref.shape[1]), part],
        preferred_element_type=jnp.float32,
    )


def chunks(width):
    return [slice(at, min(at + CHUNK, width)) for at in range(0, width, CHUNK)]


def down_kernel(theirs, begin, hidden_ref, w_ref, *refs):
    *before_refs, rows_ref = refs
    for part in chunks(w_ref.shape[1]):
        rows = down_dots(theirs, begin, hidden_ref, w_ref, part)
        for before_ref in before_refs:
            rows = rows + before_ref[:, part]
        rows_ref[:, part] = rows


def last_down_kernel(theirs, begin, hidden_ref, w_ref, before_ref, *refs):
    *out_refs, rows_ref = refs
    place = lax.axis_index("tp")
    own = out_refs[0].shape[0]
    for part in chunks(w_ref.shape[1]):
        rows_ref[:, part] = before_ref[:, part] + down_dots(
            theirs, begin, hidden_ref, w_ref, part
        )
    for k, out_ref in enumerate(out_refs):
        start = pl.multiple_of((place ^ k) * own, own)
        out_ref[...] = rows_ref[pl.ds(start, own), :].astype(jnp.bfloat16)


def local_exchange(
    residual,
    attn_gain,
    w_query,
    w_key,
    w_value,
    w_output,
    cache_keys,
    cache_values,
    lengths,
    served,
    ffn_gain,
    w_gate,
    w_up,
    w_down,
):
    if not exchange_fits(residual, w_query, w_key, w_gate):
        return local(
            residual,
            attn_gain,
            w_query,
            w_key,
            w_value,
            w_output,
            cache_keys,
            cache_values,
            lengths,
            served,
            ffn_gain,
            w_gate,
            w_up,
            w_down,
        )
    tp_count, role_count = lax.axis_size("tp"), lax.axis_size("role")
    devices = tp_count * role_count
    own, features = residual.shape
    rows = own * tp_count
    each = rows // devices
    block = jax.ShapeDtypeStruct((own, features), jnp.bfloat16)

    table = jax.ShapeDtypeStruct((each, HEAD_DIM), jnp.float32)
    cosine, sine = call(angle_kernel, [table] * 2, [lengths], smem=1, cost=COVER[0])
    others = {k: swap(residual, "tp", k) for k in reversed(range(1, tp_count))}
    blocks = [residual] + [others[k] for k in range(1, tp_count)]
    payload = w_query.shape[1] + 2 * w_key.shape[1] + LANES
    depth = -(-each * payload // (LANES * 8)) * 8
    sums, stream = call(
        project_kernel,
        [
            jax.ShapeDtypeStruct((devices, depth, LANES), jnp.bfloat16),
            jax.ShapeDtypeStruct((rows, features), jnp.bfloat16),
        ],
        [cosine, *blocks, attn_gain[None, :], in_vmem(w_query), in_vmem(w_key), in_vmem(w_value)],
        scratch=[
            pltpu.VMEM((rows, features), jnp.float32),
            pltpu.VMEM((rows * payload // LANES, LANES), jnp.float32),
            pltpu.VMEM((devices * depth, LANES), jnp.float32),
        ],
        cost=COVER[1],
    )
    parts = lax.all_to_all(sums, ("role", "tp"), 0, 0)
    (heads,) = call(
        attend_kernel,
        [jax.ShapeDtypeStruct((devices, each * GROUP, LANES), jnp.bfloat16)],
        [lengths, parts, cosine, sine, in_vmem(cache_keys), in_vmem(cache_values)],
        smem=1,
        cost=COVER[2],
    )
    heads = lax.all_to_all(heads, ("role", "tp"), 0, 0)
    piece = jax.ShapeDtypeStruct((rows, features // 2), jnp.bfloat16)
    w_output = in_vmem(w_output)
    attended, attn_0 = call(
        output_kernel,
        [jax.ShapeDtypeStruct((rows, w_output.shape[0]), jnp.bfloat16), piece],
        [heads, w_output],
        scratch=[pltpu.VMEM((rows * GROUP, LANES), jnp.float32)],
        cost=COVER[3],
    )
    got_0 = swap(attn_0, "tp", 1)
    (attn_1,) = call(
        functools.partial(more_output_kernel, features // 2),
        [piece],
        [attended, w_output],
        cost=COVER[3],
    )
    terms = []
    got_1 = swap(attn_1, "tp", 1)
    for value, got in ((attn_0, got_0), (attn_1, got_1)):
        (paired,) = call(pair_kernel, [piece], [value, got])
        terms += [paired, swap(paired, "tp", 2)]
    width = w_gate.shape[1] // 2
    first = -(-width * FIRST_PART // (100 * 2 * LANES)) * 2 * LANES
    sizes = (first, width - first)
    w_gate, w_up, w_down = in_vmem(w_gate), in_vmem(w_up), in_vmem(w_down)
    rows_f32 = jax.ShapeDtypeStruct((rows, features), jnp.float32)
    row_scratch = pltpu.VMEM((rows, features), jnp.float32)

    def wide(size, dtype, more=0):
        return jax.ShapeDtypeStruct((rows, 2 * size + more), dtype)

    def half_of(piece):
        return jax.ShapeDtypeStruct((rows, sizes[piece]), jnp.bfloat16)

    first_args = [served[None, :], stream]
    weight_args = [ffn_gain[None, :], w_gate, w_up]
    half_block = jax.ShapeDtypeStruct((own, features // 2), jnp.bfloat16)
    lane_rows = jax.ShapeDtypeStruct((rows, LANES), jnp.float32)
    half_scratch = pltpu.VMEM((rows, features // 2), jnp.float32)
    scaled_0, squares, partial, middle_0, live = call(
        middle_kernel,
        [
            piece,
            lane_rows,
            wide(sizes[0], jnp.float32),
            half_block,
            jax.ShapeDtypeStruct((own, LANES), jnp.float32),
        ],
        [*first_args, *terms[:2], *weight_args],
        scratch=[half_scratch, pltpu.VMEM((rows, LANES), jnp.float32)],
        cost=COVER[4],
    )
    scaled, tail, send, middle_1 = call(
        more_middle_kernel,
        [
            jax.ShapeDtypeStruct((rows, features), jnp.bfloat16),
            lane_rows,
            wide(sizes[0], jnp.bfloat16, LANES),
            half_block,
        ],
        [*first_args, *terms[2:], *weight_args, scaled_0, squares, partial],
        scratch=[half_scratch],
        cost=COVER[4],
    )
    middle = jnp.concatenate([middle_0, middle_1], axis=1)
    got = swap(send, "role", 1)
    (keep,) = call(
        functools.partial(piece_kernel, False, 0, sizes[0]),
        [wide(sizes[0], jnp.float32)],
        [scaled, w_gate, w_up],
        cost=COVER[5],
    )
    (chip_0,) = call(
        pair_tail_kernel, [wide(sizes[0], jnp.bfloat16, LANES)], [keep, tail, got]
    )
    far_0 = swap(chip_0, "role", 2)
    (send,) = call(
        functools.partial(piece_kernel, True, sizes[0], sizes[1]),
        [wide(sizes[1], jnp.bfloat16)],
        [scaled, w_gate, w_up, chip_0],
        cost=COVER[6],
    )
    got = swap(send, "role", 1)
    (keep,) = call(
        functools.partial(piece_kernel, False, sizes[0], sizes[1]),
        [wide(sizes[1], jnp.float32)],
        [scaled, w_gate, w_up],
        cost=COVER[7],
    )
    (chip_1,) = call(pair_kernel, [wide(sizes[1], jnp.bfloat16)], [keep, got])
    far_1 = swap(chip_1, "role", 2)
    hidden, inverse = call(
        first_hidden_kernel,
        [half_of(0), jax.ShapeDtypeStruct((rows, LANES), jnp.float32)],
        [chip_0, far_0],
    )
    other = swap(hidden, "role", 1)
    (down,) = call(
        functools.partial(down_kernel, False, 0), [rows_f32], [hidden, w_down], cost=COVER[8]
    )
    (down,) = call(
        functools.partial(down_kernel, True, 0), [rows_f32], [other, w_down, down], cost=COVER[8]
    )
    (hidden,) = call(hidden_kernel, [half_of(1)], [chip_1, far_1, inverse, down])
    other = swap(hidden, "role", 1)
    (down,) = call(
        functools.partial(down_kernel, False, sizes[0]),
        [rows_f32],
        [hidden, w_down, down],
        cost=COVER[9],
    )
    terms = call(
        functools.partial(last_down_kernel, True, sizes[0]),
        [block] * tp_count,
        [other, w_down, down],
        scratch=[row_scratch],
        cost=COVER[9],
    )
    terms = [terms[0]] + [swap(terms[k], "tp", k) for k in range(1, tp_count)]
    ffn = terms[0].astype(jnp.float32)
    for term in terms[1:]:
        ffn = ffn + term.astype(jnp.float32)
    return (middle.astype(jnp.float32) + live[:, :1] * ffn).astype(jnp.bfloat16)


def solution(mesh):
    return jax.shard_map(
        local_exchange,
        mesh=mesh,
        in_specs=(
            P(("groups", "tp"), "role"),
            P("role"),
            P("role", "tp"),
            P("role", "tp"),
            P("role", "tp"),
            P("tp", "role"),
            P(("groups", "role", "tp"), None, None),
            P(("groups", "role", "tp"), None, None),
            P(("groups", "role", "tp")),
            P("groups"),
            P("role"),
            P("role", "tp"),
            P("role", "tp"),
            P("tp", "role"),
        ),
        out_specs=P(("groups", "tp"), "role"),
        check_vma=False,
    )
```

```python
import functools
import math

import jax
import jax.numpy as jnp
from jax import lax
from jax.experimental import pallas as pl
from jax.experimental.pallas import tpu as pltpu
from jax.sharding import PartitionSpec as P


D = 8192
HEADS = 32
KV_HEADS = 4
HEAD_DIM = 128
WINDOW = 256
GROUP = 8


epsilon = 1e-05
rope_base = 500000.0


def rotate(vectors, positions):
    halfway = vectors.shape[-1] // 2
    frequency = jnp.power(
        jnp.float32(rope_base), -jnp.arange(halfway, dtype=jnp.float32) * 2.0 / vectors.shape[-1]
    )
    angles = positions.astype(jnp.float32)[:, None, None] * frequency[None, None, :]
    cosine = jnp.cos(angles)
    sine_part = jnp.sin(angles)
    leading = vectors[..., :halfway]
    trailing = vectors[..., halfway:]
    return jnp.concatenate(
        [leading * cosine - trailing * sine_part, trailing * cosine + leading * sine_part], axis=-1
    )


def attend(queries, new_key, new_value, keys, values, lengths):
    batch_rows = queries.shape[0]
    factor = HEAD_DIM ** (-0.5)
    grouped = queries.reshape(batch_rows, KV_HEADS, GROUP, HEAD_DIM)
    key_blocks = keys.reshape(batch_rows, WINDOW, KV_HEADS, HEAD_DIM)
    value_blocks = values.reshape(batch_rows, WINDOW, KV_HEADS, HEAD_DIM)
    scores = (
        jnp.einsum("nkgd,nwkd->nkgw", grouped, key_blocks, preferred_element_type=jnp.float32)
        * factor
    )
    self_score = (
        jnp.einsum("nkgd,nkd->nkg", grouped, new_key, preferred_element_type=jnp.float32) * factor
    )
    usable = jnp.arange(WINDOW, dtype=jnp.int32)[None, :] < lengths[:, None]
    scores = jnp.where(usable[:, None, None, :], scores, -jnp.inf)
    highest = jnp.maximum(jnp.max(scores, axis=-1), self_score)
    weights = jnp.exp(scores - highest[..., None])
    self_weight = jnp.exp(self_score - highest)
    denominator = jnp.sum(weights, axis=-1) + self_weight
    chances = (weights / denominator[..., None]).astype(jnp.bfloat16)
    self_chance = (self_weight / denominator).astype(jnp.bfloat16)
    attended = jnp.einsum(
        "nkgw,nwkd->nkgd", chances, value_blocks, preferred_element_type=jnp.float32
    )
    attended = (
        attended
        + self_chance.astype(jnp.float32)[..., None] * new_value.astype(jnp.float32)[:, :, None, :]
    )
    return attended.reshape(batch_rows, HEADS * HEAD_DIM).astype(jnp.bfloat16)


def feed_forward(middle, ffn_gain, w_gate, w_up, w_down):
    widened = middle.astype(jnp.float32)
    squares = lax.psum(jnp.sum(widened * widened, axis=1), "role")
    inverse = lax.rsqrt(squares / D + epsilon)
    mid_normed = (widened * inverse[:, None] * ffn_gain[None, :]).astype(jnp.bfloat16)
    gate_part = jnp.dot(mid_normed, w_gate, preferred_element_type=jnp.float32)
    up_part = jnp.dot(mid_normed, w_up, preferred_element_type=jnp.float32)
    gate_total, up_total = (
        lax.psum(gate_part.astype(jnp.bfloat16), "role").astype(jnp.float32),
        lax.psum(up_part.astype(jnp.bfloat16), "role").astype(jnp.float32),
    )
    hidden = (jax.nn.silu(gate_total) * up_total).astype(jnp.bfloat16)
    down_terms = jnp.dot(hidden, w_down, preferred_element_type=jnp.float32)
    return lax.psum_scatter(
        down_terms.astype(jnp.bfloat16), "tp", scatter_dimension=0, tiled=True
    ).astype(jnp.float32)


def local(
    residual,
    attn_gain,
    w_query,
    w_key,
    w_value,
    w_output,
    cache_keys,
    cache_values,
    lengths,
    served,
    ffn_gain,
    w_gate,
    w_up,
    w_down,
):
    own_rows = residual.shape[0]
    tp_count = lax.axis_size("tp")
    row_start = lax.axis_index("tp") * own_rows
    live_own = lax.dynamic_slice_in_dim(served, row_start, own_rows, 0).astype(jnp.float32)[:, None]
    rows_all = lax.all_gather(residual, "tp", axis=0, tiled=True)
    widened = rows_all.astype(jnp.float32)
    squares = lax.psum(jnp.sum(widened * widened, axis=1), "role")
    inverse = lax.rsqrt(squares / D + epsilon)
    normed = (widened * inverse[:, None] * attn_gain[None, :]).astype(jnp.bfloat16)
    partial_value = jnp.concatenate(
        [
            jnp.dot(normed, w_query, preferred_element_type=jnp.float32),
            jnp.dot(normed, w_key, preferred_element_type=jnp.float32),
            jnp.dot(normed, w_value, preferred_element_type=jnp.float32),
        ],
        axis=1,
    )
    summed = lax.psum_scatter(
        partial_value.astype(jnp.bfloat16), "role", scatter_dimension=0, tiled=True
    ).astype(jnp.float32)
    gathered = lax.all_to_all(
        summed.astype(jnp.bfloat16), "tp", split_axis=0, concat_axis=1, tiled=True
    ).astype(summed.dtype)
    local_rows = gathered.shape[0]
    query_cols = w_query.shape[1]
    kv_cols = w_key.shape[1]
    blocks = gathered.reshape(local_rows, tp_count, query_cols + 2 * kv_cols)
    queries = blocks[:, :, :query_cols].reshape(local_rows, HEADS, HEAD_DIM)
    new_key = blocks[:, :, query_cols : query_cols + kv_cols].reshape(
        local_rows, KV_HEADS, HEAD_DIM
    )
    new_value = (
        blocks[:, :, query_cols + kv_cols :]
        .reshape(local_rows, KV_HEADS, HEAD_DIM)
        .astype(jnp.bfloat16)
    )
    queries = rotate(queries, lengths).astype(jnp.bfloat16)
    new_key = rotate(new_key, lengths).astype(jnp.bfloat16)
    attended = attend(queries, new_key, new_value, cache_keys, cache_values, lengths)
    head_block = lax.all_to_all(attended, "tp", split_axis=1, concat_axis=0, tiled=True)
    attn_terms = jnp.dot(
        lax.all_gather(head_block, "role", axis=0, tiled=True),
        w_output,
        preferred_element_type=jnp.float32,
    )
    attn = lax.psum_scatter(
        attn_terms.astype(jnp.bfloat16), "tp", scatter_dimension=0, tiled=True
    ).astype(jnp.float32)
    middle_own = (residual.astype(jnp.float32) + live_own * attn).astype(jnp.bfloat16)
    middle = lax.all_gather(middle_own, "tp", axis=0, tiled=True)
    ffn = feed_forward(middle, ffn_gain, w_gate, w_up, w_down)
    return (middle_own.astype(jnp.float32) + live_own * ffn).astype(jnp.bfloat16)


LANES = 128
MIB = 2**20
COVER = (100, 1, 1, 1, 10, 10, 10, 1, 1, 1)
CHUNK = 512
FIRST_PART = 43


def exchange_fits(residual, w_query, w_key, w_gate):
    tp_count, role_count = lax.axis_size("tp"), lax.axis_size("role")
    return (
        tp_count == KV_HEADS
        and role_count == 4
        and residual.shape[0] % 8 == 0
        and residual.shape[1] % (2 * LANES) == 0
        and w_query.shape[1] == GROUP * LANES
        and w_key.shape[1] == LANES
        and w_gate.shape[1] % (4 * LANES) == 0
        and w_gate.shape[1] >= 8 * LANES
    )


def swap(value, axis, distance):
    count = lax.axis_size(axis)
    return lax.ppermute(value, axis, [(i, i ^ distance) for i in range(count)])


def in_vmem(value):
    return pltpu.with_memory_space_constraint(value, pltpu.VMEM)


def call(kernel, outs, args, scratch=(), limit=4 * MIB, smem=0, cost=0):
    specs = [pl.BlockSpec(memory_space=pltpu.SMEM)] * smem
    specs += [pl.BlockSpec(memory_space=pltpu.VMEM)] * (len(args) - smem)
    return pl.pallas_call(
        kernel,
        out_shape=outs,
        in_specs=specs,
        out_specs=[pl.BlockSpec(memory_space=pltpu.VMEM)] * len(outs),
        scratch_shapes=list(scratch),
        compiler_params=pltpu.CompilerParams(vmem_limit_bytes=limit),
        cost_estimate=pl.CostEstimate(flops=cost * 10**9, bytes_accessed=MIB, transcendentals=0),
    )(*args)


def split_three(column):
    first = column.astype(jnp.bfloat16)
    left = column - first.astype(jnp.float32)
    second = left.astype(jnp.bfloat16)
    third = (left - second.astype(jnp.float32)).astype(jnp.bfloat16)
    lane = lax.broadcasted_iota(jnp.int32, (column.shape[0], LANES), 1)
    wide = jnp.where(lane == 0, first.astype(jnp.float32), 0.0)
    wide = jnp.where(lane == 1, second.astype(jnp.float32), wide)
    return jnp.where(lane == 2, third.astype(jnp.float32), wide).astype(jnp.bfloat16)


def angle_kernel(lengths_ref, cosine_ref, sine_ref):
    count, width = cosine_ref.shape
    lane = lax.broadcasted_iota(jnp.int32, (1, width), 1)
    step = lax.rem(lane, width // 2).astype(jnp.float32)
    frequency = jnp.exp(step * (-2.0 / width * math.log(rope_base)))
    angles = jnp.concatenate(
        [lengths_ref[i].astype(jnp.float32) * frequency for i in range(count)], axis=0
    )
    cosine_ref[...] = jnp.cos(angles)
    sine = jnp.sin(angles)
    sine_ref[...] = jnp.where(lane < width // 2, -sine, sine)


def project_kernel(_, *refs):
    *block_refs, gain_ref, wq_ref, wk_ref, wv_ref, out_ref, stream_ref = refs[:-3]
    rows_ref, sums_ref, packed_ref = refs[-3:]
    place = lax.axis_index("tp")
    own = block_refs[0].shape[0]
    for k, block_ref in enumerate(block_refs):
        start = pl.multiple_of((place ^ k) * own, own)
        rows_ref[pl.ds(start, own), :] = block_ref[...].astype(jnp.float32)
    rows = rows_ref[...]
    stream_ref[...] = rows.astype(jnp.bfloat16)
    squares = jnp.sum(rows * rows, axis=1, keepdims=True)
    scaled = (rows * gain_ref[...]).astype(jnp.bfloat16)
    count = rows.shape[0]
    groups = 0
    for w_ref in (wq_ref, wk_ref, wv_ref):
        product = jnp.dot(scaled, w_ref[...], preferred_element_type=jnp.float32)
        for at in range(0, w_ref.shape[1], LANES):
            sums_ref[groups * count : (groups + 1) * count, :] = product[:, at : at + LANES]
            groups += 1
    sums_ref[groups * count :, :] = split_three(squares).astype(jnp.float32)
    groups += 1
    devices, depth, _ = out_ref.shape
    each = count // devices
    queries = wq_ref.shape[1] // LANES
    for row in range(each * groups, depth):
        packed_ref[pl.ds(row, devices, stride=depth), :] = jnp.zeros((devices, LANES), jnp.float32)
    for n in range(each):
        for g in range(groups):
            row = packed_row(n, g, each, queries, groups)
            packed_ref[pl.ds(row, devices, stride=depth), :] = sums_ref[
                pl.ds(g * count + n, devices, stride=each), :
            ]
    out_ref[...] = packed_ref[...].reshape(out_ref.shape).astype(jnp.bfloat16)


def packed_row(n, g, each, queries, groups):
    if g < queries:
        return n * queries + g
    return each * queries + n * (groups - queries) + g - queries


def attend_kernel(
    lengths_ref, got_ref, cosine_ref, sine_ref, keys_ref, values_ref, out_ref
):
    tp_count = KV_HEADS
    devices, depth, width = got_ref.shape
    each, window, _ = keys_ref.shape
    groups = GROUP + 3
    total = jnp.sum(
        got_ref[...].astype(jnp.float32).reshape(devices // tp_count, tp_count, depth, width),
        axis=0,
    )
    factor = HEAD_DIM ** (-0.5)
    scores, own_scores, own_values = [], [], []
    for n in range(each):
        cosine, sine = cosine_ref[n : n + 1, :], sine_ref[n : n + 1, :]
        tail = packed_row(n, GROUP, each, GROUP, groups)
        squares = jnp.sum(total[0, tail + 2 : tail + 3, :], axis=1, keepdims=True)
        inverse = lax.rsqrt(squares / D + epsilon)
        usable = lax.broadcasted_iota(jnp.int32, (GROUP, window), 1) < lengths_ref[n]
        for h in range(tp_count):
            query = total[h, n * GROUP : (n + 1) * GROUP, :]
            key = total[h, tail : tail + 1, :]
            query = query * cosine + pltpu.roll(query, width // 2, 1) * sine
            key = key * cosine + pltpu.roll(key, width // 2, 1) * sine
            query = query.astype(jnp.bfloat16)
            key = key.astype(jnp.bfloat16).astype(jnp.float32)
            score = lax.dot_general(
                query,
                keys_ref[n, :, h * width : (h + 1) * width],
                (((1,), (1,)), ((), ())),
                preferred_element_type=jnp.float32,
            )
            scores.append(jnp.where(usable, score * (inverse * factor), -jnp.inf))
            own_scores.append(
                jnp.sum(query.astype(jnp.float32) * key, axis=1, keepdims=True)
                * (inverse * inverse * factor)
            )
            value = (total[h, tail + 1 : tail + 2, :] * inverse).astype(jnp.bfloat16)
            own_values.append(value.astype(jnp.float32))
    scores, own_scores = jnp.concatenate(scores, axis=0), jnp.concatenate(own_scores, axis=0)
    highest = jnp.maximum(jnp.max(scores, axis=1, keepdims=True), own_scores)
    weights, own_weights = jnp.exp(scores - highest), jnp.exp(own_scores - highest)
    denominator = jnp.sum(weights, axis=1, keepdims=True) + own_weights
    shrink = 1.0 / denominator
    chances = weights.astype(jnp.bfloat16)
    for n in range(each):
        for h in range(tp_count):
            at = (n * tp_count + h) * GROUP
            attended = jnp.dot(
                chances[at : at + GROUP],
                values_ref[n, :, h * width : (h + 1) * width],
                preferred_element_type=jnp.float32,
            )
            attended = attended + own_weights[at : at + GROUP] * own_values[n * tp_count + h]
            attended = attended * shrink[at : at + GROUP]
            for r in range(devices // tp_count):
                out_ref[r * tp_count + h, n * GROUP : (n + 1) * GROUP, :] = attended.astype(
                    jnp.bfloat16
                )


def output_kernel(heads_ref, w_ref, attended_ref, out_ref, heads_wide_ref):
    count = attended_ref.shape[0]
    groups = w_ref.shape[0] // LANES
    heads_wide_ref[...] = heads_ref[...].astype(jnp.float32).reshape(heads_wide_ref.shape)
    for g in range(groups):
        attended_ref[:, g * LANES : (g + 1) * LANES] = heads_wide_ref[
            pl.ds(g, count, stride=groups), :
        ].astype(jnp.bfloat16)
    output_dots(attended_ref, w_ref, out_ref, 0)


def more_output_kernel(begin, attended_ref, w_ref, out_ref):
    output_dots(attended_ref, w_ref, out_ref, begin)


def output_dots(attended_ref, w_ref, out_ref, begin):
    for part in chunks(out_ref.shape[1]):
        out_ref[:, part] = jnp.dot(
            attended_ref[...],
            w_ref[:, begin + part.start : begin + part.stop],
            preferred_element_type=jnp.float32,
        ).astype(jnp.bfloat16)


def live_column(served_ref, count):
    row = lax.broadcasted_iota(jnp.int32, (count, count), 0)
    column = lax.broadcasted_iota(jnp.int32, (count, count), 1)
    return jnp.sum(
        jnp.where(row == column, served_ref[...], 0).astype(jnp.float32), axis=1, keepdims=True
    )


def middle_part(live, stream_ref, term_refs, gain_ref, at, middle_ref, rows_ref):
    width = term_refs[0].shape[1]
    part = slice(at, at + width)
    attn = term_refs[0][...].astype(jnp.float32) + term_refs[1][...].astype(jnp.float32)
    rows = (stream_ref[:, part].astype(jnp.float32) + live * attn).astype(jnp.bfloat16)
    rows = rows.astype(jnp.float32)
    rows_ref[...] = rows
    own = middle_ref.shape[0]
    start = pl.multiple_of(lax.axis_index("tp") * own, own)
    middle_ref[...] = rows_ref[pl.ds(start, own), :].astype(jnp.bfloat16)
    squares = jnp.sum(rows * rows, axis=1, keepdims=True)
    return (rows * gain_ref[:, part]).astype(jnp.bfloat16), squares


def middle_kernel(*refs):
    served_ref, stream_ref, here_ref, far_ref, gain_ref, wg_ref, wu_ref, *refs = refs
    scaled_ref, squares_ref, partial_ref, middle_ref, live_ref, rows_ref, live_rows_ref = refs
    live = live_column(served_ref, stream_ref.shape[0])
    own = middle_ref.shape[0]
    start = pl.multiple_of(lax.axis_index("tp") * own, own)
    live_rows_ref[...] = jnp.broadcast_to(live, live_rows_ref.shape)
    live_ref[...] = live_rows_ref[pl.ds(start, own), :]
    scaled_ref[...], squares = middle_part(
        live, stream_ref, (here_ref, far_ref), gain_ref, 0, middle_ref, rows_ref
    )
    squares_ref[...] = jnp.broadcast_to(squares, squares_ref.shape)
    part_dots(scaled_ref, wg_ref, wu_ref, partial_ref, 0, ())


def more_middle_kernel(*refs):
    served_ref, stream_ref, here_ref, far_ref, gain_ref, wg_ref, wu_ref, *refs = refs
    before_ref, squares_ref, partial_ref, scaled_ref, tail_ref, send_ref, middle_ref, rows_ref = refs
    live = live_column(served_ref, stream_ref.shape[0])
    width = before_ref.shape[1]
    scaled, squares = middle_part(
        live, stream_ref, (here_ref, far_ref), gain_ref, width, middle_ref, rows_ref
    )
    scaled_ref[:, :width] = before_ref[...]
    scaled_ref[:, width:] = scaled
    wide = partial_ref.shape[1]
    part_dots(scaled_ref, wg_ref, wu_ref, send_ref, width, (partial_ref,))
    tail = split_three(squares + squares_ref[:, :1])
    send_ref[:, wide:] = tail
    tail_ref[...] = tail.astype(jnp.float32)


def part_dots(scaled_ref, wg_ref, wu_ref, out_ref, at, before_refs):
    side = 1 - lax.rem(lax.axis_index("role"), 2)
    size = out_ref.shape[1] // (4 * LANES) * 2 * LANES
    depth = scaled_ref.shape[1] - at
    scaled = scaled_ref[:, at:]
    for w_ref, base in ((wg_ref, 0), (wu_ref, size)):
        for step in range(0, size, CHUNK):
            count = min(CHUNK, size - step)
            start = pl.multiple_of(side * (w_ref.shape[1] // 2) + step, LANES)
            part = slice(base + step, base + step + count)
            product = jnp.dot(
                scaled,
                w_ref[at : at + depth, pl.ds(start, count)],
                preferred_element_type=jnp.float32,
            )
            for before_ref in before_refs:
                product = product + before_ref[:, part]
            out_ref[:, part] = product.astype(out_ref.dtype)


def piece_kernel(theirs, begin, size, scaled_ref, wg_ref, wu_ref, *refs):
    half = lax.rem(lax.axis_index("role"), 2)
    side = 1 - half if theirs else half
    piece_dots(scaled_ref, wg_ref, wu_ref, refs[-1], side, begin, size)


def piece_dots(scaled_ref, wg_ref, wu_ref, out_ref, side, begin, size):
    scaled = scaled_ref[...]
    first = side * (wg_ref.shape[1] // 2) + begin
    for w_ref, base in ((wg_ref, 0), (wu_ref, size)):
        for at in range(0, size, CHUNK):
            step = min(CHUNK, size - at)
            start = pl.multiple_of(first + at, LANES)
            out_ref[:, base + at : base + at + step] = jnp.dot(
                scaled, w_ref[:, pl.ds(start, step)], preferred_element_type=jnp.float32
            ).astype(out_ref.dtype)


def pair_tail_kernel(keep_ref, tail_ref, got_ref, out_ref):
    wide = keep_ref.shape[1]
    out_ref[:, :wide] = (keep_ref[...] + got_ref[:, :wide].astype(jnp.float32)).astype(
        jnp.bfloat16
    )
    squares = jnp.sum(
        tail_ref[...] + got_ref[:, wide:].astype(jnp.float32), axis=1, keepdims=True
    )
    out_ref[:, wide:] = split_three(squares)


def pair_kernel(keep_ref, got_ref, out_ref):
    out_ref[...] = (
        keep_ref[...].astype(jnp.float32) + got_ref[...].astype(jnp.float32)
    ).astype(jnp.bfloat16)


def first_hidden_kernel(own_ref, got_ref, hidden_ref, inverse_ref):
    wide = 2 * hidden_ref.shape[1]
    squares = jnp.sum(
        own_ref[:, wide:].astype(jnp.float32) + got_ref[:, wide:].astype(jnp.float32),
        axis=1,
        keepdims=True,
    )
    inverse = lax.rsqrt(squares / D + epsilon)
    inverse_ref[...] = jnp.broadcast_to(inverse, inverse_ref.shape)
    gated(own_ref, got_ref, inverse, hidden_ref)


def hidden_kernel(own_ref, got_ref, inverse_ref, _, hidden_ref):
    gated(own_ref, got_ref, inverse_ref[:, :1], hidden_ref)


def gated(own_ref, got_ref, inverse, hidden_ref):
    size = hidden_ref.shape[1]
    total = own_ref[:, : 2 * size].astype(jnp.float32) + got_ref[:, : 2 * size].astype(jnp.float32)
    total = total * inverse
    gate, up = total[:, :size], total[:, size:]
    hidden_ref[...] = (gate / (1.0 + jnp.exp(-gate)) * up).astype(jnp.bfloat16)


def down_dots(theirs, begin, hidden_ref, w_ref, part):
    half = lax.rem(lax.axis_index("role"), 2)
    side = 1 - half if theirs else half
    start = pl.multiple_of(side * (w_ref.shape[0] // 2) + begin, LANES)
    return jnp.dot(
        hidden_ref[...],
        w_ref[pl.ds(start, hidden_ref.shape[1]), part],
        preferred_element_type=jnp.float32,
    )


def chunks(width):
    return [slice(at, min(at + CHUNK, width)) for at in range(0, width, CHUNK)]


def down_kernel(theirs, begin, hidden_ref, w_ref, *refs):
    *before_refs, rows_ref = refs
    for part in chunks(w_ref.shape[1]):
        rows = down_dots(theirs, begin, hidden_ref, w_ref, part)
        for before_ref in before_refs:
            rows = rows + before_ref[:, part]
        rows_ref[:, part] = rows


def last_down_kernel(theirs, begin, hidden_ref, w_ref, before_ref, *refs):
    *out_refs, rows_ref = refs
    place = lax.axis_index("tp")
    own = out_refs[0].shape[0]
    for part in chunks(w_ref.shape[1]):
        rows_ref[:, part] = before_ref[:, part] + down_dots(
            theirs, begin, hidden_ref, w_ref, part
        )
    for k, out_ref in enumerate(out_refs):
        start = pl.multiple_of((place ^ k) * own, own)
        out_ref[...] = rows_ref[pl.ds(start, own), :].astype(jnp.bfloat16)


def local_exchange(
    residual,
    attn_gain,
    w_query,
    w_key,
    w_value,
    w_output,
    cache_keys,
    cache_values,
    lengths,
    served,
    ffn_gain,
    w_gate,
    w_up,
    w_down,
):
    if not exchange_fits(residual, w_query, w_key, w_gate):
        return local(
            residual,
            attn_gain,
            w_query,
            w_key,
            w_value,
            w_output,
            cache_keys,
            cache_values,
            lengths,
            served,
            ffn_gain,
            w_gate,
            w_up,
            w_down,
        )
    tp_count, role_count = lax.axis_size("tp"), lax.axis_size("role")
    devices = tp_count * role_count
    own, features = residual.shape
    rows = own * tp_count
    each = rows // devices
    block = jax.ShapeDtypeStruct((own, features), jnp.bfloat16)

    table = jax.ShapeDtypeStruct((each, HEAD_DIM), jnp.float32)
    cosine, sine = call(angle_kernel, [table] * 2, [lengths], smem=1, cost=COVER[0])
    others = {k: swap(residual, "tp", k) for k in reversed(range(1, tp_count))}
    blocks = [residual] + [others[k] for k in range(1, tp_count)]
    payload = w_query.shape[1] + 2 * w_key.shape[1] + LANES
    depth = -(-each * payload // (LANES * 8)) * 8
    sums, stream = call(
        project_kernel,
        [
            jax.ShapeDtypeStruct((devices, depth, LANES), jnp.bfloat16),
            jax.ShapeDtypeStruct((rows, features), jnp.bfloat16),
        ],
        [cosine, *blocks, attn_gain[None, :], in_vmem(w_query), in_vmem(w_key), in_vmem(w_value)],
        scratch=[
            pltpu.VMEM((rows, features), jnp.float32),
            pltpu.VMEM((rows * payload // LANES, LANES), jnp.float32),
            pltpu.VMEM((devices * depth, LANES), jnp.float32),
        ],
        cost=COVER[1],
    )
    parts = lax.all_to_all(sums, ("role", "tp"), 0, 0)
    (heads,) = call(
        attend_kernel,
        [jax.ShapeDtypeStruct((devices, each * GROUP, LANES), jnp.bfloat16)],
        [lengths, parts, cosine, sine, in_vmem(cache_keys), in_vmem(cache_values)],
        smem=1,
        cost=COVER[2],
    )
    heads = lax.all_to_all(heads, ("role", "tp"), 0, 0)
    piece = jax.ShapeDtypeStruct((rows, features // 2), jnp.bfloat16)
    w_output = in_vmem(w_output)
    attended, attn_0 = call(
        output_kernel,
        [jax.ShapeDtypeStruct((rows, w_output.shape[0]), jnp.bfloat16), piece],
        [heads, w_output],
        scratch=[pltpu.VMEM((rows * GROUP, LANES), jnp.float32)],
        cost=COVER[3],
    )
    got_0 = swap(attn_0, "tp", 1)
    (attn_1,) = call(
        functools.partial(more_output_kernel, features // 2),
        [piece],
        [attended, w_output],
        cost=COVER[3],
    )
    terms = []
    got_1 = swap(attn_1, "tp", 1)
    for value, got in ((attn_0, got_0), (attn_1, got_1)):
        (paired,) = call(pair_kernel, [piece], [value, got])
        terms += [paired, swap(paired, "tp", 2)]
    width = w_gate.shape[1] // 2
    first = -(-width * FIRST_PART // (100 * 2 * LANES)) * 2 * LANES
    sizes = (first, width - first)
    w_gate, w_up, w_down = in_vmem(w_gate), in_vmem(w_up), in_vmem(w_down)
    rows_f32 = jax.ShapeDtypeStruct((rows, features), jnp.float32)
    row_scratch = pltpu.VMEM((rows, features), jnp.float32)

    def wide(size, dtype, more=0):
        return jax.ShapeDtypeStruct((rows, 2 * size + more), dtype)

    def half_of(piece):
        return jax.ShapeDtypeStruct((rows, sizes[piece]), jnp.bfloat16)

    first_args = [served[None, :], stream]
    weight_args = [ffn_gain[None, :], w_gate, w_up]
    half_block = jax.ShapeDtypeStruct((own, features // 2), jnp.bfloat16)
    lane_rows = jax.ShapeDtypeStruct((rows, LANES), jnp.float32)
    half_scratch = pltpu.VMEM((rows, features // 2), jnp.float32)
    scaled_0, squares, partial, middle_0, live = call(
        middle_kernel,
        [
            piece,
            lane_rows,
            wide(sizes[0], jnp.float32),
            half_block,
            jax.ShapeDtypeStruct((own, LANES), jnp.float32),
        ],
        [*first_args, *terms[:2], *weight_args],
        scratch=[half_scratch, pltpu.VMEM((rows, LANES), jnp.float32)],
        cost=COVER[4],
    )
    scaled, tail, send, middle_1 = call(
        more_middle_kernel,
        [
            jax.ShapeDtypeStruct((rows, features), jnp.bfloat16),
            lane_rows,
            wide(sizes[0], jnp.bfloat16, LANES),
            half_block,
        ],
        [*first_args, *terms[2:], *weight_args, scaled_0, squares, partial],
        scratch=[half_scratch],
        cost=COVER[4],
    )
    middle = jnp.concatenate([middle_0, middle_1], axis=1)
    got = swap(send, "role", 1)
    (keep,) = call(
        functools.partial(piece_kernel, False, 0, sizes[0]),
        [wide(sizes[0], jnp.float32)],
        [scaled, w_gate, w_up],
        cost=COVER[5],
    )
    (chip_0,) = call(
        pair_tail_kernel, [wide(sizes[0], jnp.bfloat16, LANES)], [keep, tail, got]
    )
    far_0 = swap(chip_0, "role", 2)
    (send,) = call(
        functools.partial(piece_kernel, True, sizes[0], sizes[1]),
        [wide(sizes[1], jnp.bfloat16)],
        [scaled, w_gate, w_up],
        cost=COVER[6],
    )
    got = swap(send, "role", 1)
    (keep,) = call(
        functools.partial(piece_kernel, False, sizes[0], sizes[1]),
        [wide(sizes[1], jnp.float32)],
        [scaled, w_gate, w_up],
        cost=COVER[7],
    )
    (chip_1,) = call(pair_kernel, [wide(sizes[1], jnp.bfloat16)], [keep, got])
    far_1 = swap(chip_1, "role", 2)
    hidden, inverse = call(
        first_hidden_kernel,
        [half_of(0), jax.ShapeDtypeStruct((rows, LANES), jnp.float32)],
        [chip_0, far_0],
    )
    other = swap(hidden, "role", 1)
    (down,) = call(
        functools.partial(down_kernel, False, 0), [rows_f32], [hidden, w_down], cost=COVER[8]
    )
    (down,) = call(
        functools.partial(down_kernel, True, 0), [rows_f32], [other, w_down, down], cost=COVER[8]
    )
    (hidden,) = call(hidden_kernel, [half_of(1)], [chip_1, far_1, inverse, down])
    other = swap(hidden, "role", 1)
    (down,) = call(
        functools.partial(down_kernel, False, sizes[0]),
        [rows_f32],
        [hidden, w_down, down],
        cost=COVER[9],
    )
    terms = call(
        functools.partial(last_down_kernel, True, sizes[0]),
        [block] * tp_count,
        [other, w_down, down],
        scratch=[row_scratch],
        cost=COVER[9],
    )
    terms = [terms[0]] + [swap(terms[k], "tp", k) for k in range(1, tp_count)]
    ffn = terms[0].astype(jnp.float32)
    for term in terms[1:]:
        ffn = ffn + term.astype(jnp.float32)
    return (middle.astype(jnp.float32) + live[:, :1] * ffn).astype(jnp.bfloat16)


def solution(mesh):
    return jax.shard_map(
        local_exchange,
        mesh=mesh,
        in_specs=(
            P(("groups", "tp"), "role"),
            P("role"),
            P("role", "tp"),
            P("role", "tp"),
            P("role", "tp"),
            P("tp", "role"),
            P(("groups", "role", "tp"), None, None),
            P(("groups", "role", "tp"), None, None),
            P(("groups", "role", "tp")),
            P("groups"),
            P("role"),
            P("role", "tp"),
            P("role", "tp"),
            P("tp", "role"),
        ),
        out_specs=P(("groups", "tp"), "role"),
        check_vma=False,
    )
```

```python
import functools
import math

import jax
import jax.numpy as jnp
from jax import lax
from jax.experimental import pallas as pl
from jax.experimental.pallas import tpu as pltpu
from jax.sharding import PartitionSpec as P


D = 8192
HEADS = 32
KV_HEADS = 4
HEAD_DIM = 128
WINDOW = 256
GROUP = 8


epsilon = 1e-05
rope_base = 500000.0


def rotate(vectors, positions):
    halfway = vectors.shape[-1] // 2
    frequency = jnp.power(
        jnp.float32(rope_base), -jnp.arange(halfway, dtype=jnp.float32) * 2.0 / vectors.shape[-1]
    )
    angles = positions.astype(jnp.float32)[:, None, None] * frequency[None, None, :]
    cosine = jnp.cos(angles)
    sine_part = jnp.sin(angles)
    leading = vectors[..., :halfway]
    trailing = vectors[..., halfway:]
    return jnp.concatenate(
        [leading * cosine - trailing * sine_part, trailing * cosine + leading * sine_part], axis=-1
    )


def attend(queries, new_key, new_value, keys, values, lengths):
    batch_rows = queries.shape[0]
    factor = HEAD_DIM ** (-0.5)
    grouped = queries.reshape(batch_rows, KV_HEADS, GROUP, HEAD_DIM)
    key_blocks = keys.reshape(batch_rows, WINDOW, KV_HEADS, HEAD_DIM)
    value_blocks = values.reshape(batch_rows, WINDOW, KV_HEADS, HEAD_DIM)
    scores = (
        jnp.einsum("nkgd,nwkd->nkgw", grouped, key_blocks, preferred_element_type=jnp.float32)
        * factor
    )
    self_score = (
        jnp.einsum("nkgd,nkd->nkg", grouped, new_key, preferred_element_type=jnp.float32) * factor
    )
    usable = jnp.arange(WINDOW, dtype=jnp.int32)[None, :] < lengths[:, None]
    scores = jnp.where(usable[:, None, None, :], scores, -jnp.inf)
    highest = jnp.maximum(jnp.max(scores, axis=-1), self_score)
    weights = jnp.exp(scores - highest[..., None])
    self_weight = jnp.exp(self_score - highest)
    denominator = jnp.sum(weights, axis=-1) + self_weight
    chances = (weights / denominator[..., None]).astype(jnp.bfloat16)
    self_chance = (self_weight / denominator).astype(jnp.bfloat16)
    attended = jnp.einsum(
        "nkgw,nwkd->nkgd", chances, value_blocks, preferred_element_type=jnp.float32
    )
    attended = (
        attended
        + self_chance.astype(jnp.float32)[..., None] * new_value.astype(jnp.float32)[:, :, None, :]
    )
    return attended.reshape(batch_rows, HEADS * HEAD_DIM).astype(jnp.bfloat16)


def feed_forward(middle, ffn_gain, w_gate, w_up, w_down):
    widened = middle.astype(jnp.float32)
    squares = lax.psum(jnp.sum(widened * widened, axis=1), "role")
    inverse = lax.rsqrt(squares / D + epsilon)
    mid_normed = (widened * inverse[:, None] * ffn_gain[None, :]).astype(jnp.bfloat16)
    gate_part = jnp.dot(mid_normed, w_gate, preferred_element_type=jnp.float32)
    up_part = jnp.dot(mid_normed, w_up, preferred_element_type=jnp.float32)
    gate_total, up_total = (
        lax.psum(gate_part.astype(jnp.bfloat16), "role").astype(jnp.float32),
        lax.psum(up_part.astype(jnp.bfloat16), "role").astype(jnp.float32),
    )
    hidden = (jax.nn.silu(gate_total) * up_total).astype(jnp.bfloat16)
    down_terms = jnp.dot(hidden, w_down, preferred_element_type=jnp.float32)
    return lax.psum_scatter(
        down_terms.astype(jnp.bfloat16), "tp", scatter_dimension=0, tiled=True
    ).astype(jnp.float32)


def local(
    residual,
    attn_gain,
    w_query,
    w_key,
    w_value,
    w_output,
    cache_keys,
    cache_values,
    lengths,
    served,
    ffn_gain,
    w_gate,
    w_up,
    w_down,
):
    own_rows = residual.shape[0]
    tp_count = lax.axis_size("tp")
    row_start = lax.axis_index("tp") * own_rows
    live_own = lax.dynamic_slice_in_dim(served, row_start, own_rows, 0).astype(jnp.float32)[:, None]
    rows_all = lax.all_gather(residual, "tp", axis=0, tiled=True)
    widened = rows_all.astype(jnp.float32)
    squares = lax.psum(jnp.sum(widened * widened, axis=1), "role")
    inverse = lax.rsqrt(squares / D + epsilon)
    normed = (widened * inverse[:, None] * attn_gain[None, :]).astype(jnp.bfloat16)
    partial_value = jnp.concatenate(
        [
            jnp.dot(normed, w_query, preferred_element_type=jnp.float32),
            jnp.dot(normed, w_key, preferred_element_type=jnp.float32),
            jnp.dot(normed, w_value, preferred_element_type=jnp.float32),
        ],
        axis=1,
    )
    summed = lax.psum_scatter(
        partial_value.astype(jnp.bfloat16), "role", scatter_dimension=0, tiled=True
    ).astype(jnp.float32)
    gathered = lax.all_to_all(
        summed.astype(jnp.bfloat16), "tp", split_axis=0, concat_axis=1, tiled=True
    ).astype(summed.dtype)
    local_rows = gathered.shape[0]
    query_cols = w_query.shape[1]
    kv_cols = w_key.shape[1]
    blocks = gathered.reshape(local_rows, tp_count, query_cols + 2 * kv_cols)
    queries = blocks[:, :, :query_cols].reshape(local_rows, HEADS, HEAD_DIM)
    new_key = blocks[:, :, query_cols : query_cols + kv_cols].reshape(
        local_rows, KV_HEADS, HEAD_DIM
    )
    new_value = (
        blocks[:, :, query_cols + kv_cols :]
        .reshape(local_rows, KV_HEADS, HEAD_DIM)
        .astype(jnp.bfloat16)
    )
    queries = rotate(queries, lengths).astype(jnp.bfloat16)
    new_key = rotate(new_key, lengths).astype(jnp.bfloat16)
    attended = attend(queries, new_key, new_value, cache_keys, cache_values, lengths)
    head_block = lax.all_to_all(attended, "tp", split_axis=1, concat_axis=0, tiled=True)
    attn_terms = jnp.dot(
        lax.all_gather(head_block, "role", axis=0, tiled=True),
        w_output,
        preferred_element_type=jnp.float32,
    )
    attn = lax.psum_scatter(
        attn_terms.astype(jnp.bfloat16), "tp", scatter_dimension=0, tiled=True
    ).astype(jnp.float32)
    middle_own = (residual.astype(jnp.float32) + live_own * attn).astype(jnp.bfloat16)
    middle = lax.all_gather(middle_own, "tp", axis=0, tiled=True)
    ffn = feed_forward(middle, ffn_gain, w_gate, w_up, w_down)
    return (middle_own.astype(jnp.float32) + live_own * ffn).astype(jnp.bfloat16)


LANES = 128
MIB = 2**20
COVER = (100, 1, 1, 1, 10, 10, 10, 1, 1, 1)
CHUNK = 1024
FIRST_PART = 43


def exchange_fits(residual, w_query, w_key, w_gate):
    tp_count, role_count = lax.axis_size("tp"), lax.axis_size("role")
    return (
        tp_count == KV_HEADS
        and role_count == 4
        and residual.shape[0] % 8 == 0
        and residual.shape[1] % (2 * LANES) == 0
        and w_query.shape[1] == GROUP * LANES
        and w_key.shape[1] == LANES
        and w_gate.shape[1] % (4 * LANES) == 0
        and w_gate.shape[1] >= 8 * LANES
    )


def swap(value, axis, distance):
    count = lax.axis_size(axis)
    return lax.ppermute(value, axis, [(i, i ^ distance) for i in range(count)])


def in_vmem(value):
    return pltpu.with_memory_space_constraint(value, pltpu.VMEM)


def call(kernel, outs, args, scratch=(), limit=4 * MIB, smem=0, cost=0):
    specs = [pl.BlockSpec(memory_space=pltpu.SMEM)] * smem
    specs += [pl.BlockSpec(memory_space=pltpu.VMEM)] * (len(args) - smem)
    return pl.pallas_call(
        kernel,
        out_shape=outs,
        in_specs=specs,
        out_specs=[pl.BlockSpec(memory_space=pltpu.VMEM)] * len(outs),
        scratch_shapes=list(scratch),
        compiler_params=pltpu.CompilerParams(vmem_limit_bytes=limit),
        cost_estimate=pl.CostEstimate(flops=cost * 10**9, bytes_accessed=MIB, transcendentals=0),
    )(*args)


def split_three(column):
    first = column.astype(jnp.bfloat16)
    left = column - first.astype(jnp.float32)
    second = left.astype(jnp.bfloat16)
    third = (left - second.astype(jnp.float32)).astype(jnp.bfloat16)
    lane = lax.broadcasted_iota(jnp.int32, (column.shape[0], LANES), 1)
    wide = jnp.where(lane == 0, first.astype(jnp.float32), 0.0)
    wide = jnp.where(lane == 1, second.astype(jnp.float32), wide)
    return jnp.where(lane == 2, third.astype(jnp.float32), wide).astype(jnp.bfloat16)


def angle_kernel(lengths_ref, cosine_ref, sine_ref):
    count, width = cosine_ref.shape
    lane = lax.broadcasted_iota(jnp.int32, (1, width), 1)
    step = lax.rem(lane, width // 2).astype(jnp.float32)
    frequency = jnp.exp(step * (-2.0 / width * math.log(rope_base)))
    angles = jnp.concatenate(
        [lengths_ref[i].astype(jnp.float32) * frequency for i in range(count)], axis=0
    )
    cosine_ref[...] = jnp.cos(angles)
    sine = jnp.sin(angles)
    sine_ref[...] = jnp.where(lane < width // 2, -sine, sine)


def project_kernel(_, *refs):
    *block_refs, gain_ref, wq_ref, wk_ref, wv_ref, out_ref, stream_ref = refs[:-3]
    rows_ref, sums_ref, packed_ref = refs[-3:]
    place = lax.axis_index("tp")
    own = block_refs[0].shape[0]
    for k, block_ref in enumerate(block_refs):
        start = pl.multiple_of((place ^ k) * own, own)
        rows_ref[pl.ds(start, own), :] = block_ref[...].astype(jnp.float32)
    rows = rows_ref[...]
    stream_ref[...] = rows.astype(jnp.bfloat16)
    squares = jnp.sum(rows * rows, axis=1, keepdims=True)
    scaled = (rows * gain_ref[...]).astype(jnp.bfloat16)
    count = rows.shape[0]
    groups = 0
    for w_ref in (wq_ref, wk_ref, wv_ref):
        product = jnp.dot(scaled, w_ref[...], preferred_element_type=jnp.float32)
        for at in range(0, w_ref.shape[1], LANES):
            sums_ref[groups * count : (groups + 1) * count, :] = product[:, at : at + LANES]
            groups += 1
    sums_ref[groups * count :, :] = split_three(squares).astype(jnp.float32)
    groups += 1
    devices, depth, _ = out_ref.shape
    each = count // devices
    queries = wq_ref.shape[1] // LANES
    packed_ref[...] = jnp.zeros_like(packed_ref)
    for n in range(each):
        for g in range(groups):
            row = packed_row(n, g, each, queries, groups)
            packed_ref[pl.ds(row, devices, stride=depth), :] = sums_ref[
                pl.ds(g * count + n, devices, stride=each), :
            ]
    out_ref[...] = packed_ref[...].reshape(out_ref.shape).astype(jnp.bfloat16)


def packed_row(n, g, each, queries, groups):
    if g < queries:
        return n * queries + g
    return each * queries + n * (groups - queries) + g - queries


def attend_kernel(
    lengths_ref, got_ref, cosine_ref, sine_ref, keys_ref, values_ref, out_ref
):
    tp_count = KV_HEADS
    devices, depth, width = got_ref.shape
    each, window, _ = keys_ref.shape
    groups = GROUP + 3
    total = jnp.sum(
        got_ref[...].astype(jnp.float32).reshape(devices // tp_count, tp_count, depth, width),
        axis=0,
    )
    factor = HEAD_DIM ** (-0.5)
    scores, own_scores, own_values = [], [], []
    for n in range(each):
        cosine, sine = cosine_ref[n : n + 1, :], sine_ref[n : n + 1, :]
        tail = packed_row(n, GROUP, each, GROUP, groups)
        squares = jnp.sum(total[0, tail + 2 : tail + 3, :], axis=1, keepdims=True)
        inverse = lax.rsqrt(squares / D + epsilon)
        usable = lax.broadcasted_iota(jnp.int32, (GROUP, window), 1) < lengths_ref[n]
        for h in range(tp_count):
            query = total[h, n * GROUP : (n + 1) * GROUP, :]
            key = total[h, tail : tail + 1, :]
            query = query * cosine + pltpu.roll(query, width // 2, 1) * sine
            key = key * cosine + pltpu.roll(key, width // 2, 1) * sine
            query = query.astype(jnp.bfloat16)
            key = key.astype(jnp.bfloat16).astype(jnp.float32)
            score = lax.dot_general(
                query,
                keys_ref[n, :, h * width : (h + 1) * width],
                (((1,), (1,)), ((), ())),
                preferred_element_type=jnp.float32,
            )
            scores.append(jnp.where(usable, score * (inverse * factor), -jnp.inf))
            own_scores.append(
                jnp.sum(query.astype(jnp.float32) * key, axis=1, keepdims=True)
                * (inverse * inverse * factor)
            )
            value = (total[h, tail + 1 : tail + 2, :] * inverse).astype(jnp.bfloat16)
            own_values.append(value.astype(jnp.float32))
    scores, own_scores = jnp.concatenate(scores, axis=0), jnp.concatenate(own_scores, axis=0)
    highest = jnp.maximum(jnp.max(scores, axis=1, keepdims=True), own_scores)
    weights, own_weights = jnp.exp(scores - highest), jnp.exp(own_scores - highest)
    denominator = jnp.sum(weights, axis=1, keepdims=True) + own_weights
    shrink = 1.0 / denominator
    chances = weights.astype(jnp.bfloat16)
    for n in range(each):
        for h in range(tp_count):
            at = (n * tp_count + h) * GROUP
            attended = jnp.dot(
                chances[at : at + GROUP],
                values_ref[n, :, h * width : (h + 1) * width],
                preferred_element_type=jnp.float32,
            )
            attended = attended + own_weights[at : at + GROUP] * own_values[n * tp_count + h]
            attended = attended * shrink[at : at + GROUP]
            for r in range(devices // tp_count):
                out_ref[r * tp_count + h, n * GROUP : (n + 1) * GROUP, :] = attended.astype(
                    jnp.bfloat16
                )


def output_kernel(heads_ref, w_ref, attended_ref, out_ref, heads_wide_ref):
    count = attended_ref.shape[0]
    groups = w_ref.shape[0] // LANES
    heads_wide_ref[...] = heads_ref[...].astype(jnp.float32).reshape(heads_wide_ref.shape)
    for g in range(groups):
        attended_ref[:, g * LANES : (g + 1) * LANES] = heads_wide_ref[
            pl.ds(g, count, stride=groups), :
        ].astype(jnp.bfloat16)
    output_dots(attended_ref, w_ref, out_ref, 0)


def more_output_kernel(begin, attended_ref, w_ref, out_ref):
    output_dots(attended_ref, w_ref, out_ref, begin)


def output_dots(attended_ref, w_ref, out_ref, begin):
    for part in chunks(out_ref.shape[1]):
        out_ref[:, part] = jnp.dot(
            attended_ref[...],
            w_ref[:, begin + part.start : begin + part.stop],
            preferred_element_type=jnp.float32,
        ).astype(jnp.bfloat16)


def live_column(served_ref, count):
    row = lax.broadcasted_iota(jnp.int32, (count, count), 0)
    column = lax.broadcasted_iota(jnp.int32, (count, count), 1)
    return jnp.sum(
        jnp.where(row == column, served_ref[...], 0).astype(jnp.float32), axis=1, keepdims=True
    )


def middle_part(live, stream_ref, term_refs, gain_ref, at, middle_ref, rows_ref):
    width = term_refs[0].shape[1]
    part = slice(at, at + width)
    attn = term_refs[0][...].astype(jnp.float32) + term_refs[1][...].astype(jnp.float32)
    rows = (stream_ref[:, part].astype(jnp.float32) + live * attn).astype(jnp.bfloat16)
    rows = rows.astype(jnp.float32)
    rows_ref[...] = rows
    own = middle_ref.shape[0]
    start = pl.multiple_of(lax.axis_index("tp") * own, own)
    middle_ref[...] = rows_ref[pl.ds(start, own), :].astype(jnp.bfloat16)
    squares = jnp.sum(rows * rows, axis=1, keepdims=True)
    return (rows * gain_ref[:, part]).astype(jnp.bfloat16), squares


def middle_kernel(*refs):
    served_ref, stream_ref, here_ref, far_ref, gain_ref, wg_ref, wu_ref, *refs = refs
    scaled_ref, squares_ref, partial_ref, middle_ref, live_ref, rows_ref, live_rows_ref = refs
    live = live_column(served_ref, stream_ref.shape[0])
    own = middle_ref.shape[0]
    start = pl.multiple_of(lax.axis_index("tp") * own, own)
    live_rows_ref[...] = jnp.broadcast_to(live, live_rows_ref.shape)
    live_ref[...] = live_rows_ref[pl.ds(start, own), :]
    scaled_ref[...], squares = middle_part(
        live, stream_ref, (here_ref, far_ref), gain_ref, 0, middle_ref, rows_ref
    )
    squares_ref[...] = jnp.broadcast_to(squares, squares_ref.shape)
    part_dots(scaled_ref, wg_ref, wu_ref, partial_ref, 0, ())


def more_middle_kernel(*refs):
    served_ref, stream_ref, here_ref, far_ref, gain_ref, wg_ref, wu_ref, *refs = refs
    before_ref, squares_ref, partial_ref, scaled_ref, tail_ref, send_ref, middle_ref, rows_ref = refs
    live = live_column(served_ref, stream_ref.shape[0])
    width = before_ref.shape[1]
    scaled, squares = middle_part(
        live, stream_ref, (here_ref, far_ref), gain_ref, width, middle_ref, rows_ref
    )
    scaled_ref[:, :width] = before_ref[...]
    scaled_ref[:, width:] = scaled
    wide = partial_ref.shape[1]
    part_dots(scaled_ref, wg_ref, wu_ref, send_ref, width, (partial_ref,))
    tail = split_three(squares + squares_ref[:, :1])
    send_ref[:, wide:] = tail
    tail_ref[...] = tail.astype(jnp.float32)


def part_dots(scaled_ref, wg_ref, wu_ref, out_ref, at, before_refs):
    side = 1 - lax.rem(lax.axis_index("role"), 2)
    size = out_ref.shape[1] // (4 * LANES) * 2 * LANES
    depth = scaled_ref.shape[1] - at
    scaled = scaled_ref[:, at:]
    for w_ref, base in ((wg_ref, 0), (wu_ref, size)):
        for step in range(0, size, CHUNK):
            count = min(CHUNK, size - step)
            start = pl.multiple_of(side * (w_ref.shape[1] // 2) + step, LANES)
            part = slice(base + step, base + step + count)
            product = jnp.dot(
                scaled,
                w_ref[at : at + depth, pl.ds(start, count)],
                preferred_element_type=jnp.float32,
            )
            for before_ref in before_refs:
                product = product + before_ref[:, part]
            out_ref[:, part] = product.astype(out_ref.dtype)


def piece_kernel(theirs, begin, size, scaled_ref, wg_ref, wu_ref, *refs):
    half = lax.rem(lax.axis_index("role"), 2)
    side = 1 - half if theirs else half
    piece_dots(scaled_ref, wg_ref, wu_ref, refs[-1], side, begin, size)


def piece_dots(scaled_ref, wg_ref, wu_ref, out_ref, side, begin, size):
    scaled = scaled_ref[...]
    first = side * (wg_ref.shape[1] // 2) + begin
    for w_ref, base in ((wg_ref, 0), (wu_ref, size)):
        for at in range(0, size, CHUNK):
            step = min(CHUNK, size - at)
            start = pl.multiple_of(first + at, LANES)
            out_ref[:, base + at : base + at + step] = jnp.dot(
                scaled, w_ref[:, pl.ds(start, step)], preferred_element_type=jnp.float32
            ).astype(out_ref.dtype)


def pair_tail_kernel(keep_ref, tail_ref, got_ref, out_ref):
    wide = keep_ref.shape[1]
    out_ref[:, :wide] = (keep_ref[...] + got_ref[:, :wide].astype(jnp.float32)).astype(
        jnp.bfloat16
    )
    squares = jnp.sum(
        tail_ref[...] + got_ref[:, wide:].astype(jnp.float32), axis=1, keepdims=True
    )
    out_ref[:, wide:] = split_three(squares)


def pair_kernel(keep_ref, got_ref, out_ref):
    out_ref[...] = (
        keep_ref[...].astype(jnp.float32) + got_ref[...].astype(jnp.float32)
    ).astype(jnp.bfloat16)


def first_hidden_kernel(own_ref, got_ref, hidden_ref, inverse_ref):
    wide = 2 * hidden_ref.shape[1]
    squares = jnp.sum(
        own_ref[:, wide:].astype(jnp.float32) + got_ref[:, wide:].astype(jnp.float32),
        axis=1,
        keepdims=True,
    )
    inverse = lax.rsqrt(squares / D + epsilon)
    inverse_ref[...] = jnp.broadcast_to(inverse, inverse_ref.shape)
    gated(own_ref, got_ref, inverse, hidden_ref)


def hidden_kernel(own_ref, got_ref, inverse_ref, _, hidden_ref):
    gated(own_ref, got_ref, inverse_ref[:, :1], hidden_ref)


def gated(own_ref, got_ref, inverse, hidden_ref):
    size = hidden_ref.shape[1]
    total = own_ref[:, : 2 * size].astype(jnp.float32) + got_ref[:, : 2 * size].astype(jnp.float32)
    total = total * inverse
    gate, up = total[:, :size], total[:, size:]
    hidden_ref[...] = (gate / (1.0 + jnp.exp(-gate)) * up).astype(jnp.bfloat16)


def down_dots(theirs, begin, hidden_ref, w_ref, part):
    half = lax.rem(lax.axis_index("role"), 2)
    side = 1 - half if theirs else half
    start = pl.multiple_of(side * (w_ref.shape[0] // 2) + begin, LANES)
    return jnp.dot(
        hidden_ref[...],
        w_ref[pl.ds(start, hidden_ref.shape[1]), part],
        preferred_element_type=jnp.float32,
    )


def chunks(width):
    return [slice(at, min(at + CHUNK, width)) for at in range(0, width, CHUNK)]


def down_kernel(theirs, begin, hidden_ref, w_ref, *refs):
    *before_refs, rows_ref = refs
    for part in chunks(w_ref.shape[1]):
        rows = down_dots(theirs, begin, hidden_ref, w_ref, part)
        for before_ref in before_refs:
            rows = rows + before_ref[:, part]
        rows_ref[:, part] = rows


def last_down_kernel(theirs, begin, hidden_ref, w_ref, before_ref, *refs):
    *out_refs, rows_ref = refs
    place = lax.axis_index("tp")
    own = out_refs[0].shape[0]
    for part in chunks(w_ref.shape[1]):
        rows_ref[:, part] = before_ref[:, part] + down_dots(
            theirs, begin, hidden_ref, w_ref, part
        )
    for k, out_ref in enumerate(out_refs):
        start = pl.multiple_of((place ^ k) * own, own)
        out_ref[...] = rows_ref[pl.ds(start, own), :].astype(jnp.bfloat16)


def local_exchange(
    residual,
    attn_gain,
    w_query,
    w_key,
    w_value,
    w_output,
    cache_keys,
    cache_values,
    lengths,
    served,
    ffn_gain,
    w_gate,
    w_up,
    w_down,
):
    if not exchange_fits(residual, w_query, w_key, w_gate):
        return local(
            residual,
            attn_gain,
            w_query,
            w_key,
            w_value,
            w_output,
            cache_keys,
            cache_values,
            lengths,
            served,
            ffn_gain,
            w_gate,
            w_up,
            w_down,
        )
    tp_count, role_count = lax.axis_size("tp"), lax.axis_size("role")
    devices = tp_count * role_count
    own, features = residual.shape
    rows = own * tp_count
    each = rows // devices
    block = jax.ShapeDtypeStruct((own, features), jnp.bfloat16)

    table = jax.ShapeDtypeStruct((each, HEAD_DIM), jnp.float32)
    cosine, sine = call(angle_kernel, [table] * 2, [lengths], smem=1, cost=COVER[0])
    others = {k: swap(residual, "tp", k) for k in reversed(range(1, tp_count))}
    blocks = [residual] + [others[k] for k in range(1, tp_count)]
    payload = w_query.shape[1] + 2 * w_key.shape[1] + LANES
    depth = -(-each * payload // (LANES * 8)) * 8
    sums, stream = call(
        project_kernel,
        [
            jax.ShapeDtypeStruct((devices, depth, LANES), jnp.bfloat16),
            jax.ShapeDtypeStruct((rows, features), jnp.bfloat16),
        ],
        [cosine, *blocks, attn_gain[None, :], in_vmem(w_query), in_vmem(w_key), in_vmem(w_value)],
        scratch=[
            pltpu.VMEM((rows, features), jnp.float32),
            pltpu.VMEM((rows * payload // LANES, LANES), jnp.float32),
            pltpu.VMEM((devices * depth, LANES), jnp.float32),
        ],
        cost=COVER[1],
    )
    parts = lax.all_to_all(sums, ("role", "tp"), 0, 0)
    (heads,) = call(
        attend_kernel,
        [jax.ShapeDtypeStruct((devices, each * GROUP, LANES), jnp.bfloat16)],
        [lengths, parts, cosine, sine, in_vmem(cache_keys), in_vmem(cache_values)],
        smem=1,
        cost=COVER[2],
    )
    heads = lax.all_to_all(heads, ("role", "tp"), 0, 0)
    piece = jax.ShapeDtypeStruct((rows, features // 2), jnp.bfloat16)
    w_output = in_vmem(w_output)
    attended, attn_0 = call(
        output_kernel,
        [jax.ShapeDtypeStruct((rows, w_output.shape[0]), jnp.bfloat16), piece],
        [heads, w_output],
        scratch=[pltpu.VMEM((rows * GROUP, LANES), jnp.float32)],
        cost=COVER[3],
    )
    got_0 = swap(attn_0, "tp", 1)
    (attn_1,) = call(
        functools.partial(more_output_kernel, features // 2),
        [piece],
        [attended, w_output],
        cost=COVER[3],
    )
    terms = []
    got_1 = swap(attn_1, "tp", 1)
    for value, got in ((attn_0, got_0), (attn_1, got_1)):
        (paired,) = call(pair_kernel, [piece], [value, got])
        terms += [paired, swap(paired, "tp", 2)]
    width = w_gate.shape[1] // 2
    first = -(-width * FIRST_PART // (100 * 2 * LANES)) * 2 * LANES
    sizes = (first, width - first)
    w_gate, w_up, w_down = in_vmem(w_gate), in_vmem(w_up), in_vmem(w_down)
    rows_f32 = jax.ShapeDtypeStruct((rows, features), jnp.float32)
    row_scratch = pltpu.VMEM((rows, features), jnp.float32)

    def wide(size, dtype, more=0):
        return jax.ShapeDtypeStruct((rows, 2 * size + more), dtype)

    def half_of(piece):
        return jax.ShapeDtypeStruct((rows, sizes[piece]), jnp.bfloat16)

    first_args = [served[None, :], stream]
    weight_args = [ffn_gain[None, :], w_gate, w_up]
    half_block = jax.ShapeDtypeStruct((own, features // 2), jnp.bfloat16)
    lane_rows = jax.ShapeDtypeStruct((rows, LANES), jnp.float32)
    half_scratch = pltpu.VMEM((rows, features // 2), jnp.float32)
    scaled_0, squares, partial, middle_0, live = call(
        middle_kernel,
        [
            piece,
            lane_rows,
            wide(sizes[0], jnp.float32),
            half_block,
            jax.ShapeDtypeStruct((own, LANES), jnp.float32),
        ],
        [*first_args, *terms[:2], *weight_args],
        scratch=[half_scratch, pltpu.VMEM((rows, LANES), jnp.float32)],
        cost=COVER[4],
    )
    scaled, tail, send, middle_1 = call(
        more_middle_kernel,
        [
            jax.ShapeDtypeStruct((rows, features), jnp.bfloat16),
            lane_rows,
            wide(sizes[0], jnp.bfloat16, LANES),
            half_block,
        ],
        [*first_args, *terms[2:], *weight_args, scaled_0, squares, partial],
        scratch=[half_scratch],
        cost=COVER[4],
    )
    middle = jnp.concatenate([middle_0, middle_1], axis=1)
    got = swap(send, "role", 1)
    (keep,) = call(
        functools.partial(piece_kernel, False, 0, sizes[0]),
        [wide(sizes[0], jnp.float32)],
        [scaled, w_gate, w_up],
        cost=COVER[5],
    )
    (chip_0,) = call(
        pair_tail_kernel, [wide(sizes[0], jnp.bfloat16, LANES)], [keep, tail, got]
    )
    far_0 = swap(chip_0, "role", 2)
    (send,) = call(
        functools.partial(piece_kernel, True, sizes[0], sizes[1]),
        [wide(sizes[1], jnp.bfloat16)],
        [scaled, w_gate, w_up, chip_0],
        cost=COVER[6],
    )
    got = swap(send, "role", 1)
    (keep,) = call(
        functools.partial(piece_kernel, False, sizes[0], sizes[1]),
        [wide(sizes[1], jnp.float32)],
        [scaled, w_gate, w_up],
        cost=COVER[7],
    )
    (chip_1,) = call(pair_kernel, [wide(sizes[1], jnp.bfloat16)], [keep, got])
    far_1 = swap(chip_1, "role", 2)
    hidden, inverse = call(
        first_hidden_kernel,
        [half_of(0), jax.ShapeDtypeStruct((rows, LANES), jnp.float32)],
        [chip_0, far_0],
    )
    other = swap(hidden, "role", 1)
    (down,) = call(
        functools.partial(down_kernel, False, 0), [rows_f32], [hidden, w_down], cost=COVER[8]
    )
    (down,) = call(
        functools.partial(down_kernel, True, 0), [rows_f32], [other, w_down, down], cost=COVER[8]
    )
    (hidden,) = call(hidden_kernel, [half_of(1)], [chip_1, far_1, inverse, down])
    other = swap(hidden, "role", 1)
    (down,) = call(
        functools.partial(down_kernel, False, sizes[0]),
        [rows_f32],
        [hidden, w_down, down],
        cost=COVER[9],
    )
    terms = call(
        functools.partial(last_down_kernel, True, sizes[0]),
        [block] * tp_count,
        [other, w_down, down],
        scratch=[row_scratch],
        cost=COVER[9],
    )
    terms = [terms[0]] + [swap(terms[k], "tp", k) for k in range(1, tp_count)]
    ffn = terms[0].astype(jnp.float32)
    for term in terms[1:]:
        ffn = ffn + term.astype(jnp.float32)
    return (middle.astype(jnp.float32) + live[:, :1] * ffn).astype(jnp.bfloat16)


def solution(mesh):
    return jax.shard_map(
        local_exchange,
        mesh=mesh,
        in_specs=(
            P(("groups", "tp"), "role"),
            P("role"),
            P("role", "tp"),
            P("role", "tp"),
            P("role", "tp"),
            P("tp", "role"),
            P(("groups", "role", "tp"), None, None),
            P(("groups", "role", "tp"), None, None),
            P(("groups", "role", "tp")),
            P("groups"),
            P("role"),
            P("role", "tp"),
            P("role", "tp"),
            P("tp", "role"),
        ),
        out_specs=P(("groups", "tp"), "role"),
        check_vma=False,
    )
```
